32 devices in a mesh: task: 4 (over z), feat: 8 (over y, x, core).
Axes of the slice: x: 2, y: 2, z: 4, core: 2. Of those that a mesh axis runs over, the one named last changes fastest.
Arguments:
- inputs: bfloat16 [4, 64, 512, 512], P('task', 'feat'), may hold values from -6 to 6
- context: int32 [4], P('task'), may hold values from 50 to 500, as said below
- sample_mask: int32 [4, 512], P('task'), may hold values from 0 to 1, as said below
- sample_gain: float32 [512], replicated, may hold values from 0.5 to 1.5
- sample_shift: float32 [512], replicated, may hold values from -2 to 2
- sample_project: bfloat16 [512, 1536], replicated, may hold values from -0.25 to 0.25
- sample_output: bfloat16 [512, 512], replicated, may hold values from -1 to 1
- sample_bias: float32 [512], replicated, may hold values from -2 to 2
- feature_gain: float32 [512], replicated, may hold values from 0.5 to 1.5
- feature_shift: float32 [512], replicated, may hold values from -2 to 2
- feature_project: bfloat16 [512, 1536], replicated, may hold values from -0.25 to 0.25
- feature_output: bfloat16 [512, 512], replicated, may hold values from -0.75 to 0.75
- feature_bias: float32 [512], replicated, may hold values from -2 to 2
- dense_gain: float32 [512], replicated, may hold values from 0.5 to 1.5
- dense_shift: float32 [512], replicated, may hold values from -2 to 2
- up_weight: bfloat16 [512, 2048], replicated, may hold values from -0.25 to 0.25
- up_bias: float32 [2048], replicated, may hold values from -2 to 2
- down_weight: bfloat16 [2048, 512], replicated, may hold values from -0.125 to 0.125
- down_bias: float32 [512], replicated, may hold values from -2 to 2
- cotangent: bfloat16 [4, 64, 512, 512], P('task', 'feat'), may hold values from -6 to 6
Outputs:
- output: bfloat16 [4, 64, 512, 512], P('task', 'feat')
- input_grad: float32 [4, 64, 512, 512], P('task', 'feat')
- sample_gain_grad: float32 [512], replicated
- sample_shift_grad: float32 [512], replicated
- sample_project_grad: float32 [512, 1536], replicated
- sample_output_grad: float32 [512, 512], replicated
- sample_bias_grad: float32 [512], replicated
- feature_gain_grad: float32 [512], replicated
- feature_shift_grad: float32 [512], replicated
- feature_project_grad: float32 [512, 1536], replicated
- feature_output_grad: float32 [512, 512], replicated
- feature_bias_grad: float32 [512], replicated
- dense_gain_grad: float32 [512], replicated
- dense_shift_grad: float32 [512], replicated
- up_weight_grad: float32 [512, 2048], replicated
- up_bias_grad: float32 [2048], replicated
- down_weight_grad: float32 [2048, 512], replicated
- down_bias_grad: float32 [512], replicated
The draws below stay inside these ranges and needn't reach their ends.
Inputs may be any that keep to these rules, and one draw needn't show every extreme that they name: In every draw one task has context 50 and another 500. `sample_mask`: sample 0 of every task is present.
All inputs are finite; a program needn't handle non-finite values.
Results may differ from the reference program's by a relative error of at most 0.015.
Values may be sent and summed in bfloat16 or wider, within the bound.
A program may use at most 384 MiB of HBM per device.

```python
import jax
import jax.numpy as jnp
from jax import lax

D = 512
HEADS = 8
HEAD = 64
FF = 2048
F = 64
S = 512
CTX_LEAST = 50
CTX_MOST = 500
TASKS = 4


def draw_context(key, part):
    key_one, key_two = jax.random.split(key)
    lengths = jax.random.randint(key_one, (TASKS,), CTX_LEAST, CTX_MOST + 1)
    ranking = jax.random.permutation(key_two, TASKS)
    lengths = lengths.at[ranking[0]].set(CTX_MOST)
    lengths = lengths.at[ranking[1]].set(CTX_LEAST)
    return lengths.astype(jnp.int32)


def draw_sample_mask(key, part):
    picked = jax.random.randint(key, (TASKS, S), 0, 16)
    column = lax.broadcasted_iota(jnp.int32, (TASKS, S), 1)
    return jnp.where((picked != 0) | (column == 0), 1, 0).astype(jnp.int32)


def block_levels(key, extent, shards, smallest, largest):
    factor_of, own = 1.0, jax.random.fold_in(key, 6)
    for dim, parts in shards:
        steps = jnp.exp(jax.random.uniform(jax.random.fold_in(own, dim), (parts,), jnp.float32, smallest / len(shards), largest / len(shards)))
        factor_of = factor_of * jnp.repeat(steps, extent[dim] // parts).reshape([-1 if axis == dim else 1 for axis in range(len(extent))])
    return factor_of


def normal_values(key, extent, scale, most, cuts=(), held_as=jnp.bfloat16):
    values = jax.random.normal(key, extent, jnp.float32) * scale
    if len(cuts) > 0:
        values = block_levels(key, extent, cuts, -0.22, 0.18) * values
    return jnp.clip(values, min=-most, max=most).astype(held_as)


def setup_inputs(seed: int = 0) -> dict:
    streams_of = jax.random.split(jax.random.key(seed), 21)
    return {
        "inputs": normal_values(streams_of[0], (TASKS, F, S, D), 1.0, 6.0, ((0, 4), (1, 8))),
        "context": draw_context(jax.random.fold_in(streams_of[20], 71), 0),
        "sample_mask": draw_sample_mask(jax.random.fold_in(streams_of[20], 71), 0),
        "sample_gain": jnp.clip(1.0 + 0.1 * jax.random.normal(streams_of[3], (D,), jnp.float32), 0.5, 1.5),
        "sample_shift": normal_values(streams_of[4], (D,), 0.3, 2.0, (), jnp.float32),
        "sample_project": normal_values(streams_of[5], (D, 3 * D), D ** -0.5, 0.25),
        "sample_output": normal_values(streams_of[6], (D, D), (D // 16) ** -0.5, 1.0),
        "sample_bias": normal_values(streams_of[7], (D,), 0.3, 2.0, (), jnp.float32),
        "feature_gain": jnp.clip(1.0 + 0.1 * jax.random.normal(streams_of[8], (D,), jnp.float32), 0.5, 1.5),
        "feature_shift": normal_values(streams_of[9], (D,), 0.3, 2.0, (), jnp.float32),
        "feature_project": normal_values(streams_of[10], (D, 3 * D), D ** -0.5, 0.25),
        "feature_output": normal_values(streams_of[11], (D, D), (D // 8) ** -0.5, 0.75),
        "feature_bias": normal_values(streams_of[12], (D,), 0.3, 2.0, (), jnp.float32),
        "dense_gain": jnp.clip(1.0 + 0.1 * jax.random.normal(streams_of[13], (D,), jnp.float32), 0.5, 1.5),
        "dense_shift": normal_values(streams_of[14], (D,), 0.3, 2.0, (), jnp.float32),
        "up_weight": normal_values(streams_of[15], (D, FF), D ** -0.5, 0.25),
        "up_bias": normal_values(streams_of[16], (FF,), 0.3, 2.0, (), jnp.float32),
        "down_weight": normal_values(streams_of[17], (FF, D), FF ** -0.5, 0.125),
        "down_bias": normal_values(streams_of[18], (D,), 0.3, 2.0, (), jnp.float32),
        "cotangent": normal_values(streams_of[19], (TASKS, F, S, D), 1.0, 6.0, ((0, 4), (1, 8))),
    }


EPSILON = 1e-05
HIGHEST = lax.Precision.HIGHEST

@jax.custom_vjp
def low(v):
    return lax.optimization_barrier(v.astype(jnp.bfloat16)).astype(jnp.float32)

@jax.custom_vjp
def low_back(v):
    return v

def low_keep(v):
    return (low(v), None)

def low_pass(kept, grad):
    return (grad,)

def back_keep(v):
    return (v, None)

def back_low(kept, grad):
    return (low(grad),)
low.defvjp(low_keep, low_pass)
low_back.defvjp(back_keep, back_low)

def norm_apply(token_rows, norm_gain, norm_shift):
    center = token_rows - lax.optimization_barrier(jnp.mean(token_rows, axis=-1, keepdims=True))
    spread = lax.optimization_barrier(jnp.mean(center * center, axis=-1, keepdims=True))
    return center * lax.rsqrt(spread + EPSILON) * norm_gain + norm_shift

def attend(hidden, norm_gain, norm_shift, input_weight, output_weight, output_bias, visible):
    full_shape = hidden.shape
    normed = low(norm_apply(hidden, norm_gain, norm_shift))
    packed = low(low_back(jnp.dot(normed, input_weight, precision=HIGHEST)))
    packed = packed.reshape(full_shape[:3] + (3, HEADS, HEAD))
    queries = packed[:, :, :, 0]
    key_rows = packed[:, :, :, 1]
    values = packed[:, :, :, 2]
    scores = jnp.einsum('bqche,bkche->bchqk', queries, key_rows, precision=HIGHEST) * HEAD ** (-0.5)
    scores = jnp.where(visible[:, None, None, None, :], low_back(scores), -1e+30)
    shares = low(jax.nn.softmax(scores, axis=-1))
    mixed = jnp.einsum('bchqk,bkche->bqche', shares, values, precision=HIGHEST).reshape(full_shape)
    mixed = low(low_back(mixed))
    return low_back(jnp.dot(mixed, output_weight, precision=HIGHEST) + output_bias)

def dense_branch(token_rows, norm_gain, norm_shift, up_matrix, up_vector, down_matrix, down_vector):
    normed = low(norm_apply(token_rows, norm_gain, norm_shift))
    pre_act = low_back(jnp.dot(normed, up_matrix, precision=HIGHEST) + up_vector)
    activated = low(jax.nn.gelu(pre_act))
    return low_back(jnp.dot(activated, down_matrix, precision=HIGHEST) + down_vector)

def reference(inputs, context, sample_mask, sample_gain, sample_shift, sample_project, sample_output, sample_bias, feature_gain, feature_shift, feature_project, feature_output, feature_bias, dense_gain, dense_shift, up_weight, up_bias, down_weight, down_bias, cotangent):
    position = jnp.arange(S, dtype=jnp.int32)
    task_keys = (position[None, :] < context[:, None]) & (sample_mask == 1)
    pair_keys = jnp.broadcast_to(task_keys[:, None, :], (TASKS, F, S)).reshape(TASKS * F // 8, 8, S)
    feature_keys = jnp.ones((1, F), jnp.bool_)
    sample_block = min(S, 4096 // F)
    weights = tuple((single.astype(jnp.float32) for single in (sample_gain, sample_shift, sample_project, sample_output, sample_bias, feature_gain, feature_shift, feature_project, feature_output, feature_bias, dense_gain, dense_shift, up_weight, up_bias, down_weight, down_bias)))

    def forward(stream_in, params):

        def sample_step(block_items):
            hidden, visible = block_items
            return hidden + attend(hidden, params[0], params[1], params[2], params[3], params[4], visible)
        grouped = stream_in.reshape(TASKS * F // 8, 8, S, 1, D)
        after_sample = lax.map(jax.checkpoint(sample_step), (grouped, pair_keys)).reshape(TASKS, F, S, D)
        sent = low(low_back(after_sample))
        blocks = sent.reshape(TASKS, F, S // sample_block, sample_block, D).transpose(0, 2, 1, 3, 4)
        blocks = blocks.reshape(-1, F, sample_block, D)

        def feature_step(hidden):
            hidden = hidden[None]
            middle = hidden + attend(hidden, params[5], params[6], params[7], params[8], params[9], feature_keys)
            token_rows = middle.reshape(-1, D)
            result = token_rows + dense_branch(token_rows, params[10], params[11], params[12], params[13], params[14], params[15])
            return result.reshape(hidden.shape[1:])
        result = lax.map(jax.checkpoint(feature_step), blocks)
        result = result.reshape(TASKS, S // sample_block, F, sample_block, D).transpose(0, 2, 1, 3, 4)
        return result.reshape(TASKS, F, S, D)
    output, pullback = jax.vjp(forward, inputs.astype(jnp.float32), weights)
    grad_input, grads = pullback(cotangent.astype(jnp.float32))
    return (output.astype(jnp.bfloat16), grad_input, grads[0], grads[1], grads[2], grads[3], grads[4], grads[5], grads[6], grads[7], grads[8], grads[9], grads[10], grads[11], grads[12], grads[13], grads[14], grads[15])
```

```python
import functools
import math

import jax
import jax.numpy as jnp
from jax import lax
from jax.experimental import pallas as pl
from jax.experimental.pallas import tpu as pltpu
from jax.sharding import PartitionSpec as P

HEADS = 8
HEAD = 64
PAIR = 2 * HEAD
EPSILON = 1e-05
SCALE = HEAD ** (-0.5)
POWER = SCALE * math.log2(math.e)
MASKED = -1e30
GELU_A = math.sqrt(2.0 / math.pi)
GELU_B = 0.044715
BF = jnp.bfloat16
F32 = jnp.float32
LIMIT = 60 * 1024 * 1024


def dot(left, right, left_dim, right_dim):
    return lax.dot_general(
        left, right, (((left_dim,), (right_dim,)), ((), ())), preferred_element_type=F32
    )


def normalize(rows):
    center = rows - jnp.mean(rows, axis=-1, keepdims=True)
    spread = jnp.mean(center * center, axis=-1, keepdims=True)
    inverse = lax.rsqrt(spread + EPSILON)
    return center * inverse, inverse


def normalize_back(grad_normed, gain, hat, inverse):
    scaled = grad_normed * gain
    middle = jnp.mean(scaled, axis=-1, keepdims=True)
    along = jnp.mean(scaled * hat, axis=-1, keepdims=True)
    grad_rows = inverse * (scaled - middle - hat * along)
    grad_gain = jnp.sum(grad_normed * hat, axis=0, keepdims=True)
    grad_shift = jnp.sum(grad_normed, axis=0, keepdims=True)
    return grad_rows, grad_gain, grad_shift


def pieces(row):
    high = row.astype(BF).astype(F32)
    rest = row - high
    middle = rest.astype(BF).astype(F32)
    return high, middle, rest - middle


def extra_rows(count, width, rows):
    place = lax.broadcasted_iota(jnp.int32, (16, width), 0)
    block = jnp.zeros((16, width), F32)
    for index, row in enumerate(rows):
        block = jnp.where(place == index, row, block)
    return jnp.concatenate([block.astype(BF), jnp.zeros((HEAD - 16, width), BF)], axis=0)


def half_ones(odd, depth):
    lane = lax.broadcasted_iota(jnp.int32, (depth, PAIR), 1)
    own = (lane >= HEAD) if odd else (lane < HEAD)
    return own.astype(F32).astype(BF)


def stack_half(odd, own, extra):
    return jnp.concatenate([extra, own] if odd else [own, extra], axis=0)


def extra_columns(odd, depth, columns):
    lane = lax.broadcasted_iota(jnp.int32, (depth, PAIR), 1)
    first = 0 if odd else HEAD
    block = jnp.zeros((depth, PAIR), F32)
    for index, column in enumerate(columns):
        block = jnp.where(lane == first + index, column, block)
    return block.astype(BF)


def attend_head(keys, left_extra, own, query_rows, extra, odd, value_rows):
    left = keys * own + left_extra
    scores = dot(left, stack_half(odd, query_rows, extra), 1, 0)
    highest = jnp.max(scores, axis=0, keepdims=True)
    weights = jnp.exp2((scores - highest) * POWER)
    totals = jnp.sum(weights, axis=0, keepdims=True)
    mixed = dot(value_rows, weights.astype(BF), 1, 0) / totals
    log_total = highest + jnp.log2(totals) * (1.0 / POWER)
    return mixed, log_total


def attend_head_back(left, right, value_left, value_right, query_rows, key_rows, grad_rows):
    shares = jnp.exp2(dot(left, right, 1, 0) * POWER)
    grad_shares = dot(value_left, value_right, 1, 0)
    low_scores = (shares * grad_shares).astype(BF)
    grad_values = dot(grad_rows, shares.astype(BF), 1, 1)
    grad_keys = dot(query_rows, low_scores, 1, 1) * SCALE
    grad_queries = dot(key_rows, low_scores, 1, 0) * SCALE
    return grad_queries, grad_keys, grad_values


def sample_forward_kernel(
    inputs_ref, mask_ref, gain_ref, shift_ref, query_w, key_w, value_w, output_w, bias_ref,
    sent_ref, saved_ref, mixed_ref, log_ref,
):
    rows = inputs_ref[0].astype(F32)
    samples, width = rows.shape
    hat, _ = normalize(rows)
    normed = (hat * gain_ref[...] + shift_ref[...]).astype(BF)
    saved_ref[0, 0] = dot(query_w[...], normed, 1, 1).astype(BF)
    saved_ref[0, 1] = dot(normed, key_w[...], 1, 0).astype(BF)
    saved_ref[0, 2] = dot(value_w[...], normed, 1, 1).astype(BF)
    mask = mask_ref[...]
    extra = extra_rows(1, samples, [jnp.ones((1, samples), F32)])
    for odd in (False, True):
        own = half_ones(odd, samples)
        left_extra = extra_columns(odd, samples, [mask])
        for pair in range(width // PAIR):
            head = 2 * pair + odd
            first = head * HEAD
            mixed, log_total = attend_head(
                saved_ref[0, 1, :, pair * PAIR:(pair + 1) * PAIR], left_extra, own,
                saved_ref[0, 0, first:first + HEAD, :], extra, odd,
                saved_ref[0, 2, first:first + HEAD, :],
            )
            mixed_ref[0, first:first + HEAD, :] = mixed.astype(BF)
            log_ref[0, head:head + 1, :] = log_total
    branch = dot(mixed_ref[0], output_w[...], 0, 0) + bias_ref[...]
    after = (inputs_ref[0].astype(F32) + branch).astype(BF)
    sent_ref[...] = after.reshape(sent_ref.shape)


def sample_backward_kernel(
    inputs_ref, mask_ref, gain_ref, shift_ref, project_t, output_w,
    saved_ref, mixed_ref, log_ref, grad_ref, result_ref,
    input_grad_ref, final_ref, project_grad, output_grad, vector_grad,
    project_sum, output_sum, packed_grad,
):
    step = pl.program_id(0)

    @pl.when(step == 0)
    def _():
        project_sum[...] = jnp.zeros_like(project_sum)
        output_sum[...] = jnp.zeros_like(output_sum)
        vector_grad[...] = jnp.zeros_like(vector_grad)

    samples, width = inputs_ref.shape[1:]
    final_ref[0] = result_ref[...].reshape(samples, width)
    low_grad = grad_ref[...].reshape(samples, width)
    output_sum[...] += dot(mixed_ref[0], low_grad, 1, 0)
    grad_mixed = dot(output_w[...], low_grad, 1, 1)
    low_mixed = grad_mixed.astype(BF)
    delta = (low_mixed.astype(F32) * mixed_ref[0].astype(F32))
    delta = jnp.sum(delta.reshape(width // HEAD, HEAD, samples), axis=1)
    mask = mask_ref[...]
    ones = jnp.ones((samples, 1), F32)
    one_row = jnp.ones((1, samples), F32)
    for odd in (False, True):
        own = half_ones(odd, samples)
        key_extra = extra_columns(odd, samples, [mask, ones, ones, ones])
        value_extra = extra_columns(odd, samples, [ones, ones, ones])
        for pair in range(width // PAIR):
            head = 2 * pair + odd
            first = head * HEAD
            lanes = slice(pair * PAIR, (pair + 1) * PAIR)
            query_rows = saved_ref[0, 0, first:first + HEAD, :]
            value_rows = saved_ref[0, 2, first:first + HEAD, :]
            grad_rows = low_mixed[first:first + HEAD, :]
            keys = saved_ref[0, 1, :, lanes]
            key_rows = keys.T[HEAD:] if odd else keys.T[:HEAD]
            high, middle, low = pieces(-log_ref[0, head:head + 1, :])
            right = stack_half(odd, query_rows, extra_rows(4, samples, [one_row, high, middle, low]))
            high, middle, low = pieces(-delta[head:head + 1, :])
            value_right = jnp.concatenate(
                [grad_rows, extra_rows(3, samples, [high, middle, low])], axis=0
            )
            value_left = jnp.concatenate(
                [value_rows, extra_rows(3, samples, [one_row] * 3)], axis=0
            )
            shares = jnp.exp2(dot(keys * own + key_extra, right, 1, 0) * POWER)
            grad_shares = dot(value_left, value_right, 0, 0)
            low_scores = (shares * grad_shares).astype(BF)
            packed_grad[2 * width + first:2 * width + first + HEAD, :] = dot(
                grad_rows, shares.astype(BF), 1, 1
            ).astype(BF)
            packed_grad[width + first:width + first + HEAD, :] = (
                dot(query_rows, low_scores, 1, 1) * SCALE
            ).astype(BF)
            packed_grad[first:first + HEAD, :] = (
                dot(key_rows, low_scores, 1, 0) * SCALE
            ).astype(BF)
    hat, inverse = normalize(inputs_ref[0].astype(F32))
    normed = (hat * gain_ref[...] + shift_ref[...]).astype(BF)
    project_sum[...] += dot(packed_grad[...], normed, 1, 0)
    grad_normed = dot(packed_grad[...], project_t[...], 0, 0)
    grad_rows, grad_gain, grad_shift = normalize_back(grad_normed, gain_ref[...], hat, inverse)
    stream = low_grad.astype(F32)
    input_grad_ref[0] = stream + grad_rows
    vector_grad[0:1, :] += grad_gain
    vector_grad[1:2, :] += grad_shift
    vector_grad[2:3, :] += jnp.sum(stream, axis=0, keepdims=True)

    @pl.when(step == pl.num_programs(0) - 1)
    def _():
        project_grad[...] = project_sum[...].T.astype(BF)
        output_grad[...] = output_sum[...].astype(BF)


def to_groups(block_ref, spare):
    features, group, width = block_ref.shape
    rows = block_ref[...].astype(F32).reshape(features * group, width)
    columns = []
    for lanes in range(width // 128):
        spare[lanes] = rows[:, lanes * 128:(lanes + 1) * 128]
        columns.append(
            jnp.concatenate(
                [spare[lanes, pl.ds(one, features, stride=group), :] for one in range(group)],
                axis=0,
            )
        )
    return jnp.concatenate(columns, axis=1)


def from_groups(rows, block_ref, spare):
    features, group, width = block_ref.shape
    for lanes in range(width // 128):
        span = slice(lanes * 128, (lanes + 1) * 128)
        for one in range(group):
            spare[lanes, pl.ds(one, features, stride=group), :] = rows[
                one * features:(one + 1) * features, span
            ]
        block_ref[:, :, span] = spare[lanes].reshape(features, group, 128).astype(BF)


def feature_kernel(
    stream_ref, cotangent_ref, gain_ref, shift_ref, query_w, key_w, value_w, project_t, output_w,
    bias_ref, dense_gain_ref, dense_shift_ref, up_ref, up_bias_ref, down_ref, down_bias_ref,
    result_ref, grad_ref, project_grad, output_grad, up_grad, down_grad, vector_grad, hidden_grad,
    project_sum, output_sum, up_sum, down_sum, spare, query_t, keys_s, value_t, mixed_t, logs,
    packed_grad,
):
    step = pl.program_id(0)
    chunks, width, chunk = up_ref.shape
    features, group = stream_ref.shape[:2]
    tokens = features * group
    joined = 2 * features

    @pl.when(step == 0)
    def _():
        project_sum[...] = jnp.zeros_like(project_sum)
        output_sum[...] = jnp.zeros_like(output_sum)
        up_sum[...] = jnp.zeros_like(up_sum)
        down_sum[...] = jnp.zeros_like(down_sum)
        vector_grad[...] = jnp.zeros_like(vector_grad)
        hidden_grad[...] = jnp.zeros_like(hidden_grad)

    rows = to_groups(stream_ref, spare)
    hat, inverse = normalize(rows)
    normed = (hat * gain_ref[...] + shift_ref[...]).astype(BF)
    query_t[...] = dot(query_w[...], normed, 1, 1).astype(BF)
    keys_s[...] = dot(normed, key_w[...], 1, 0).astype(BF)
    value_t[...] = dot(value_w[...], normed, 1, 1).astype(BF)
    place = lax.broadcasted_iota(jnp.int32, (joined, 1), 0)
    place_row = lax.broadcasted_iota(jnp.int32, (1, joined), 1)
    key_first = (place < features).astype(F32)
    key_second = (place >= features).astype(F32)
    hide_first = jnp.where(place_row >= features, MASKED, 0.0)
    hide_second = jnp.where(place_row < features, MASKED, 0.0)
    ones = jnp.ones((joined, 1), F32)
    one_row = jnp.ones((1, joined), F32)
    extra = extra_rows(2, joined, [hide_first, hide_second])
    for odd in (False, True):
        own = half_ones(odd, joined)
        left_extra = extra_columns(odd, joined, [key_first, key_second])
        for pair in range(width // PAIR):
            head = 2 * pair + odd
            first = head * HEAD
            for part in range(tokens // joined):
                span = slice(part * joined, (part + 1) * joined)
                mixed, log_total = attend_head(
                    keys_s[span, pair * PAIR:(pair + 1) * PAIR], left_extra, own,
                    query_t[first:first + HEAD, span], extra, odd,
                    value_t[first:first + HEAD, span],
                )
                mixed_t[first:first + HEAD, span] = mixed.astype(BF)
                logs[head:head + 1, span] = log_total
    after = rows + dot(mixed_t[...], output_w[...], 0, 0) + bias_ref[...]

    dense_hat, dense_inverse = normalize(after)
    dense_in = (dense_hat * dense_gain_ref[...] + dense_shift_ref[...]).astype(BF)
    stream = to_groups(cotangent_ref, spare)
    low_stream = stream.astype(BF)
    result = after + down_bias_ref[...]
    grad_dense = jnp.zeros((tokens, width), F32)
    for index in range(chunks):
        pre = dot(dense_in, up_ref[index], 1, 0) + up_bias_ref[index]
        square = pre * pre
        bend = jnp.tanh(pre * (GELU_A + (GELU_A * GELU_B) * square))
        half = 0.5 + 0.5 * bend
        activated = (pre * half).astype(BF)
        slope = half + (pre * half) * (1.0 - bend) * (GELU_A + (3.0 * GELU_A * GELU_B) * square)
        result = result + dot(activated, down_ref[index], 1, 0)
        grad_pre = (slope * dot(low_stream, down_ref[index], 1, 1)).astype(BF)
        grad_dense = grad_dense + dot(grad_pre, up_ref[index], 1, 1)
        down_sum[index] += dot(activated, low_stream, 0, 0)
        up_sum[index] += dot(dense_in, grad_pre, 0, 0)
        hidden_grad[index] += jnp.sum(grad_pre.astype(F32), axis=0, keepdims=True)
    from_groups(result, result_ref, spare)
    dense_rows, dense_gain_grad, dense_shift_grad = normalize_back(
        grad_dense, dense_gain_ref[...], dense_hat, dense_inverse
    )
    grad_after = stream + dense_rows

    low_grad = grad_after.astype(BF)
    output_sum[...] += dot(mixed_t[...], low_grad, 1, 0)
    low_mixed = dot(output_w[...], low_grad, 1, 1).astype(BF)
    delta = low_mixed.astype(F32) * mixed_t[...].astype(F32)
    delta = jnp.sum(delta.reshape(width // HEAD, HEAD, tokens), axis=1)
    for odd in (False, True):
        own = half_ones(odd, joined)
        key_extra = extra_columns(odd, joined, [key_first, key_second, ones, ones, ones])
        for pair in range(width // PAIR):
            head = 2 * pair + odd
            first = head * HEAD
            for part in range(tokens // joined):
                span = slice(part * joined, (part + 1) * joined)
                query_rows = query_t[first:first + HEAD, span]
                value_rows = value_t[first:first + HEAD, span]
                grad_rows = low_mixed[first:first + HEAD, span]
                keys = keys_s[span, pair * PAIR:(pair + 1) * PAIR]
                key_rows = keys.T[HEAD:] if odd else keys.T[:HEAD]
                high, middle, low = pieces(-logs[head:head + 1, span])
                right = stack_half(
                    odd, query_rows,
                    extra_rows(5, joined, [hide_first, hide_second, high, middle, low]),
                )
                high, middle, low = pieces(-delta[head:head + 1, span])
                value_right = jnp.concatenate(
                    [grad_rows, extra_rows(3, joined, [high, middle, low])], axis=0
                )
                value_left = jnp.concatenate(
                    [value_rows, extra_rows(3, joined, [one_row] * 3)], axis=0
                )
                shares = jnp.exp2(dot(keys * own + key_extra, right, 1, 0) * POWER)
                grad_shares = dot(value_left, value_right, 0, 0)
                low_scores = (shares * grad_shares).astype(BF)
                packed_grad[2 * width + first:2 * width + first + HEAD, span] = dot(
                    grad_rows, shares.astype(BF), 1, 1
                ).astype(BF)
                packed_grad[width + first:width + first + HEAD, span] = (
                    dot(query_rows, low_scores, 1, 1) * SCALE
                ).astype(BF)
                packed_grad[first:first + HEAD, span] = (
                    dot(key_rows, low_scores, 1, 0) * SCALE
                ).astype(BF)
    project_sum[...] += dot(packed_grad[...], normed, 1, 0)
    grad_normed = dot(packed_grad[...], project_t[...], 0, 0)
    grad_rows, gain_grad, shift_grad = normalize_back(grad_normed, gain_ref[...], hat, inverse)
    from_groups(grad_after + grad_rows, grad_ref, spare)
    vector_grad[0:1, :] += gain_grad
    vector_grad[1:2, :] += shift_grad
    vector_grad[2:3, :] += jnp.sum(low_grad.astype(F32), axis=0, keepdims=True)
    vector_grad[3:4, :] += dense_gain_grad
    vector_grad[4:5, :] += dense_shift_grad
    vector_grad[5:6, :] += jnp.sum(stream, axis=0, keepdims=True)

    @pl.when(step == pl.num_programs(0) - 1)
    def _():
        project_grad[...] = project_sum[...].T.astype(BF)
        output_grad[...] = output_sum[...].astype(BF)
        up_grad[...] = up_sum[...].astype(BF)
        down_grad[...] = down_sum[...].astype(BF)


def whole(shape):
    return pl.BlockSpec(shape, lambda step: (0,) * len(shape), pipeline_mode=pl.Buffered(1))


def whole_out(shape):
    return pl.BlockSpec(shape, lambda step: (0,) * len(shape))


def call(kernel, grid, in_specs, out_specs, out_shape, scratch, name, flops, nbytes):
    return pl.pallas_call(
        kernel,
        grid=(grid,),
        in_specs=in_specs,
        out_specs=out_specs,
        out_shape=[jax.ShapeDtypeStruct(*one) for one in out_shape],
        scratch_shapes=scratch,
        compiler_params=pltpu.CompilerParams(
            dimension_semantics=("arbitrary",), vmem_limit_bytes=LIMIT
        ),
        cost_estimate=pl.CostEstimate(flops=flops, bytes_accessed=nbytes, transcendentals=0),
        name=name,
    )


def split_project(project):
    width = project.shape[0]
    return (
        project[:, :width].T, project[:, width:2 * width], project[:, 2 * width:].T, project.T
    )


def body(
    peers,
    inputs, context, sample_mask,
    sample_gain, sample_shift, sample_project, sample_output, sample_bias,
    feature_gain, feature_shift, feature_project, feature_output, feature_bias,
    dense_gain, dense_shift, up_weight, up_bias, down_weight, down_bias,
    cotangent,
):
    _, local, samples, width = inputs.shape
    hidden = up_weight.shape[1]
    features = local * peers
    share = samples // peers
    group = 8
    chunk = 512
    chunks = hidden // chunk
    row = lambda vector: vector.reshape(1, -1)
    exchange = functools.partial(lax.all_to_all, axis_name="feat", tiled=True)

    position = lax.iota(jnp.int32, samples)
    visible = (position < context[0]) & (sample_mask[0] == 1)
    mask = jnp.where(visible, 0.0, MASKED).astype(F32).reshape(samples, 1)
    query_w, key_w, value_w, project_t = split_project(sample_project)
    tokens = inputs[0]
    grad_seen = exchange(cotangent[0], split_axis=1, concat_axis=0)

    square = whole((width, width))
    line = whole((1, width))
    token_spec = pl.BlockSpec((1, samples, width), lambda step: (step, 0, 0))
    peer_spec = pl.BlockSpec((peers, 1, share, width), lambda step: (0, step, 0, 0))
    saved_spec = pl.BlockSpec((1, 3, samples, width), lambda step: (step, 0, 0, 0))
    log_spec = pl.BlockSpec((1, HEADS, samples), lambda step: (step, 0, 0))
    sent, saved, mixed, logs = call(
        sample_forward_kernel, local,
        [token_spec, whole((samples, 1)), line, line, square, square, square, square, line],
        [peer_spec, saved_spec, token_spec, log_spec],
        [
            ((peers, local, share, width), BF), ((local, 3, samples, width), BF),
            ((local, width, samples), BF), ((local, HEADS, samples), F32),
        ],
        [], "sample_forward", 60_000_000_000, 30_000_000,
    )(
        tokens, mask, row(sample_gain), row(sample_shift), query_w, key_w, value_w,
        sample_output, row(sample_bias),
    )
    seen = exchange(sent, split_axis=0, concat_axis=0)

    query_f, key_f, value_f, project_ft = split_project(feature_project)
    block_tokens = features * group
    block_spec = pl.BlockSpec((features, group, width), lambda step: (0, step, 0))
    up_chunks = up_weight.reshape(width, chunks, chunk).transpose(1, 0, 2)
    down_chunks = down_weight.reshape(chunks, chunk, width)
    (
        result, grad_sent, feature_project_grad, feature_output_grad, up_grad, down_grad,
        feature_vectors, hidden_grad,
    ) = call(
        feature_kernel, share // group,
        [
            block_spec, block_spec, line, line, square, square, square, whole((3 * width, width)),
            square, line, line, line, whole((chunks, width, chunk)), whole((chunks, 1, chunk)),
            whole((chunks, chunk, width)), line,
        ],
        [
            block_spec, block_spec, whole_out((width, 3 * width)), whole_out((width, width)),
            whole_out((chunks, width, chunk)), whole_out((chunks, chunk, width)),
            whole_out((8, width)), whole_out((chunks, 1, chunk)),
        ],
        [
            ((features, share, width), BF), ((features, share, width), BF),
            ((width, 3 * width), BF), ((width, width), BF),
            ((chunks, width, chunk), BF), ((chunks, chunk, width), BF),
            ((8, width), F32), ((chunks, 1, chunk), F32),
        ],
        [
            pltpu.VMEM((3 * width, width), F32), pltpu.VMEM((width, width), F32),
            pltpu.VMEM((chunks, width, chunk), F32), pltpu.VMEM((chunks, chunk, width), F32),
            pltpu.VMEM((width // 128, block_tokens, 128), F32),
            pltpu.VMEM((width, block_tokens), BF),
            pltpu.VMEM((block_tokens, width), BF), pltpu.VMEM((width, block_tokens), BF),
            pltpu.VMEM((width, block_tokens), BF), pltpu.VMEM((HEADS, block_tokens), F32),
            pltpu.VMEM((3 * width, block_tokens), BF),
        ],
        "feature_block", 130_000_000_000, 40_000_000,
    )(
        seen.reshape(features, share, width), grad_seen.reshape(features, share, width),
        row(feature_gain), row(feature_shift), query_f, key_f, value_f, project_ft,
        feature_output, row(feature_bias), row(dense_gain), row(dense_shift),
        up_chunks, up_bias.reshape(chunks, 1, chunk), down_chunks, row(down_bias),
    )
    peer_shape = (peers, local, share, width)
    grad_returned = exchange(grad_sent.reshape(peer_shape), split_axis=0, concat_axis=0)
    result_returned = exchange(result.reshape(peer_shape), split_axis=0, concat_axis=0)

    everyone = ("task", "feat")
    up_grad, down_grad, feature_project_grad, feature_output_grad = lax.psum(
        (up_grad, down_grad, feature_project_grad, feature_output_grad), everyone
    )
    (
        input_grad, output, sample_project_grad, sample_output_grad, sample_vectors,
    ) = call(
        sample_backward_kernel, local,
        [
            token_spec, whole((samples, 1)), line, line, whole((3 * width, width)), square,
            saved_spec, token_spec, log_spec, peer_spec, peer_spec,
        ],
        [
            token_spec, token_spec, whole_out((width, 3 * width)), whole_out((width, width)),
            whole_out((8, width)),
        ],
        [
            ((local, samples, width), F32), ((local, samples, width), BF),
            ((width, 3 * width), BF), ((width, width), BF), ((8, width), F32),
        ],
        [
            pltpu.VMEM((3 * width, width), F32), pltpu.VMEM((width, width), F32),
            pltpu.VMEM((3 * width, samples), BF),
        ],
        "sample_backward", 110_000_000_000, 50_000_000,
    )(
        tokens, mask, row(sample_gain), row(sample_shift), project_t, sample_output,
        saved, mixed, logs, grad_returned, result_returned,
    )
    vectors = jnp.concatenate(
        [sample_vectors, feature_vectors, hidden_grad.reshape(chunks, width)], axis=0
    )
    sample_project_grad, sample_output_grad = lax.psum(
        (sample_project_grad, sample_output_grad), everyone
    )
    vectors = lax.psum(vectors, everyone)
    wide = lambda array: array.astype(F32)
    return (
        output[None], input_grad[None],
        vectors[0], vectors[1], wide(sample_project_grad), wide(sample_output_grad), vectors[2],
        vectors[8], vectors[9], wide(feature_project_grad), wide(feature_output_grad), vectors[10],
        vectors[11], vectors[12],
        wide(up_grad).transpose(1, 0, 2).reshape(width, hidden), vectors[16:].reshape(hidden),
        wide(down_grad).reshape(hidden, width), vectors[13],
    )


def solution(mesh):
    split = P("task", "feat", None, None)
    return jax.shard_map(
        functools.partial(body, mesh.shape["feat"]),
        mesh=mesh,
        in_specs=(split, P("task"), P("task", None)) + (P(),) * 16 + (split,),
        out_specs=(split, split) + (P(),) * 16,
        check_vma=False,
    )
```

```python
import functools
import math

import jax
import jax.numpy as jnp
from jax import lax
from jax.experimental import pallas as pl
from jax.experimental.pallas import tpu as pltpu
from jax.sharding import PartitionSpec as P

HEADS = 8
HEAD = 64
PAIR = 2 * HEAD
EPSILON = 1e-05
SCALE = HEAD ** (-0.5)
POWER = SCALE * math.log2(math.e)
MASKED = -1e30
GELU_A = math.sqrt(2.0 / math.pi)
GELU_B = 0.044715
BF = jnp.bfloat16
F32 = jnp.float32
LIMIT = 60 * 1024 * 1024
MESH = pl.DeviceIdType.MESH


def dot(left, right, left_dim, right_dim):
    return lax.dot_general(
        left, right, (((left_dim,), (right_dim,)), ((), ())), preferred_element_type=F32
    )


def normalize(rows):
    center = rows - jnp.mean(rows, axis=-1, keepdims=True)
    spread = jnp.mean(center * center, axis=-1, keepdims=True)
    inverse = lax.rsqrt(spread + EPSILON)
    return center * inverse, inverse


def normalize_back(grad_normed, gain, hat, inverse):
    scaled = grad_normed * gain
    middle = jnp.mean(scaled, axis=-1, keepdims=True)
    along = jnp.mean(scaled * hat, axis=-1, keepdims=True)
    grad_rows = inverse * (scaled - middle - hat * along)
    grad_gain = jnp.sum(grad_normed * hat, axis=0, keepdims=True)
    grad_shift = jnp.sum(grad_normed, axis=0, keepdims=True)
    return grad_rows, grad_gain, grad_shift


def pieces(row):
    high = row.astype(BF).astype(F32)
    rest = row - high
    middle = rest.astype(BF).astype(F32)
    return high, middle, rest - middle


def extra_rows(count, width, rows):
    place = lax.broadcasted_iota(jnp.int32, (16, width), 0)
    block = jnp.zeros((16, width), F32)
    for index, row in enumerate(rows):
        block = jnp.where(place == index, row, block)
    return jnp.concatenate([block.astype(BF), jnp.zeros((HEAD - 16, width), BF)], axis=0)


def half_ones(odd, depth):
    lane = lax.broadcasted_iota(jnp.int32, (depth, PAIR), 1)
    own = (lane >= HEAD) if odd else (lane < HEAD)
    return own.astype(F32).astype(BF)


def stack_half(odd, own, extra):
    return jnp.concatenate([extra, own] if odd else [own, extra], axis=0)


def extra_columns(odd, depth, columns):
    lane = lax.broadcasted_iota(jnp.int32, (depth, PAIR), 1)
    first = 0 if odd else HEAD
    block = jnp.zeros((depth, PAIR), F32)
    for index, column in enumerate(columns):
        block = jnp.where(lane == first + index, column, block)
    return block.astype(BF)


def attend_head(keys, left_extra, own, query_rows, extra, odd, value_rows):
    left = keys * own + left_extra
    scores = dot(left, stack_half(odd, query_rows, extra), 1, 0)
    highest = jnp.max(scores, axis=0, keepdims=True)
    weights = jnp.exp2((scores - highest) * POWER)
    totals = jnp.sum(weights, axis=0, keepdims=True)
    mixed = dot(value_rows, weights.astype(BF), 1, 0) / totals
    log_total = highest + jnp.log2(totals) * (1.0 / POWER)
    return mixed, log_total


def attend_head_back(left, right, value_left, value_right, query_rows, key_rows, grad_rows):
    shares = jnp.exp2(dot(left, right, 1, 0) * POWER)
    grad_shares = dot(value_left, value_right, 1, 0)
    low_scores = (shares * grad_shares).astype(BF)
    grad_values = dot(grad_rows, shares.astype(BF), 1, 1)
    grad_keys = dot(query_rows, low_scores, 1, 1) * SCALE
    grad_queries = dot(key_rows, low_scores, 1, 0) * SCALE
    return grad_queries, grad_keys, grad_values


def push(source, target, send_sem, recv_sem, peer):
    return pltpu.make_async_remote_copy(
        src_ref=source, dst_ref=target, send_sem=send_sem, recv_sem=recv_sem,
        device_id={"feat": peer}, device_id_type=MESH,
    )


def greet(peers, me):
    barrier = pltpu.get_barrier_semaphore()
    for hop in range(1, peers):
        pl.semaphore_signal(
            barrier, inc=1, device_id={"feat": (me + hop) % peers}, device_id_type=MESH
        )
    pl.semaphore_wait(barrier, peers - 1)


def arrived(buffer, sem):
    pltpu.make_async_copy(buffer, buffer, sem).wait()


def sample_forward_kernel(
    peers,
    inputs_ref, mask_ref, gain_ref, shift_ref, query_w, key_w, value_w, output_w, bias_ref,
    seen_ref, saved_ref, mixed_ref, log_ref,
    outbox, send_sems, recv_sems, own_sems,
):
    step = pl.program_id(0)
    steps = pl.num_programs(0)
    slot = step % 2
    me = lax.axis_index("feat")

    @pl.when(step == 0)
    def _():
        greet(peers, me)

    def moves(at, slot):
        sends = []
        for hop in range(1, peers):
            peer = (me + hop) % peers
            sends.append(
                push(
                    outbox.at[slot, peer], seen_ref.at[me, at],
                    send_sems.at[slot, hop], recv_sems.at[hop], peer,
                )
            )
        own = pltpu.make_async_copy(outbox.at[slot, me], seen_ref.at[me, at], own_sems.at[slot])
        return sends, own

    def drain(at, slot):
        sends, own = moves(at, slot)
        for send in sends:
            send.wait_send()
        own.wait()

    rows = inputs_ref[0].astype(F32)
    samples, width = rows.shape
    hat, _ = normalize(rows)
    normed = (hat * gain_ref[...] + shift_ref[...]).astype(BF)
    saved_ref[0, 0] = dot(query_w[...], normed, 1, 1).astype(BF)
    saved_ref[0, 1] = dot(normed, key_w[...], 1, 0).astype(BF)
    saved_ref[0, 2] = dot(value_w[...], normed, 1, 1).astype(BF)
    mask = mask_ref[...]
    extra = extra_rows(1, samples, [jnp.ones((1, samples), F32)])
    for odd in (False, True):
        own = half_ones(odd, samples)
        left_extra = extra_columns(odd, samples, [mask])
        for pair in range(width // PAIR):
            head = 2 * pair + odd
            first = head * HEAD
            mixed, log_total = attend_head(
                saved_ref[0, 1, :, pair * PAIR:(pair + 1) * PAIR], left_extra, own,
                saved_ref[0, 0, first:first + HEAD, :], extra, odd,
                saved_ref[0, 2, first:first + HEAD, :],
            )
            mixed_ref[0, first:first + HEAD, :] = mixed.astype(BF)
            log_ref[0, head:head + 1, :] = log_total
    branch = dot(mixed_ref[0], output_w[...], 0, 0) + bias_ref[...]
    after = (inputs_ref[0].astype(F32) + branch).astype(BF)

    @pl.when(step >= 2)
    def _():
        drain(step - 2, slot)

    outbox[slot] = after.reshape(outbox.shape[1:])
    sends, own = moves(step, slot)
    for send in sends:
        send.start()
    own.start()

    @pl.when(step == steps - 1)
    def _():
        drain(step, slot)
        if seen_ref.shape[1] > 1:
            drain(step - 1, 1 - slot)
        for hop in range(1, peers):
            arrived(seen_ref.at[(me + peers - hop) % peers], recv_sems.at[hop])


def sample_backward_kernel(
    inputs_ref, mask_ref, gain_ref, shift_ref, project_t, output_w,
    saved_ref, mixed_ref, log_ref, grad_ref, result_ref,
    input_grad_ref, final_ref, project_grad, output_grad, vector_grad,
    project_sum, output_sum, packed_grad,
):
    step = pl.program_id(0)

    @pl.when(step == 0)
    def _():
        project_sum[...] = jnp.zeros_like(project_sum)
        output_sum[...] = jnp.zeros_like(output_sum)
        vector_grad[...] = jnp.zeros_like(vector_grad)

    samples, width = inputs_ref.shape[1:]
    final_ref[0] = result_ref[...].reshape(samples, width)
    low_grad = grad_ref[...].reshape(samples, width)
    output_sum[...] += dot(mixed_ref[0], low_grad, 1, 0)
    grad_mixed = dot(output_w[...], low_grad, 1, 1)
    low_mixed = grad_mixed.astype(BF)
    delta = (low_mixed.astype(F32) * mixed_ref[0].astype(F32))
    delta = jnp.sum(delta.reshape(width // HEAD, HEAD, samples), axis=1)
    mask = mask_ref[...]
    ones = jnp.ones((samples, 1), F32)
    one_row = jnp.ones((1, samples), F32)
    for odd in (False, True):
        own = half_ones(odd, samples)
        key_extra = extra_columns(odd, samples, [mask, ones, ones, ones])
        value_extra = extra_columns(odd, samples, [ones, ones, ones])
        for pair in range(width // PAIR):
            head = 2 * pair + odd
            first = head * HEAD
            lanes = slice(pair * PAIR, (pair + 1) * PAIR)
            query_rows = saved_ref[0, 0, first:first + HEAD, :]
            value_rows = saved_ref[0, 2, first:first + HEAD, :]
            grad_rows = low_mixed[first:first + HEAD, :]
            keys = saved_ref[0, 1, :, lanes]
            key_rows = keys.T[HEAD:] if odd else keys.T[:HEAD]
            high, middle, low = pieces(-log_ref[0, head:head + 1, :])
            right = stack_half(odd, query_rows, extra_rows(4, samples, [one_row, high, middle, low]))
            high, middle, low = pieces(-delta[head:head + 1, :])
            value_right = jnp.concatenate(
                [grad_rows, extra_rows(3, samples, [high, middle, low])], axis=0
            )
            value_left = jnp.concatenate(
                [value_rows, extra_rows(3, samples, [one_row] * 3)], axis=0
            )
            shares = jnp.exp2(dot(keys * own + key_extra, right, 1, 0) * POWER)
            grad_shares = dot(value_left, value_right, 0, 0)
            low_scores = (shares * grad_shares).astype(BF)
            packed_grad[2 * width + first:2 * width + first + HEAD, :] = dot(
                grad_rows, shares.astype(BF), 1, 1
            ).astype(BF)
            packed_grad[width + first:width + first + HEAD, :] = (
                dot(query_rows, low_scores, 1, 1) * SCALE
            ).astype(BF)
            packed_grad[first:first + HEAD, :] = (
                dot(key_rows, low_scores, 1, 0) * SCALE
            ).astype(BF)
    hat, inverse = normalize(inputs_ref[0].astype(F32))
    normed = (hat * gain_ref[...] + shift_ref[...]).astype(BF)
    project_sum[...] += dot(packed_grad[...], normed, 1, 0)
    grad_normed = dot(packed_grad[...], project_t[...], 0, 0)
    grad_rows, grad_gain, grad_shift = normalize_back(grad_normed, gain_ref[...], hat, inverse)
    stream = low_grad.astype(F32)
    input_grad_ref[0] = stream + grad_rows
    vector_grad[0:1, :] += grad_gain
    vector_grad[1:2, :] += grad_shift
    vector_grad[2:3, :] += jnp.sum(stream, axis=0, keepdims=True)

    @pl.when(step == pl.num_programs(0) - 1)
    def _():
        project_grad[...] = project_sum[...].T.astype(BF)
        output_grad[...] = output_sum[...].astype(BF)


def to_groups(block_ref, spare):
    features, group, width = block_ref.shape
    rows = block_ref[...].astype(F32).reshape(features * group, width)
    columns = []
    for lanes in range(width // 128):
        spare[lanes] = rows[:, lanes * 128:(lanes + 1) * 128]
        columns.append(
            jnp.concatenate(
                [spare[lanes, pl.ds(one, features, stride=group), :] for one in range(group)],
                axis=0,
            )
        )
    return jnp.concatenate(columns, axis=1)


def from_groups(rows, block_ref, spare):
    features, group, width = block_ref.shape
    for lanes in range(width // 128):
        span = slice(lanes * 128, (lanes + 1) * 128)
        for one in range(group):
            spare[lanes, pl.ds(one, features, stride=group), :] = rows[
                one * features:(one + 1) * features, span
            ]
        block_ref[:, :, span] = spare[lanes].reshape(features, group, 128).astype(BF)


def feature_kernel(
    peers,
    stream_ref, cotangent_hbm, gain_ref, shift_ref, query_w, key_w, value_w, project_t, output_w,
    bias_ref, dense_gain_ref, dense_shift_ref, up_ref, up_bias_ref, down_ref, down_bias_ref,
    results_ref, grads_ref, project_grad, output_grad, up_grad, down_grad, vector_grad, hidden_grad,
    project_sum, output_sum, up_sum, down_sum, spare, query_t, keys_s, value_t, mixed_t, logs,
    packed_grad, cotangents, result_box, grad_box,
    cotangent_sends, cotangent_recvs, result_sends, grad_sends, result_recvs, grad_recvs, own_sems,
):
    step = pl.program_id(0)
    steps, features, group, _ = cotangents.shape
    slot = step % 2
    me = lax.axis_index("feat")
    local = features // peers
    share = steps * group
    chunks, width, chunk = up_ref.shape
    tokens = features * group
    joined = 2 * features

    def cotangent_moves(at, own=False):
        def part(peer):
            return cotangent_hbm.at[:, pl.ds(pl.multiple_of(peer * share + at * group, group), group), :]

        inbox = cotangents.at[at, pl.ds(me * local, local)]
        if own:
            return pltpu.make_async_copy(part(me), inbox, cotangent_recvs.at[at])
        sends = []
        for hop in range(1, peers):
            peer = (me + hop) % peers
            sends.append(
                push(part(peer), inbox, cotangent_sends.at[at % 2, hop], cotangent_recvs.at[at], peer)
            )
        return sends

    def start_cotangent(at):
        for send in cotangent_moves(at):
            send.start()
        cotangent_moves(at, own=True).start()

    def back_moves(at, slot, box, target, send_sems, recv_sems, own_sem):
        place = target.at[me, :, pl.ds(pl.multiple_of(at * group, group), group), :]
        sends = []
        for hop in range(1, peers):
            peer = (me + hop) % peers
            sends.append(
                push(
                    box.at[slot, pl.ds(peer * local, local)], place,
                    send_sems.at[slot, hop], recv_sems.at[hop], peer,
                )
            )
        own = pltpu.make_async_copy(box.at[slot, pl.ds(me * local, local)], place, own_sem)
        return sends, own

    def result_moves(at, slot):
        return back_moves(
            at, slot, result_box, results_ref, result_sends, result_recvs, own_sems.at[0, slot]
        )

    def grad_moves(at, slot):
        return back_moves(
            at, slot, grad_box, grads_ref, grad_sends, grad_recvs, own_sems.at[1, slot]
        )

    def begin(moves):
        sends, own = moves
        for send in sends:
            send.start()
        own.start()

    def drain(moves):
        sends, own = moves
        for send in sends:
            send.wait_send()
        own.wait()

    @pl.when(step == 0)
    def _():
        greet(peers, me)
        start_cotangent(0)

    @pl.when(step + 1 < steps)
    def _():
        @pl.when(step >= 1)
        def _():
            for send in cotangent_moves(step - 1):
                send.wait_send()

        start_cotangent(step + 1)

    @pl.when(step == 0)
    def _():
        project_sum[...] = jnp.zeros_like(project_sum)
        output_sum[...] = jnp.zeros_like(output_sum)
        up_sum[...] = jnp.zeros_like(up_sum)
        down_sum[...] = jnp.zeros_like(down_sum)
        vector_grad[...] = jnp.zeros_like(vector_grad)
        hidden_grad[...] = jnp.zeros_like(hidden_grad)

    rows = to_groups(stream_ref, spare)
    hat, inverse = normalize(rows)
    normed = (hat * gain_ref[...] + shift_ref[...]).astype(BF)
    query_t[...] = dot(query_w[...], normed, 1, 1).astype(BF)
    keys_s[...] = dot(normed, key_w[...], 1, 0).astype(BF)
    value_t[...] = dot(value_w[...], normed, 1, 1).astype(BF)
    place = lax.broadcasted_iota(jnp.int32, (joined, 1), 0)
    place_row = lax.broadcasted_iota(jnp.int32, (1, joined), 1)
    key_first = (place < features).astype(F32)
    key_second = (place >= features).astype(F32)
    hide_first = jnp.where(place_row >= features, MASKED, 0.0)
    hide_second = jnp.where(place_row < features, MASKED, 0.0)
    ones = jnp.ones((joined, 1), F32)
    one_row = jnp.ones((1, joined), F32)
    extra = extra_rows(2, joined, [hide_first, hide_second])
    for odd in (False, True):
        own = half_ones(odd, joined)
        left_extra = extra_columns(odd, joined, [key_first, key_second])
        for pair in range(width // PAIR):
            head = 2 * pair + odd
            first = head * HEAD
            for part in range(tokens // joined):
                span = slice(part * joined, (part + 1) * joined)
                mixed, log_total = attend_head(
                    keys_s[span, pair * PAIR:(pair + 1) * PAIR], left_extra, own,
                    query_t[first:first + HEAD, span], extra, odd,
                    value_t[first:first + HEAD, span],
                )
                mixed_t[first:first + HEAD, span] = mixed.astype(BF)
                logs[head:head + 1, span] = log_total
    after = rows + dot(mixed_t[...], output_w[...], 0, 0) + bias_ref[...]

    dense_hat, dense_inverse = normalize(after)
    dense_in = (dense_hat * dense_gain_ref[...] + dense_shift_ref[...]).astype(BF)
    arrived(cotangents.at[step], cotangent_recvs.at[step])
    stream = to_groups(cotangents.at[step], spare)
    low_stream = stream.astype(BF)
    result = after + down_bias_ref[...]
    grad_dense = jnp.zeros((tokens, width), F32)
    for index in range(chunks):
        pre = dot(dense_in, up_ref[index], 1, 0) + up_bias_ref[index]
        square = pre * pre
        bend = jnp.tanh(pre * (GELU_A + (GELU_A * GELU_B) * square))
        half = 0.5 + 0.5 * bend
        activated = (pre * half).astype(BF)
        slope = half + (pre * half) * (1.0 - bend) * (GELU_A + (3.0 * GELU_A * GELU_B) * square)
        result = result + dot(activated, down_ref[index], 1, 0)
        grad_pre = (slope * dot(low_stream, down_ref[index], 1, 1)).astype(BF)
        grad_dense = grad_dense + dot(grad_pre, up_ref[index], 1, 1)
        down_sum[index] += dot(activated, low_stream, 0, 0)
        up_sum[index] += dot(dense_in, grad_pre, 0, 0)
        hidden_grad[index] += jnp.sum(grad_pre.astype(F32), axis=0, keepdims=True)

    @pl.when(step >= 2)
    def _():
        drain(result_moves(step - 2, slot))
        drain(grad_moves(step - 2, slot))

    from_groups(result, result_box.at[slot], spare)
    begin(result_moves(step, slot))
    dense_rows, dense_gain_grad, dense_shift_grad = normalize_back(
        grad_dense, dense_gain_ref[...], dense_hat, dense_inverse
    )
    grad_after = stream + dense_rows

    low_grad = grad_after.astype(BF)
    output_sum[...] += dot(mixed_t[...], low_grad, 1, 0)
    low_mixed = dot(output_w[...], low_grad, 1, 1).astype(BF)
    delta = low_mixed.astype(F32) * mixed_t[...].astype(F32)
    delta = jnp.sum(delta.reshape(width // HEAD, HEAD, tokens), axis=1)
    for odd in (False, True):
        own = half_ones(odd, joined)
        key_extra = extra_columns(odd, joined, [key_first, key_second, ones, ones, ones])
        for pair in range(width // PAIR):
            head = 2 * pair + odd
            first = head * HEAD
            for part in range(tokens // joined):
                span = slice(part * joined, (part + 1) * joined)
                query_rows = query_t[first:first + HEAD, span]
                value_rows = value_t[first:first + HEAD, span]
                grad_rows = low_mixed[first:first + HEAD, span]
                keys = keys_s[span, pair * PAIR:(pair + 1) * PAIR]
                key_rows = keys.T[HEAD:] if odd else keys.T[:HEAD]
                high, middle, low = pieces(-logs[head:head + 1, span])
                right = stack_half(
                    odd, query_rows,
                    extra_rows(5, joined, [hide_first, hide_second, high, middle, low]),
                )
                high, middle, low = pieces(-delta[head:head + 1, span])
                value_right = jnp.concatenate(
                    [grad_rows, extra_rows(3, joined, [high, middle, low])], axis=0
                )
                value_left = jnp.concatenate(
                    [value_rows, extra_rows(3, joined, [one_row] * 3)], axis=0
                )
                shares = jnp.exp2(dot(keys * own + key_extra, right, 1, 0) * POWER)
                grad_shares = dot(value_left, value_right, 0, 0)
                low_scores = (shares * grad_shares).astype(BF)
                packed_grad[2 * width + first:2 * width + first + HEAD, span] = dot(
                    grad_rows, shares.astype(BF), 1, 1
                ).astype(BF)
                packed_grad[width + first:width + first + HEAD, span] = (
                    dot(query_rows, low_scores, 1, 1) * SCALE
                ).astype(BF)
                packed_grad[first:first + HEAD, span] = (
                    dot(key_rows, low_scores, 1, 0) * SCALE
                ).astype(BF)
    project_sum[...] += dot(packed_grad[...], normed, 1, 0)
    grad_normed = dot(packed_grad[...], project_t[...], 0, 0)
    grad_rows, gain_grad, shift_grad = normalize_back(grad_normed, gain_ref[...], hat, inverse)
    from_groups(grad_after + grad_rows, grad_box.at[slot], spare)
    begin(grad_moves(step, slot))
    vector_grad[0:1, :] += gain_grad
    vector_grad[1:2, :] += shift_grad
    vector_grad[2:3, :] += jnp.sum(low_grad.astype(F32), axis=0, keepdims=True)
    vector_grad[3:4, :] += dense_gain_grad
    vector_grad[4:5, :] += dense_shift_grad
    vector_grad[5:6, :] += jnp.sum(stream, axis=0, keepdims=True)

    @pl.when(step == pl.num_programs(0) - 1)
    def _():
        project_grad[...] = project_sum[...].T.astype(BF)
        output_grad[...] = output_sum[...].astype(BF)
        up_grad[...] = up_sum[...].astype(BF)
        down_grad[...] = down_sum[...].astype(BF)
        for send in cotangent_moves(step):
            send.wait_send()
        drain(result_moves(step, slot))
        drain(grad_moves(step, slot))
        if steps > 1:
            for send in cotangent_moves(step - 1):
                send.wait_send()
            drain(result_moves(step - 1, 1 - slot))
            drain(grad_moves(step - 1, 1 - slot))
        for hop in range(1, peers):
            source = (me + peers - hop) % peers
            arrived(results_ref.at[source], result_recvs.at[hop])
            arrived(grads_ref.at[source], grad_recvs.at[hop])


def whole(shape):
    return pl.BlockSpec(shape, lambda step: (0,) * len(shape), pipeline_mode=pl.Buffered(1))


def whole_out(shape):
    return pl.BlockSpec(shape, lambda step: (0,) * len(shape))


def call(kernel, grid, in_specs, out_specs, out_shape, scratch, name, flops, nbytes, remote=None):
    return pl.pallas_call(
        kernel,
        grid=(grid,),
        in_specs=in_specs,
        out_specs=out_specs,
        out_shape=[jax.ShapeDtypeStruct(*one) for one in out_shape],
        scratch_shapes=scratch,
        compiler_params=pltpu.CompilerParams(
            dimension_semantics=("arbitrary",), vmem_limit_bytes=LIMIT,
            collective_id=remote, has_side_effects=remote is not None,
        ),
        cost_estimate=pl.CostEstimate(flops=flops, bytes_accessed=nbytes, transcendentals=0),
        name=name,
    )


def split_project(project):
    width = project.shape[0]
    return (
        project[:, :width].T, project[:, width:2 * width], project[:, 2 * width:].T, project.T
    )


def body(
    peers,
    inputs, context, sample_mask,
    sample_gain, sample_shift, sample_project, sample_output, sample_bias,
    feature_gain, feature_shift, feature_project, feature_output, feature_bias,
    dense_gain, dense_shift, up_weight, up_bias, down_weight, down_bias,
    cotangent,
):
    _, local, samples, width = inputs.shape
    hidden = up_weight.shape[1]
    features = local * peers
    share = samples // peers
    group = 8
    chunk = 512
    chunks = hidden // chunk
    row = lambda vector: vector.reshape(1, -1)

    position = lax.iota(jnp.int32, samples)
    visible = (position < context[0]) & (sample_mask[0] == 1)
    mask = jnp.where(visible, 0.0, MASKED).astype(F32).reshape(samples, 1)
    query_w, key_w, value_w, project_t = split_project(sample_project)
    tokens = inputs[0]

    square = whole((width, width))
    line = whole((1, width))
    token_spec = pl.BlockSpec((1, samples, width), lambda step: (step, 0, 0))
    peer_spec = pl.BlockSpec((peers, 1, share, width), lambda step: (0, step, 0, 0))
    saved_spec = pl.BlockSpec((1, 3, samples, width), lambda step: (step, 0, 0, 0))
    log_spec = pl.BlockSpec((1, HEADS, samples), lambda step: (step, 0, 0))
    anywhere = pl.BlockSpec(memory_space=pl.ANY)
    peer_shape = (peers, local, share, width)
    sems = pltpu.SemaphoreType.DMA
    seen, saved, mixed, logs = call(
        functools.partial(sample_forward_kernel, peers), local,
        [token_spec, whole((samples, 1)), line, line, square, square, square, square, line],
        [anywhere, saved_spec, token_spec, log_spec],
        [
            (peer_shape, BF), ((local, 3, samples, width), BF),
            ((local, width, samples), BF), ((local, HEADS, samples), F32),
        ],
        [
            pltpu.VMEM((2, peers, share, width), BF), sems((2, peers)), sems((peers,)), sems((2,)),
        ],
        "sample_forward", 60_000_000_000, 30_000_000, 0,
    )(
        tokens, mask, row(sample_gain), row(sample_shift), query_w, key_w, value_w,
        sample_output, row(sample_bias),
    )

    query_f, key_f, value_f, project_ft = split_project(feature_project)
    block_tokens = features * group
    block_spec = pl.BlockSpec((features, group, width), lambda step: (0, step, 0))
    up_chunks = up_weight.reshape(width, chunks, chunk).transpose(1, 0, 2)
    down_chunks = down_weight.reshape(chunks, chunk, width)
    (
        result_returned, grad_returned, feature_project_grad, feature_output_grad, up_grad, down_grad,
        feature_vectors, hidden_grad,
    ) = call(
        functools.partial(feature_kernel, peers), share // group,
        [
            block_spec, anywhere, line, line, square, square, square, whole((3 * width, width)),
            square, line, line, line, whole((chunks, width, chunk)), whole((chunks, 1, chunk)),
            whole((chunks, chunk, width)), line,
        ],
        [
            anywhere, anywhere, whole_out((width, 3 * width)), whole_out((width, width)),
            whole_out((chunks, width, chunk)), whole_out((chunks, chunk, width)),
            whole_out((8, width)), whole_out((chunks, 1, chunk)),
        ],
        [
            (peer_shape, BF), (peer_shape, BF),
            ((width, 3 * width), BF), ((width, width), BF),
            ((chunks, width, chunk), BF), ((chunks, chunk, width), BF),
            ((8, width), F32), ((chunks, 1, chunk), F32),
        ],
        [
            pltpu.VMEM((3 * width, width), F32), pltpu.VMEM((width, width), F32),
            pltpu.VMEM((chunks, width, chunk), F32), pltpu.VMEM((chunks, chunk, width), F32),
            pltpu.VMEM((width // 128, block_tokens, 128), F32),
            pltpu.VMEM((width, block_tokens), BF),
            pltpu.VMEM((block_tokens, width), BF), pltpu.VMEM((width, block_tokens), BF),
            pltpu.VMEM((width, block_tokens), BF), pltpu.VMEM((HEADS, block_tokens), F32),
            pltpu.VMEM((3 * width, block_tokens), BF),
            pltpu.VMEM((share // group, features, group, width), BF),
            pltpu.VMEM((2, features, group, width), BF), pltpu.VMEM((2, features, group, width), BF),
            sems((2, peers)), sems((share // group,)), sems((2, peers)), sems((2, peers)),
            sems((peers,)), sems((peers,)), sems((2, 2)),
        ],
        "feature_block", 130_000_000_000, 40_000_000, 1,
    )(
        seen.reshape(features, share, width), cotangent[0],
        row(feature_gain), row(feature_shift), query_f, key_f, value_f, project_ft,
        feature_output, row(feature_bias), row(dense_gain), row(dense_shift),
        up_chunks, up_bias.reshape(chunks, 1, chunk), down_chunks, row(down_bias),
    )
    everyone = ("task", "feat")
    up_grad, down_grad, feature_project_grad, feature_output_grad = lax.psum(
        (up_grad, down_grad, feature_project_grad, feature_output_grad), everyone
    )
    (
        input_grad, output, sample_project_grad, sample_output_grad, sample_vectors,
    ) = call(
        sample_backward_kernel, local,
        [
            token_spec, whole((samples, 1)), line, line, whole((3 * width, width)), square,
            saved_spec, token_spec, log_spec, peer_spec, peer_spec,
        ],
        [
            token_spec, token_spec, whole_out((width, 3 * width)), whole_out((width, width)),
            whole_out((8, width)),
        ],
        [
            ((local, samples, width), F32), ((local, samples, width), BF),
            ((width, 3 * width), BF), ((width, width), BF), ((8, width), F32),
        ],
        [
            pltpu.VMEM((3 * width, width), F32), pltpu.VMEM((width, width), F32),
            pltpu.VMEM((3 * width, samples), BF),
        ],
        "sample_backward", 110_000_000_000, 50_000_000,
    )(
        tokens, mask, row(sample_gain), row(sample_shift), project_t, sample_output,
        saved, mixed, logs, grad_returned, result_returned,
    )
    vectors = jnp.concatenate(
        [sample_vectors, feature_vectors, hidden_grad.reshape(chunks, width)], axis=0
    )
    sample_project_grad, sample_output_grad = lax.psum(
        (sample_project_grad, sample_output_grad), everyone
    )
    vectors = lax.psum(vectors, everyone)
    wide = lambda array: array.astype(F32)
    return (
        output[None], input_grad[None],
        vectors[0], vectors[1], wide(sample_project_grad), wide(sample_output_grad), vectors[2],
        vectors[8], vectors[9], wide(feature_project_grad), wide(feature_output_grad), vectors[10],
        vectors[11], vectors[12],
        wide(up_grad).transpose(1, 0, 2).reshape(width, hidden), vectors[16:].reshape(hidden),
        wide(down_grad).reshape(hidden, width), vectors[13],
    )


def solution(mesh):
    split = P("task", "feat", None, None)
    return jax.shard_map(
        functools.partial(body, mesh.shape["feat"]),
        mesh=mesh,
        in_specs=(split, P("task"), P("task", None)) + (P(),) * 16 + (split,),
        out_specs=(split, split) + (P(),) * 16,
        check_vma=False,
    )
```

```python
import functools
import math

import jax
import jax.numpy as jnp
from jax import lax
from jax.experimental import pallas as pl
from jax.experimental.pallas import tpu as pltpu
from jax.sharding import PartitionSpec as P

HEADS = 8
HEAD = 64
PAIR = 2 * HEAD
EPSILON = 1e-05
SCALE = HEAD ** (-0.5)
POWER = SCALE * math.log2(math.e)
MASKED = -1e30
GELU_A = math.sqrt(2.0 / math.pi)
GELU_B = 0.044715
BF = jnp.bfloat16
F32 = jnp.float32
LIMIT = 60 * 1024 * 1024
MESH = pl.DeviceIdType.MESH


def dot(left, right, left_dim, right_dim):
    return lax.dot_general(
        left, right, (((left_dim,), (right_dim,)), ((), ())), preferred_element_type=F32
    )


def normalize(rows):
    center = rows - jnp.mean(rows, axis=-1, keepdims=True)
    spread = jnp.mean(center * center, axis=-1, keepdims=True)
    inverse = lax.rsqrt(spread + EPSILON)
    return center * inverse, inverse


def normalize_back(grad_normed, gain, hat, inverse):
    scaled = grad_normed * gain
    middle = jnp.mean(scaled, axis=-1, keepdims=True)
    along = jnp.mean(scaled * hat, axis=-1, keepdims=True)
    grad_rows = inverse * (scaled - middle - hat * along)
    grad_gain = jnp.sum(grad_normed * hat, axis=0, keepdims=True)
    grad_shift = jnp.sum(grad_normed, axis=0, keepdims=True)
    return grad_rows, grad_gain, grad_shift


def pieces(row):
    high = row.astype(BF).astype(F32)
    rest = row - high
    middle = rest.astype(BF).astype(F32)
    return high, middle, rest - middle


def extra_rows(count, width, rows):
    place = lax.broadcasted_iota(jnp.int32, (16, width), 0)
    block = jnp.zeros((16, width), F32)
    for index, row in enumerate(rows):
        block = jnp.where(place == index, row, block)
    return jnp.concatenate([block.astype(BF), jnp.zeros((HEAD - 16, width), BF)], axis=0)


def half_ones(odd, depth):
    lane = lax.broadcasted_iota(jnp.int32, (depth, PAIR), 1)
    own = (lane >= HEAD) if odd else (lane < HEAD)
    return own.astype(F32).astype(BF)


def stack_half(odd, own, extra):
    return jnp.concatenate([extra, own] if odd else [own, extra], axis=0)


def extra_columns(odd, depth, columns):
    lane = lax.broadcasted_iota(jnp.int32, (depth, PAIR), 1)
    first = 0 if odd else HEAD
    block = jnp.zeros((depth, PAIR), F32)
    for index, column in enumerate(columns):
        block = jnp.where(lane == first + index, column, block)
    return block.astype(BF)


def attend_head(keys, left_extra, own, query_rows, extra, odd, value_rows):
    left = keys * own + left_extra
    scores = dot(left, stack_half(odd, query_rows, extra), 1, 0)
    highest = jnp.max(scores, axis=0, keepdims=True)
    weights = jnp.exp2((scores - highest) * POWER)
    totals = jnp.sum(weights, axis=0, keepdims=True)
    mixed = dot(value_rows, weights.astype(BF), 1, 0) / totals
    log_total = highest + jnp.log2(totals) * (1.0 / POWER)
    return mixed, log_total


def attend_head_back(left, right, value_left, value_right, query_rows, key_rows, grad_rows):
    shares = jnp.exp2(dot(left, right, 1, 0) * POWER)
    grad_shares = dot(value_left, value_right, 1, 0)
    low_scores = (shares * grad_shares).astype(BF)
    grad_values = dot(grad_rows, shares.astype(BF), 1, 1)
    grad_keys = dot(query_rows, low_scores, 1, 1) * SCALE
    grad_queries = dot(key_rows, low_scores, 1, 0) * SCALE
    return grad_queries, grad_keys, grad_values


def push(source, target, send_sem, recv_sem, peer):
    return pltpu.make_async_remote_copy(
        src_ref=source, dst_ref=target, send_sem=send_sem, recv_sem=recv_sem,
        device_id={"feat": peer}, device_id_type=MESH,
    )


def greet(peers, me):
    barrier = pltpu.get_barrier_semaphore()
    for hop in range(1, peers):
        pl.semaphore_signal(
            barrier, inc=1, device_id={"feat": (me + hop) % peers}, device_id_type=MESH
        )
    pl.semaphore_wait(barrier, peers - 1)


def arrived(buffer, sem):
    pltpu.make_async_copy(buffer, buffer, sem).wait()


def sample_forward_kernel(
    peers,
    inputs_ref, mask_ref, gain_ref, shift_ref, project, output_w, bias_ref,
    seen_ref, saved_ref, mixed_ref, log_ref,
    turned, outbox, send_sems, recv_sems, own_sems,
):
    step = pl.program_id(0)
    steps = pl.num_programs(0)
    slot = step % 2
    me = lax.axis_index("feat")

    @pl.when(step == 0)
    def _():
        greet(peers, me)
        turned[...] = project[...].T

    def moves(at, slot):
        sends = []
        for hop in range(1, peers):
            peer = (me + hop) % peers
            sends.append(
                push(
                    outbox.at[slot, peer], seen_ref.at[me, at],
                    send_sems.at[slot, hop], recv_sems.at[hop], peer,
                )
            )
        own = pltpu.make_async_copy(outbox.at[slot, me], seen_ref.at[me, at], own_sems.at[slot])
        return sends, own

    def drain(at, slot):
        sends, own = moves(at, slot)
        for send in sends:
            send.wait_send()
        own.wait()

    rows = inputs_ref[0].astype(F32)
    samples, width = rows.shape
    hat, _ = normalize(rows)
    normed = (hat * gain_ref[...] + shift_ref[...]).astype(BF)
    saved_ref[0, 0] = dot(turned[:width], normed, 1, 1).astype(BF)
    saved_ref[0, 1] = dot(normed, project[:, width:2 * width], 1, 0).astype(BF)
    saved_ref[0, 2] = dot(turned[2 * width:], normed, 1, 1).astype(BF)
    mask = mask_ref[...]
    extra = extra_rows(1, samples, [jnp.ones((1, samples), F32)])
    for odd in (False, True):
        own = half_ones(odd, samples)
        left_extra = extra_columns(odd, samples, [mask])
        for pair in range(width // PAIR):
            head = 2 * pair + odd
            first = head * HEAD
            mixed, log_total = attend_head(
                saved_ref[0, 1, :, pair * PAIR:(pair + 1) * PAIR], left_extra, own,
                saved_ref[0, 0, first:first + HEAD, :], extra, odd,
                saved_ref[0, 2, first:first + HEAD, :],
            )
            mixed_ref[0, first:first + HEAD, :] = mixed.astype(BF)
            log_ref[0, head:head + 1, :] = log_total
    branch = dot(mixed_ref[0], output_w[...], 0, 0) + bias_ref[...]
    after = (inputs_ref[0].astype(F32) + branch).astype(BF)

    @pl.when(step >= 2)
    def _():
        drain(step - 2, slot)

    outbox[slot] = after.reshape(outbox.shape[1:])
    sends, own = moves(step, slot)
    for send in sends:
        send.start()
    own.start()

    @pl.when(step == steps - 1)
    def _():
        drain(step, slot)
        if seen_ref.shape[1] > 1:
            drain(step - 1, 1 - slot)
        for hop in range(1, peers):
            arrived(seen_ref.at[(me + peers - hop) % peers], recv_sems.at[hop])


def sample_backward_kernel(
    inputs_ref, mask_ref, gain_ref, shift_ref, project, output_w,
    saved_ref, mixed_ref, log_ref, grad_ref, result_ref,
    input_grad_ref, final_ref, project_grad, output_grad,
    project_sum, output_sum, vector_grad, turned, packed_grad,
):
    step = pl.program_id(0)

    @pl.when(step == 0)
    def _():
        turned[...] = project[...].T
        project_sum[...] = jnp.zeros_like(project_sum)
        output_sum[...] = jnp.zeros_like(output_sum)
        vector_grad[...] = jnp.zeros_like(vector_grad)

    samples, width = inputs_ref.shape[1:]
    final_ref[0] = result_ref[...].reshape(samples, width)
    low_grad = grad_ref[...].reshape(samples, width)
    output_sum[...] += dot(mixed_ref[0], low_grad, 1, 0)
    grad_mixed = dot(output_w[...], low_grad, 1, 1)
    low_mixed = grad_mixed.astype(BF)
    delta = (low_mixed.astype(F32) * mixed_ref[0].astype(F32))
    delta = jnp.sum(delta.reshape(width // HEAD, HEAD, samples), axis=1)
    mask = mask_ref[...]
    ones = jnp.ones((samples, 1), F32)
    one_row = jnp.ones((1, samples), F32)
    for odd in (False, True):
        own = half_ones(odd, samples)
        key_extra = extra_columns(odd, samples, [mask, ones, ones, ones])
        value_extra = extra_columns(odd, samples, [ones, ones, ones])
        for pair in range(width // PAIR):
            head = 2 * pair + odd
            first = head * HEAD
            lanes = slice(pair * PAIR, (pair + 1) * PAIR)
            query_rows = saved_ref[0, 0, first:first + HEAD, :]
            value_rows = saved_ref[0, 2, first:first + HEAD, :]
            grad_rows = low_mixed[first:first + HEAD, :]
            keys = saved_ref[0, 1, :, lanes]
            key_rows = keys.T[HEAD:] if odd else keys.T[:HEAD]
            high, middle, low = pieces(-log_ref[0, head:head + 1, :])
            right = stack_half(odd, query_rows, extra_rows(4, samples, [one_row, high, middle, low]))
            high, middle, low = pieces(-delta[head:head + 1, :])
            value_right = jnp.concatenate(
                [grad_rows, extra_rows(3, samples, [high, middle, low])], axis=0
            )
            value_left = jnp.concatenate(
                [value_rows, extra_rows(3, samples, [one_row] * 3)], axis=0
            )
            shares = jnp.exp2(dot(keys * own + key_extra, right, 1, 0) * POWER)
            grad_shares = dot(value_left, value_right, 0, 0)
            low_scores = (shares * grad_shares).astype(BF)
            packed_grad[2 * width + first:2 * width + first + HEAD, :] = dot(
                grad_rows, shares.astype(BF), 1, 1
            ).astype(BF)
            packed_grad[width + first:width + first + HEAD, :] = (
                dot(query_rows, low_scores, 1, 1) * SCALE
            ).astype(BF)
            packed_grad[first:first + HEAD, :] = (
                dot(key_rows, low_scores, 1, 0) * SCALE
            ).astype(BF)
    hat, inverse = normalize(inputs_ref[0].astype(F32))
    normed = (hat * gain_ref[...] + shift_ref[...]).astype(BF)
    project_sum[...] += dot(packed_grad[...], normed, 1, 0)
    grad_normed = dot(packed_grad[...], turned[...], 0, 0)
    grad_rows, grad_gain, grad_shift = normalize_back(grad_normed, gain_ref[...], hat, inverse)
    stream = low_grad.astype(F32)
    input_grad_ref[0] = stream + grad_rows
    vector_grad[0:1, :] += grad_gain
    vector_grad[1:2, :] += grad_shift
    vector_grad[2:3, :] += jnp.sum(stream, axis=0, keepdims=True)

    @pl.when(step == pl.num_programs(0) - 1)
    def _():
        project_grad[...] = project_sum[...].T.astype(BF)
        output_grad[:width] = output_sum[...].astype(BF)
        output_grad[width:] = vector_grad[...].astype(BF)


def to_groups(block_ref, spare):
    features, group, width = block_ref.shape
    rows = block_ref[...].astype(F32).reshape(features * group, width)
    columns = []
    for lanes in range(width // 128):
        spare[lanes] = rows[:, lanes * 128:(lanes + 1) * 128]
        columns.append(
            jnp.concatenate(
                [spare[lanes, pl.ds(one, features, stride=group), :] for one in range(group)],
                axis=0,
            )
        )
    return jnp.concatenate(columns, axis=1)


def from_groups(rows, block_ref, spare):
    features, group, width = block_ref.shape
    for lanes in range(width // 128):
        span = slice(lanes * 128, (lanes + 1) * 128)
        for one in range(group):
            spare[lanes, pl.ds(one, features, stride=group), :] = rows[
                one * features:(one + 1) * features, span
            ]
        block_ref[:, :, span] = spare[lanes].reshape(features, group, 128).astype(BF)


def feature_kernel(
    peers,
    stream_ref, cotangent_hbm, gain_ref, shift_ref, project, output_w,
    bias_ref, dense_gain_ref, dense_shift_ref, up_ref, up_bias_ref, down_ref, down_bias_ref,
    results_ref, grads_ref, project_grad, output_grad, up_grad, down_grad,
    vector_grad, hidden_grad, project_sum, output_sum, up_sum, down_sum, turned, spare, query_t, keys_s, value_t, mixed_t, logs,
    packed_grad, cotangents, result_box, grad_box,
    cotangent_sends, cotangent_recvs, result_sends, grad_sends, result_recvs, grad_recvs, own_sems,
):
    step = pl.program_id(0)
    steps, features, group, _ = cotangents.shape
    slot = step % 2
    me = lax.axis_index("feat")
    local = features // peers
    share = steps * group
    chunks, chunk, width = down_ref.shape
    tokens = features * group
    joined = 2 * features

    def cotangent_moves(at, own=False):
        def part(peer):
            return cotangent_hbm.at[:, pl.ds(pl.multiple_of(peer * share + at * group, group), group), :]

        inbox = cotangents.at[at, pl.ds(me * local, local)]
        if own:
            return pltpu.make_async_copy(part(me), inbox, cotangent_recvs.at[at])
        sends = []
        for hop in range(1, peers):
            peer = (me + hop) % peers
            sends.append(
                push(part(peer), inbox, cotangent_sends.at[at % 2, hop], cotangent_recvs.at[at], peer)
            )
        return sends

    def start_cotangent(at):
        for send in cotangent_moves(at):
            send.start()
        cotangent_moves(at, own=True).start()

    def back_moves(at, slot, box, target, send_sems, recv_sems, own_sem):
        place = target.at[me, :, pl.ds(pl.multiple_of(at * group, group), group), :]
        sends = []
        for hop in range(1, peers):
            peer = (me + hop) % peers
            sends.append(
                push(
                    box.at[slot, pl.ds(peer * local, local)], place,
                    send_sems.at[slot, hop], recv_sems.at[hop], peer,
                )
            )
        own = pltpu.make_async_copy(box.at[slot, pl.ds(me * local, local)], place, own_sem)
        return sends, own

    def result_moves(at, slot):
        return back_moves(
            at, slot, result_box, results_ref, result_sends, result_recvs, own_sems.at[0, slot]
        )

    def grad_moves(at, slot):
        return back_moves(
            at, slot, grad_box, grads_ref, grad_sends, grad_recvs, own_sems.at[1, slot]
        )

    def begin(moves):
        sends, own = moves
        for send in sends:
            send.start()
        own.start()

    def drain(moves):
        sends, own = moves
        for send in sends:
            send.wait_send()
        own.wait()

    @pl.when(step == 0)
    def _():
        greet(peers, me)
        start_cotangent(0)
        turned[...] = project[...].T

    @pl.when(step + 1 < steps)
    def _():
        @pl.when(step >= 1)
        def _():
            for send in cotangent_moves(step - 1):
                send.wait_send()

        start_cotangent(step + 1)

    @pl.when(step == 0)
    def _():
        project_sum[...] = jnp.zeros_like(project_sum)
        output_sum[...] = jnp.zeros_like(output_sum)
        up_sum[...] = jnp.zeros_like(up_sum)
        down_sum[...] = jnp.zeros_like(down_sum)
        vector_grad[...] = jnp.zeros_like(vector_grad)
        hidden_grad[...] = jnp.zeros_like(hidden_grad)

    rows = to_groups(stream_ref, spare)
    hat, inverse = normalize(rows)
    normed = (hat * gain_ref[...] + shift_ref[...]).astype(BF)
    query_t[...] = dot(turned[:width], normed, 1, 1).astype(BF)
    keys_s[...] = dot(normed, project[:, width:2 * width], 1, 0).astype(BF)
    value_t[...] = dot(turned[2 * width:], normed, 1, 1).astype(BF)
    place = lax.broadcasted_iota(jnp.int32, (joined, 1), 0)
    place_row = lax.broadcasted_iota(jnp.int32, (1, joined), 1)
    key_first = (place < features).astype(F32)
    key_second = (place >= features).astype(F32)
    hide_first = jnp.where(place_row >= features, MASKED, 0.0)
    hide_second = jnp.where(place_row < features, MASKED, 0.0)
    ones = jnp.ones((joined, 1), F32)
    one_row = jnp.ones((1, joined), F32)
    extra = extra_rows(2, joined, [hide_first, hide_second])
    for odd in (False, True):
        own = half_ones(odd, joined)
        left_extra = extra_columns(odd, joined, [key_first, key_second])
        for pair in range(width // PAIR):
            head = 2 * pair + odd
            first = head * HEAD
            for part in range(tokens // joined):
                span = slice(part * joined, (part + 1) * joined)
                mixed, log_total = attend_head(
                    keys_s[span, pair * PAIR:(pair + 1) * PAIR], left_extra, own,
                    query_t[first:first + HEAD, span], extra, odd,
                    value_t[first:first + HEAD, span],
                )
                mixed_t[first:first + HEAD, span] = mixed.astype(BF)
                logs[head:head + 1, span] = log_total
    after = rows + dot(mixed_t[...], output_w[...], 0, 0) + bias_ref[...]

    dense_hat, dense_inverse = normalize(after)
    dense_in = (dense_hat * dense_gain_ref[...] + dense_shift_ref[...]).astype(BF)
    arrived(cotangents.at[step], cotangent_recvs.at[step])
    stream = to_groups(cotangents.at[step], spare)
    low_stream = stream.astype(BF)
    result = after + down_bias_ref[...]
    grad_dense = jnp.zeros((tokens, width), F32)
    for index in range(chunks):
        up = up_ref[:, index * chunk:(index + 1) * chunk]
        pre = dot(dense_in, up, 1, 0) + up_bias_ref[index]
        square = pre * pre
        bend = jnp.tanh(pre * (GELU_A + (GELU_A * GELU_B) * square))
        half = 0.5 + 0.5 * bend
        activated = (pre * half).astype(BF)
        slope = half + (pre * half) * (1.0 - bend) * (GELU_A + (3.0 * GELU_A * GELU_B) * square)
        result = result + dot(activated, down_ref[index], 1, 0)
        grad_pre = (slope * dot(low_stream, down_ref[index], 1, 1)).astype(BF)
        grad_dense = grad_dense + dot(grad_pre, up, 1, 1)
        down_sum[index] += dot(activated, low_stream, 0, 0)
        up_sum[index] += dot(dense_in, grad_pre, 0, 0)
        hidden_grad[index] += jnp.sum(grad_pre.astype(F32), axis=0, keepdims=True)

    @pl.when(step >= 2)
    def _():
        drain(result_moves(step - 2, slot))
        drain(grad_moves(step - 2, slot))

    from_groups(result, result_box.at[slot], spare)
    begin(result_moves(step, slot))
    dense_rows, dense_gain_grad, dense_shift_grad = normalize_back(
        grad_dense, dense_gain_ref[...], dense_hat, dense_inverse
    )
    grad_after = stream + dense_rows

    low_grad = grad_after.astype(BF)
    output_sum[...] += dot(mixed_t[...], low_grad, 1, 0)
    low_mixed = dot(output_w[...], low_grad, 1, 1).astype(BF)
    delta = low_mixed.astype(F32) * mixed_t[...].astype(F32)
    delta = jnp.sum(delta.reshape(width // HEAD, HEAD, tokens), axis=1)
    for odd in (False, True):
        own = half_ones(odd, joined)
        key_extra = extra_columns(odd, joined, [key_first, key_second, ones, ones, ones])
        for pair in range(width // PAIR):
            head = 2 * pair + odd
            first = head * HEAD
            for part in range(tokens // joined):
                span = slice(part * joined, (part + 1) * joined)
                query_rows = query_t[first:first + HEAD, span]
                value_rows = value_t[first:first + HEAD, span]
                grad_rows = low_mixed[first:first + HEAD, span]
                keys = keys_s[span, pair * PAIR:(pair + 1) * PAIR]
                key_rows = keys.T[HEAD:] if odd else keys.T[:HEAD]
                high, middle, low = pieces(-logs[head:head + 1, span])
                right = stack_half(
                    odd, query_rows,
                    extra_rows(5, joined, [hide_first, hide_second, high, middle, low]),
                )
                high, middle, low = pieces(-delta[head:head + 1, span])
                value_right = jnp.concatenate(
                    [grad_rows, extra_rows(3, joined, [high, middle, low])], axis=0
                )
                value_left = jnp.concatenate(
                    [value_rows, extra_rows(3, joined, [one_row] * 3)], axis=0
                )
                shares = jnp.exp2(dot(keys * own + key_extra, right, 1, 0) * POWER)
                grad_shares = dot(value_left, value_right, 0, 0)
                low_scores = (shares * grad_shares).astype(BF)
                packed_grad[2 * width + first:2 * width + first + HEAD, span] = dot(
                    grad_rows, shares.astype(BF), 1, 1
                ).astype(BF)
                packed_grad[width + first:width + first + HEAD, span] = (
                    dot(query_rows, low_scores, 1, 1) * SCALE
                ).astype(BF)
                packed_grad[first:first + HEAD, span] = (
                    dot(key_rows, low_scores, 1, 0) * SCALE
                ).astype(BF)
    project_sum[...] += dot(packed_grad[...], normed, 1, 0)
    grad_normed = dot(packed_grad[...], turned[...], 0, 0)
    grad_rows, gain_grad, shift_grad = normalize_back(grad_normed, gain_ref[...], hat, inverse)
    from_groups(grad_after + grad_rows, grad_box.at[slot], spare)
    begin(grad_moves(step, slot))
    vector_grad[0:1, :] += gain_grad
    vector_grad[1:2, :] += shift_grad
    vector_grad[2:3, :] += jnp.sum(low_grad.astype(F32), axis=0, keepdims=True)
    vector_grad[3:4, :] += dense_gain_grad
    vector_grad[4:5, :] += dense_shift_grad
    vector_grad[5:6, :] += jnp.sum(stream, axis=0, keepdims=True)

    @pl.when(step == pl.num_programs(0) - 1)
    def _():
        project_grad[...] = project_sum[...].T.astype(BF)
        output_grad[:width] = output_sum[...].astype(BF)
        output_grad[width:] = jnp.concatenate(
            [vector_grad[...]]
            + [hidden_grad[index].reshape(chunk // width, width) for index in range(chunks)]
            + [jnp.zeros((8 - hidden_grad.size // width, width), F32)], axis=0,
        ).astype(BF)
        for index in range(chunks):
            up_grad[:, index * chunk:(index + 1) * chunk] = up_sum[index].astype(BF)
        down_grad[...] = down_sum[...].astype(BF)
        for send in cotangent_moves(step):
            send.wait_send()
        drain(result_moves(step, slot))
        drain(grad_moves(step, slot))
        if steps > 1:
            for send in cotangent_moves(step - 1):
                send.wait_send()
            drain(result_moves(step - 1, 1 - slot))
            drain(grad_moves(step - 1, 1 - slot))
        for hop in range(1, peers):
            source = (me + peers - hop) % peers
            arrived(results_ref.at[source], result_recvs.at[hop])
            arrived(grads_ref.at[source], grad_recvs.at[hop])


def whole(shape):
    return pl.BlockSpec(shape, lambda step: (0,) * len(shape), pipeline_mode=pl.Buffered(1))


def whole_out(shape):
    return pl.BlockSpec(shape, lambda step: (0,) * len(shape))


def call(kernel, grid, in_specs, out_specs, out_shape, scratch, name, flops, nbytes, remote=None):
    return pl.pallas_call(
        kernel,
        grid=(grid,),
        in_specs=in_specs,
        out_specs=out_specs,
        out_shape=[jax.ShapeDtypeStruct(*one) for one in out_shape],
        scratch_shapes=scratch,
        compiler_params=pltpu.CompilerParams(
            dimension_semantics=("arbitrary",), vmem_limit_bytes=LIMIT,
            collective_id=remote, has_side_effects=remote is not None,
        ),
        cost_estimate=pl.CostEstimate(flops=flops, bytes_accessed=nbytes, transcendentals=0),
        name=name,
    )


def body(
    peers,
    inputs, context, sample_mask,
    sample_gain, sample_shift, sample_project, sample_output, sample_bias,
    feature_gain, feature_shift, feature_project, feature_output, feature_bias,
    dense_gain, dense_shift, up_weight, up_bias, down_weight, down_bias,
    cotangent,
):
    _, local, samples, width = inputs.shape
    hidden = up_weight.shape[1]
    features = local * peers
    share = samples // peers
    group = 8
    chunk = 512
    chunks = hidden // chunk
    row = lambda vector: vector.reshape(1, -1)

    position = lax.iota(jnp.int32, samples)
    visible = (position < context[0]) & (sample_mask[0] == 1)
    mask = jnp.where(visible, 0.0, MASKED).astype(F32).reshape(samples, 1)
    tokens = inputs[0]

    square = whole((width, width))
    line = whole((1, width))
    token_spec = pl.BlockSpec((1, samples, width), lambda step: (step, 0, 0))
    peer_spec = pl.BlockSpec((peers, 1, share, width), lambda step: (0, step, 0, 0))
    saved_spec = pl.BlockSpec((1, 3, samples, width), lambda step: (step, 0, 0, 0))
    log_spec = pl.BlockSpec((1, HEADS, samples), lambda step: (step, 0, 0))
    anywhere = pl.BlockSpec(memory_space=pl.ANY)
    peer_shape = (peers, local, share, width)
    sems = pltpu.SemaphoreType.DMA
    seen, saved, mixed, logs = call(
        functools.partial(sample_forward_kernel, peers), local,
        [token_spec, whole((samples, 1)), line, line, whole((width, 3 * width)), square, line],
        [anywhere, saved_spec, token_spec, log_spec],
        [
            (peer_shape, BF), ((local, 3, samples, width), BF),
            ((local, width, samples), BF), ((local, HEADS, samples), F32),
        ],
        [
            pltpu.VMEM((3 * width, width), BF), pltpu.VMEM((2, peers, share, width), BF),
            sems((2, peers)), sems((peers,)), sems((2,)),
        ],
        "sample_forward", 60_000_000_000, 30_000_000, 0,
    )(
        tokens, mask, row(sample_gain), row(sample_shift), sample_project, sample_output, row(sample_bias),
    )

    block_tokens = features * group
    block_spec = pl.BlockSpec((features, group, width), lambda step: (0, step, 0))
    down_chunks = down_weight.reshape(chunks, chunk, width)
    (
        result_returned, grad_returned, feature_project_grad, feature_output_grad, up_grad, down_grad,
    ) = call(
        functools.partial(feature_kernel, peers), share // group,
        [
            block_spec, anywhere, line, line, whole((width, 3 * width)),
            square, line, line, line, whole((width, hidden)), whole((chunks, 1, chunk)),
            whole((chunks, chunk, width)), line,
        ],
        [
            anywhere, anywhere, whole_out((width, 3 * width)), whole_out((width + 16, width)),
            whole_out((width, hidden)), whole_out((chunks, chunk, width)),
        ],
        [
            (peer_shape, BF), (peer_shape, BF),
            ((width, 3 * width), BF), ((width + 16, width), BF),
            ((width, hidden), BF), ((chunks, chunk, width), BF),
        ],
        [
            pltpu.VMEM((8, width), F32), pltpu.VMEM((chunks, 1, chunk), F32),
            pltpu.VMEM((3 * width, width), F32), pltpu.VMEM((width, width), F32),
            pltpu.VMEM((chunks, width, chunk), F32), pltpu.VMEM((chunks, chunk, width), F32),
            pltpu.VMEM((3 * width, width), BF), pltpu.VMEM((width // 128, block_tokens, 128), F32),
            pltpu.VMEM((width, block_tokens), BF),
            pltpu.VMEM((block_tokens, width), BF), pltpu.VMEM((width, block_tokens), BF),
            pltpu.VMEM((width, block_tokens), BF), pltpu.VMEM((HEADS, block_tokens), F32),
            pltpu.VMEM((3 * width, block_tokens), BF),
            pltpu.VMEM((share // group, features, group, width), BF),
            pltpu.VMEM((2, features, group, width), BF), pltpu.VMEM((2, features, group, width), BF),
            sems((2, peers)), sems((share // group,)), sems((2, peers)), sems((2, peers)),
            sems((peers,)), sems((peers,)), sems((2, 2)),
        ],
        "feature_block", 130_000_000_000, 40_000_000, 1,
    )(
        seen.reshape(features, share, width), cotangent[0],
        row(feature_gain), row(feature_shift), feature_project,
        feature_output, row(feature_bias), row(dense_gain), row(dense_shift),
        up_weight, up_bias.reshape(chunks, 1, chunk), down_chunks, row(down_bias),
    )
    everyone = ("task", "feat")
    feature_grads = lax.psum(
        (up_grad, down_grad, feature_project_grad, feature_output_grad), everyone
    )
    (
        input_grad, output, sample_project_grad, sample_output_grad,
    ) = call(
        sample_backward_kernel, local,
        [
            token_spec, whole((samples, 1)), line, line, whole((width, 3 * width)), square,
            saved_spec, token_spec, log_spec, peer_spec, peer_spec,
        ],
        [
            token_spec, token_spec, whole_out((width, 3 * width)), whole_out((width + 16, width)),
        ],
        [
            ((local, samples, width), F32), ((local, samples, width), BF),
            ((width, 3 * width), BF), ((width + 16, width), BF),
        ],
        [
            pltpu.VMEM((3 * width, width), F32), pltpu.VMEM((width, width), F32),
            pltpu.VMEM((16, width), F32),
            pltpu.VMEM((3 * width, width), BF), pltpu.VMEM((3 * width, samples), BF),
        ],
        "sample_backward", 110_000_000_000, 50_000_000,
    )(
        tokens, mask, row(sample_gain), row(sample_shift), sample_project, sample_output,
        saved, mixed, logs, grad_returned, result_returned,
    )
    sample_grads, feature_grads = lax.optimization_barrier(
        ((sample_project_grad, sample_output_grad), feature_grads)
    )
    sample_project_grad, sample_output_grad = lax.psum(sample_grads, everyone)
    up_grad, down_grad, feature_project_grad, feature_output_grad = feature_grads
    wide = lambda array: array.astype(F32)
    sample_vectors = wide(sample_output_grad[width:])
    feature_vectors = wide(feature_output_grad[width:])
    return (
        output[None], input_grad[None],
        sample_vectors[0], sample_vectors[1], wide(sample_project_grad), wide(sample_output_grad[:width]),
        sample_vectors[2], feature_vectors[0], feature_vectors[1], wide(feature_project_grad),
        wide(feature_output_grad[:width]), feature_vectors[2], feature_vectors[3], feature_vectors[4],
        wide(up_grad), feature_vectors[8:8 + hidden // width].reshape(hidden), wide(down_grad).reshape(hidden, width),
        feature_vectors[5],
    )


def solution(mesh):
    split = P("task", "feat", None, None)
    return jax.shard_map(
        functools.partial(body, mesh.shape["feat"]),
        mesh=mesh,
        in_specs=(split, P("task"), P("task", None)) + (P(),) * 16 + (split,),
        out_specs=(split, split) + (P(),) * 16,
        check_vma=False,
    )
```

```python
import functools
import math

import jax
import jax.numpy as jnp
from jax import lax
from jax.experimental import pallas as pl
from jax.experimental.pallas import tpu as pltpu
from jax.sharding import PartitionSpec as P

HEADS = 8
HEAD = 64
PAIR = 2 * HEAD
EPSILON = 1e-05
SCALE = HEAD ** (-0.5)
POWER = SCALE * math.log2(math.e)
MASKED = -1e30
GELU_A = math.sqrt(2.0 / math.pi)
GELU_B = 0.044715
BF = jnp.bfloat16
F32 = jnp.float32
LIMIT = 60 * 1024 * 1024
MESH = pl.DeviceIdType.MESH
TILE = 16
LANES = 128
TICKS = 4


def dot(left, right, left_dim, right_dim):
    return lax.dot_general(
        left, right, (((left_dim,), (right_dim,)), ((), ())), preferred_element_type=F32
    )


def normalize(rows):
    center = rows - jnp.mean(rows, axis=-1, keepdims=True)
    spread = jnp.mean(center * center, axis=-1, keepdims=True)
    inverse = lax.rsqrt(spread + EPSILON)
    return center * inverse, inverse


def normalize_back(grad_normed, gain, hat, inverse):
    scaled = grad_normed * gain
    middle = jnp.mean(scaled, axis=-1, keepdims=True)
    along = jnp.mean(scaled * hat, axis=-1, keepdims=True)
    grad_rows = inverse * (scaled - middle - hat * along)
    grad_gain = jnp.sum(grad_normed * hat, axis=0, keepdims=True)
    grad_shift = jnp.sum(grad_normed, axis=0, keepdims=True)
    return grad_rows, grad_gain, grad_shift


def pieces(row):
    high = row.astype(BF).astype(F32)
    rest = row - high
    middle = rest.astype(BF).astype(F32)
    return high, middle, rest - middle


def extra_rows(count, width, rows):
    place = lax.broadcasted_iota(jnp.int32, (16, width), 0)
    block = jnp.zeros((16, width), F32)
    for index, row in enumerate(rows):
        block = jnp.where(place == index, row, block)
    return jnp.concatenate([block.astype(BF), jnp.zeros((HEAD - 16, width), BF)], axis=0)


def half_ones(odd, depth):
    lane = lax.broadcasted_iota(jnp.int32, (depth, PAIR), 1)
    own = (lane >= HEAD) if odd else (lane < HEAD)
    return own.astype(F32).astype(BF)


def stack_half(odd, own, extra):
    return jnp.concatenate([extra, own] if odd else [own, extra], axis=0)


def extra_columns(odd, depth, columns):
    lane = lax.broadcasted_iota(jnp.int32, (depth, PAIR), 1)
    first = 0 if odd else HEAD
    block = jnp.zeros((depth, PAIR), F32)
    for index, column in enumerate(columns):
        block = jnp.where(lane == first + index, column, block)
    return block.astype(BF)


def attend_head(keys, left_extra, own, query_rows, extra, odd, value_rows):
    left = keys * own + left_extra
    scores = dot(left, stack_half(odd, query_rows, extra), 1, 0)
    highest = jnp.max(scores, axis=0, keepdims=True)
    weights = jnp.exp2((scores - highest) * POWER)
    totals = jnp.sum(weights, axis=0, keepdims=True)
    mixed = dot(value_rows, weights.astype(BF), 1, 0) / totals
    log_total = highest + jnp.log2(totals) * (1.0 / POWER)
    return mixed, log_total


def attend_head_back(left, right, value_left, value_right, query_rows, key_rows, grad_rows):
    shares = jnp.exp2(dot(left, right, 1, 0) * POWER)
    grad_shares = dot(value_left, value_right, 1, 0)
    low_scores = (shares * grad_shares).astype(BF)
    grad_values = dot(grad_rows, shares.astype(BF), 1, 1)
    grad_keys = dot(query_rows, low_scores, 1, 1) * SCALE
    grad_queries = dot(key_rows, low_scores, 1, 0) * SCALE
    return grad_queries, grad_keys, grad_values


def push(source, target, send_sem, recv_sem, peer):
    return pltpu.make_async_remote_copy(
        src_ref=source, dst_ref=target, send_sem=send_sem, recv_sem=recv_sem,
        device_id={"feat": peer}, device_id_type=MESH,
    )


def greet(peers, me):
    barrier = pltpu.get_barrier_semaphore()
    for hop in range(1, peers):
        pl.semaphore_signal(
            barrier, inc=1, device_id={"feat": (me + hop) % peers}, device_id_type=MESH
        )
    pl.semaphore_wait(barrier, peers - 1)


def arrived(buffer, sem):
    pltpu.make_async_copy(buffer, buffer, sem).wait()


def sample_forward_kernel(
    peers,
    inputs_ref, mask_ref, gain_ref, shift_ref, project, output_w, bias_ref,
    seen_ref, saved_ref, mixed_ref, log_ref,
    turned, outbox, send_sems, recv_sems, own_sems,
):
    step = pl.program_id(0)
    steps = pl.num_programs(0)
    slot = step % 2
    me = lax.axis_index("feat")

    @pl.when(step == 0)
    def _():
        greet(peers, me)
        turned[...] = project[...].T

    def moves(at, slot):
        sends = []
        for hop in range(1, peers):
            peer = (me + hop) % peers
            sends.append(
                push(
                    outbox.at[slot, peer], seen_ref.at[me, at],
                    send_sems.at[slot, hop], recv_sems.at[hop], peer,
                )
            )
        own = pltpu.make_async_copy(outbox.at[slot, me], seen_ref.at[me, at], own_sems.at[slot])
        return sends, own

    def drain(at, slot):
        sends, own = moves(at, slot)
        for send in sends:
            send.wait_send()
        own.wait()

    rows = inputs_ref[0].astype(F32)
    samples, width = rows.shape
    hat, _ = normalize(rows)
    normed = (hat * gain_ref[...] + shift_ref[...]).astype(BF)
    saved_ref[0, 0] = dot(turned[:width], normed, 1, 1).astype(BF)
    saved_ref[0, 1] = dot(normed, project[:, width:2 * width], 1, 0).astype(BF)
    saved_ref[0, 2] = dot(turned[2 * width:], normed, 1, 1).astype(BF)
    mask = mask_ref[...]
    extra = extra_rows(1, samples, [jnp.ones((1, samples), F32)])
    for odd in (False, True):
        own = half_ones(odd, samples)
        left_extra = extra_columns(odd, samples, [mask])
        for pair in range(width // PAIR):
            head = 2 * pair + odd
            first = head * HEAD
            mixed, log_total = attend_head(
                saved_ref[0, 1, :, pair * PAIR:(pair + 1) * PAIR], left_extra, own,
                saved_ref[0, 0, first:first + HEAD, :], extra, odd,
                saved_ref[0, 2, first:first + HEAD, :],
            )
            mixed_ref[0, first:first + HEAD, :] = mixed.astype(BF)
            log_ref[0, head:head + 1, :] = log_total
    branch = dot(mixed_ref[0], output_w[...], 0, 0) + bias_ref[...]
    after = (inputs_ref[0].astype(F32) + branch).astype(BF)

    @pl.when(step >= 2)
    def _():
        drain(step - 2, slot)

    outbox[slot] = after.reshape(outbox.shape[1:])
    sends, own = moves(step, slot)
    for send in sends:
        send.start()
    own.start()

    @pl.when(step == steps - 1)
    def _():
        drain(step, slot)
        if seen_ref.shape[1] > 1:
            drain(step - 1, 1 - slot)
        for hop in range(1, peers):
            arrived(seen_ref.at[(me + peers - hop) % peers], recv_sems.at[hop])


def axis_orders(peers, tasks):
    feat_bits = peers.bit_length() - 1
    split = 1 + (feat_bits - 1) // 2
    core = [("feat", 0)]
    across = [("feat", bit) for bit in range(1, split)]
    along = [("feat", bit) for bit in range(split, feat_bits)]
    task = [("task", bit) for bit in range(tasks.bit_length() - 1)]
    return core + across + along + task, core + along + across + task


def sample_backward_kernel(
    peers, tasks, feature_jobs, sample_jobs,
    inputs_ref, mask_ref, gain_ref, shift_ref, project, output_w,
    saved_ref, mixed_ref, log_ref, grad_ref, feature_vectors, feature_stacked,
    input_grad_ref, summed_ref, vectors_ref,
    project_sum, output_sum, vector_grad, turned, packed_grad,
    parts, inbox, full, vector_parts, vector_inbox,
    load_sems, store_sems, sends, recvs, vector_sends, vector_recvs,
):
    step = pl.program_id(0)
    steps = pl.num_programs(0)
    orders = axis_orders(peers, tasks)
    bits = len(orders[0])
    size = parts.shape[2]
    place = {"feat": lax.axis_index("feat"), "task": lax.axis_index("task")}

    def side(axis, bit):
        return (place[axis] // 2 ** bit) % 2

    def partner(axis, bit):
        return {axis: place[axis] + (1 - 2 * side(axis, bit)) * 2 ** bit}

    bases = []
    for order in orders:
        base = [0]
        for index, where in enumerate(order):
            base.append(base[-1] + side(*where) * (size >> (index + 1)))
        bases.append(base)

    def exchange(job, lane, stage):
        index = stage if stage < bits else 2 * bits - 1 - stage
        where = orders[lane][index]
        part = size >> (index + 1)
        if stage < bits:
            gone = bases[lane][index] + (1 - side(*where)) * part
            source = parts.at[job, lane, pl.ds(gone, part)]
            target = inbox.at[job, lane, pl.ds(size - (size >> index), part)]
        else:
            source = target = full.at[job, lane, pl.ds(bases[lane][index + 1], part)]
        return pltpu.make_async_remote_copy(
            src_ref=source, dst_ref=target, send_sem=sends.at[job % 2, lane, stage],
            recv_sem=recvs.at[job % 2, lane, stage], device_id=partner(*where),
            device_id_type=MESH,
        )

    def load(job):
        return pltpu.make_async_copy(feature_stacked.at[job], parts.at[job], load_sems.at[job])

    def store(job):
        return pltpu.make_async_copy(full.at[job], summed_ref.at[job], store_sems.at[job])

    def advance(action, job, loaded):
        if action == 0 and loaded:
            load(job).wait()
        for lane in range(2):
            if action > 0:
                exchange(job, lane, action - 1).wait()
            if 0 < action <= bits:
                part = size >> action
                kept = pl.ds(bases[lane][action], part)
                arrival = inbox[job, lane, pl.ds(size - 2 * part, part)].astype(F32)
                total = (parts[job, lane, kept].astype(F32) + arrival).astype(BF)
                if action < bits:
                    parts[job, lane, kept] = total
                else:
                    full[job, lane, kept] = total
            if action < 2 * bits:
                exchange(job, lane, action).start()
        if action == 2 * bits:
            store(job).start()

    offsets = [3 * action // 2 for action in range(2 * bits + 1)]
    first_sample = max(steps, feature_jobs)

    def tick(point):
        for action in reversed(range(2 * bits + 1)):
            if offsets[action] % TICKS == point:
                job = step - offsets[action] // TICKS

                @pl.when((job >= 0) & (job < feature_jobs))
                def _():
                    advance(action, job, True)

    def vector_exchange(stage):
        return pltpu.make_async_remote_copy(
            src_ref=vector_parts.at[stage], dst_ref=vector_inbox.at[stage],
            send_sem=vector_sends.at[stage], recv_sem=vector_recvs.at[stage],
            device_id=partner(*orders[0][stage]), device_id_type=MESH,
        )

    def vector_advance(action):
        if action > 0:
            vector_exchange(action - 1).wait()
            vector_parts[action] = vector_parts[action - 1] + vector_inbox[action - 1]
        if action < bits:
            vector_exchange(action).start()
        else:
            vectors_ref[...] = vector_parts[bits]

    @pl.when(step == 0)
    def _():
        barrier = pltpu.get_barrier_semaphore()
        for where in orders[0]:
            pl.semaphore_signal(
                barrier, inc=1, device_id=partner(*where), device_id_type=MESH
            )
        for job in range(feature_jobs):
            load(job).start()
        turned[...] = project[...].T
        project_sum[...] = jnp.zeros_like(project_sum)
        output_sum[...] = jnp.zeros_like(output_sum)
        vector_grad[...] = jnp.zeros_like(vector_grad)
        pl.semaphore_wait(barrier, bits)

    samples, width = inputs_ref.shape[1:]
    low_grad = grad_ref[...].reshape(samples, width)
    output_sum[...] += dot(mixed_ref[0], low_grad, 1, 0)
    grad_mixed = dot(output_w[...], low_grad, 1, 1)
    low_mixed = grad_mixed.astype(BF)
    delta = (low_mixed.astype(F32) * mixed_ref[0].astype(F32))
    delta = jnp.sum(delta.reshape(width // HEAD, HEAD, samples), axis=1)
    mask = mask_ref[...]
    ones = jnp.ones((samples, 1), F32)
    one_row = jnp.ones((1, samples), F32)
    for odd in (False, True):
        own = half_ones(odd, samples)
        key_extra = extra_columns(odd, samples, [mask, ones, ones, ones])
        value_extra = extra_columns(odd, samples, [ones, ones, ones])
        for pair in range(width // PAIR):
            head = 2 * pair + odd
            first = head * HEAD
            done = odd * (width // PAIR) + pair
            if done % (HEADS // TICKS) == 0:
                tick(done // (HEADS // TICKS))
            lanes = slice(pair * PAIR, (pair + 1) * PAIR)
            query_rows = saved_ref[0, 0, first:first + HEAD, :]
            value_rows = saved_ref[0, 2, first:first + HEAD, :]
            grad_rows = low_mixed[first:first + HEAD, :]
            keys = saved_ref[0, 1, :, lanes]
            key_rows = keys.T[HEAD:] if odd else keys.T[:HEAD]
            high, middle, low = pieces(-log_ref[0, head:head + 1, :])
            right = stack_half(odd, query_rows, extra_rows(4, samples, [one_row, high, middle, low]))
            high, middle, low = pieces(-delta[head:head + 1, :])
            value_right = jnp.concatenate(
                [grad_rows, extra_rows(3, samples, [high, middle, low])], axis=0
            )
            value_left = jnp.concatenate(
                [value_rows, extra_rows(3, samples, [one_row] * 3)], axis=0
            )
            shares = jnp.exp2(dot(keys * own + key_extra, right, 1, 0) * POWER)
            grad_shares = dot(value_left, value_right, 0, 0)
            low_scores = (shares * grad_shares).astype(BF)
            packed_grad[2 * width + first:2 * width + first + HEAD, :] = dot(
                grad_rows, shares.astype(BF), 1, 1
            ).astype(BF)
            packed_grad[width + first:width + first + HEAD, :] = (
                dot(query_rows, low_scores, 1, 1) * SCALE
            ).astype(BF)
            packed_grad[first:first + HEAD, :] = (
                dot(key_rows, low_scores, 1, 0) * SCALE
            ).astype(BF)
    hat, inverse = normalize(inputs_ref[0].astype(F32))
    normed = (hat * gain_ref[...] + shift_ref[...]).astype(BF)
    project_sum[...] += dot(packed_grad[...], normed, 1, 0)
    grad_normed = dot(packed_grad[...], turned[...], 0, 0)
    grad_rows, grad_gain, grad_shift = normalize_back(grad_normed, gain_ref[...], hat, inverse)
    stream = low_grad.astype(F32)
    input_grad_ref[0] = (stream + grad_rows).astype(BF)
    vector_grad[0:1, :] += grad_gain
    vector_grad[1:2, :] += grad_shift
    vector_grad[2:3, :] += jnp.sum(stream, axis=0, keepdims=True)

    @pl.when(step == steps - 1)
    def _():
        vector_parts[0] = jnp.concatenate([feature_vectors[...], vector_grad[...]], axis=0)
        vector_advance(0)
        sums = [project_sum.at[part * width:(part + 1) * width] for part in range(3)]
        per_column = parts.shape[2] // 2
        for piece, total in enumerate(sums + [output_sum]):
            job, first = divmod(piece * width // TILE, per_column)
            for column in range(width // LANES):
                lane, inner = divmod(column, width // LANES // 2)
                begin = inner * per_column + first
                parts[feature_jobs + job, lane, begin:begin + width // TILE] = total[
                    :, column * LANES:(column + 1) * LANES
                ].astype(BF).reshape(width // TILE, TILE, LANES)
        vector_at = 1
        for at in range(steps, first_sample + sample_jobs + offsets[-1] // TICKS):
            for point in range(TICKS):
                for action in reversed(range(2 * bits + 1)):
                    slot = at - offsets[action] // TICKS
                    if offsets[action] % TICKS != point:
                        continue
                    if 0 <= slot < feature_jobs:
                        advance(action, slot, True)
                    if 0 <= slot - first_sample < sample_jobs:
                        advance(action, feature_jobs + slot - first_sample, False)
                if vector_at <= bits:
                    vector_advance(vector_at)
                    vector_at += 1
        for late in range(vector_at, bits + 1):
            vector_advance(late)
        for job in range(feature_jobs + sample_jobs):
            store(job).wait()


def finish_kernel(
    chunks, summed_ref, input_ref, result_ref,
    up_grad, down_grad, feature_project, feature_output, sample_project, sample_output,
    input_grad_ref, output_ref,
):
    step = pl.program_id(0)
    _, rows, width = output_ref.shape
    input_grad_ref[...] = input_ref[...].astype(F32)
    output_ref[...] = result_ref[...].reshape(1, rows, width)
    bounds = [
        (up_grad, chunks, False), (down_grad, chunks, False), (feature_project, 3, True),
        (feature_output, 1, False), (sample_project, 3, True), (sample_output, 1, False),
    ]
    start = 0
    for target, count, turn in bounds:
        @pl.when((step >= start) & (step < start + count))
        def _():
            for column in range(width // LANES):
                piece = summed_ref[0, column].astype(F32)
                span = slice(column * LANES, (column + 1) * LANES)
                if turn:
                    target[span, :] = piece.T
                else:
                    target[:, span] = piece

        start += count


def to_groups(block_ref, spare):
    features, group, width = block_ref.shape
    rows = block_ref[...].astype(F32).reshape(features * group, width)
    columns = []
    for lanes in range(width // 128):
        spare[lanes] = rows[:, lanes * 128:(lanes + 1) * 128]
        columns.append(
            jnp.concatenate(
                [spare[lanes, pl.ds(one, features, stride=group), :] for one in range(group)],
                axis=0,
            )
        )
    return jnp.concatenate(columns, axis=1)


def from_groups(rows, block_ref, spare):
    features, group, width = block_ref.shape
    for lanes in range(width // 128):
        span = slice(lanes * 128, (lanes + 1) * 128)
        for one in range(group):
            spare[lanes, pl.ds(one, features, stride=group), :] = rows[
                one * features:(one + 1) * features, span
            ]
        block_ref[:, :, span] = spare[lanes].reshape(features, group, 128).astype(BF)


def feature_kernel(
    peers,
    stream_ref, cotangent_hbm, gain_ref, shift_ref, project, output_w,
    bias_ref, dense_gain_ref, dense_shift_ref, up_ref, up_bias_ref, down_ref, down_bias_ref,
    results_ref, grads_ref, stacked_ref, vectors_ref,
    vector_grad, hidden_grad, project_sum, output_sum, up_sum, down_sum, turned, spare, query_t, keys_s, value_t, mixed_t, logs,
    packed_grad, cotangents, result_box, grad_box,
    cotangent_sends, cotangent_recvs, result_sends, grad_sends, result_recvs, grad_recvs, own_sems,
):
    step = pl.program_id(0)
    steps, features, group, _ = cotangents.shape
    slot = step % 2
    me = lax.axis_index("feat")
    local = features // peers
    share = steps * group
    chunks, chunk, width = down_ref.shape
    tokens = features * group
    joined = 2 * features

    def cotangent_moves(at, own=False):
        def part(peer):
            return cotangent_hbm.at[:, pl.ds(pl.multiple_of(peer * share + at * group, group), group), :]

        inbox = cotangents.at[at, pl.ds(me * local, local)]
        if own:
            return pltpu.make_async_copy(part(me), inbox, cotangent_recvs.at[at])
        sends = []
        for hop in range(1, peers):
            peer = (me + hop) % peers
            sends.append(
                push(part(peer), inbox, cotangent_sends.at[at % 2, hop], cotangent_recvs.at[at], peer)
            )
        return sends

    def start_cotangent(at):
        for send in cotangent_moves(at):
            send.start()
        cotangent_moves(at, own=True).start()

    def back_moves(at, slot, box, target, send_sems, recv_sems, own_sem):
        place = target.at[me, :, pl.ds(pl.multiple_of(at * group, group), group), :]
        sends = []
        for hop in range(1, peers):
            peer = (me + hop) % peers
            sends.append(
                push(
                    box.at[slot, pl.ds(peer * local, local)], place,
                    send_sems.at[slot, hop], recv_sems.at[hop], peer,
                )
            )
        own = pltpu.make_async_copy(box.at[slot, pl.ds(me * local, local)], place, own_sem)
        return sends, own

    def result_moves(at, slot):
        return back_moves(
            at, slot, result_box, results_ref, result_sends, result_recvs, own_sems.at[0, slot]
        )

    def grad_moves(at, slot):
        return back_moves(
            at, slot, grad_box, grads_ref, grad_sends, grad_recvs, own_sems.at[1, slot]
        )

    def begin(moves):
        sends, own = moves
        for send in sends:
            send.start()
        own.start()

    def drain(moves):
        sends, own = moves
        for send in sends:
            send.wait_send()
        own.wait()

    @pl.when(step == 0)
    def _():
        greet(peers, me)
        start_cotangent(0)
        turned[...] = project[...].T

    @pl.when(step + 1 < steps)
    def _():
        @pl.when(step >= 1)
        def _():
            for send in cotangent_moves(step - 1):
                send.wait_send()

        start_cotangent(step + 1)

    @pl.when(step == 0)
    def _():
        project_sum[...] = jnp.zeros_like(project_sum)
        output_sum[...] = jnp.zeros_like(output_sum)
        up_sum[...] = jnp.zeros_like(up_sum)
        down_sum[...] = jnp.zeros_like(down_sum)
        vector_grad[...] = jnp.zeros_like(vector_grad)
        hidden_grad[...] = jnp.zeros_like(hidden_grad)

    rows = to_groups(stream_ref, spare)
    hat, inverse = normalize(rows)
    normed = (hat * gain_ref[...] + shift_ref[...]).astype(BF)
    query_t[...] = dot(turned[:width], normed, 1, 1).astype(BF)
    keys_s[...] = dot(normed, project[:, width:2 * width], 1, 0).astype(BF)
    value_t[...] = dot(turned[2 * width:], normed, 1, 1).astype(BF)
    place = lax.broadcasted_iota(jnp.int32, (joined, 1), 0)
    place_row = lax.broadcasted_iota(jnp.int32, (1, joined), 1)
    key_first = (place < features).astype(F32)
    key_second = (place >= features).astype(F32)
    hide_first = jnp.where(place_row >= features, MASKED, 0.0)
    hide_second = jnp.where(place_row < features, MASKED, 0.0)
    ones = jnp.ones((joined, 1), F32)
    one_row = jnp.ones((1, joined), F32)
    extra = extra_rows(2, joined, [hide_first, hide_second])
    for odd in (False, True):
        own = half_ones(odd, joined)
        left_extra = extra_columns(odd, joined, [key_first, key_second])
        for pair in range(width // PAIR):
            head = 2 * pair + odd
            first = head * HEAD
            for part in range(tokens // joined):
                span = slice(part * joined, (part + 1) * joined)
                mixed, log_total = attend_head(
                    keys_s[span, pair * PAIR:(pair + 1) * PAIR], left_extra, own,
                    query_t[first:first + HEAD, span], extra, odd,
                    value_t[first:first + HEAD, span],
                )
                mixed_t[first:first + HEAD, span] = mixed.astype(BF)
                logs[head:head + 1, span] = log_total
    after = rows + dot(mixed_t[...], output_w[...], 0, 0) + bias_ref[...]

    dense_hat, dense_inverse = normalize(after)
    dense_in = (dense_hat * dense_gain_ref[...] + dense_shift_ref[...]).astype(BF)
    arrived(cotangents.at[step], cotangent_recvs.at[step])
    stream = to_groups(cotangents.at[step], spare)
    low_stream = stream.astype(BF)
    result = after + down_bias_ref[...]
    grad_dense = jnp.zeros((tokens, width), F32)
    for index in range(chunks):
        up = up_ref[:, index * chunk:(index + 1) * chunk]
        pre = dot(dense_in, up, 1, 0) + up_bias_ref[index]
        square = pre * pre
        bend = jnp.tanh(pre * (GELU_A + (GELU_A * GELU_B) * square))
        half = 0.5 + 0.5 * bend
        activated = (pre * half).astype(BF)
        slope = half + (pre * half) * (1.0 - bend) * (GELU_A + (3.0 * GELU_A * GELU_B) * square)
        result = result + dot(activated, down_ref[index], 1, 0)
        grad_pre = (slope * dot(low_stream, down_ref[index], 1, 1)).astype(BF)
        grad_dense = grad_dense + dot(grad_pre, up, 1, 1)
        down_sum[index] += dot(activated, low_stream, 0, 0)
        up_sum[index] += dot(dense_in, grad_pre, 0, 0)
        hidden_grad[index] += jnp.sum(grad_pre.astype(F32), axis=0, keepdims=True)

    @pl.when(step >= 2)
    def _():
        drain(result_moves(step - 2, slot))
        drain(grad_moves(step - 2, slot))

    from_groups(result, result_box.at[slot], spare)
    begin(result_moves(step, slot))
    dense_rows, dense_gain_grad, dense_shift_grad = normalize_back(
        grad_dense, dense_gain_ref[...], dense_hat, dense_inverse
    )
    grad_after = stream + dense_rows

    low_grad = grad_after.astype(BF)
    output_sum[...] += dot(mixed_t[...], low_grad, 1, 0)
    low_mixed = dot(output_w[...], low_grad, 1, 1).astype(BF)
    delta = low_mixed.astype(F32) * mixed_t[...].astype(F32)
    delta = jnp.sum(delta.reshape(width // HEAD, HEAD, tokens), axis=1)
    for odd in (False, True):
        own = half_ones(odd, joined)
        key_extra = extra_columns(odd, joined, [key_first, key_second, ones, ones, ones])
        for pair in range(width // PAIR):
            head = 2 * pair + odd
            first = head * HEAD
            for part in range(tokens // joined):
                span = slice(part * joined, (part + 1) * joined)
                query_rows = query_t[first:first + HEAD, span]
                value_rows = value_t[first:first + HEAD, span]
                grad_rows = low_mixed[first:first + HEAD, span]
                keys = keys_s[span, pair * PAIR:(pair + 1) * PAIR]
                key_rows = keys.T[HEAD:] if odd else keys.T[:HEAD]
                high, middle, low = pieces(-logs[head:head + 1, span])
                right = stack_half(
                    odd, query_rows,
                    extra_rows(5, joined, [hide_first, hide_second, high, middle, low]),
                )
                high, middle, low = pieces(-delta[head:head + 1, span])
                value_right = jnp.concatenate(
                    [grad_rows, extra_rows(3, joined, [high, middle, low])], axis=0
                )
                value_left = jnp.concatenate(
                    [value_rows, extra_rows(3, joined, [one_row] * 3)], axis=0
                )
                shares = jnp.exp2(dot(keys * own + key_extra, right, 1, 0) * POWER)
                grad_shares = dot(value_left, value_right, 0, 0)
                low_scores = (shares * grad_shares).astype(BF)
                packed_grad[2 * width + first:2 * width + first + HEAD, span] = dot(
                    grad_rows, shares.astype(BF), 1, 1
                ).astype(BF)
                packed_grad[width + first:width + first + HEAD, span] = (
                    dot(query_rows, low_scores, 1, 1) * SCALE
                ).astype(BF)
                packed_grad[first:first + HEAD, span] = (
                    dot(key_rows, low_scores, 1, 0) * SCALE
                ).astype(BF)
    project_sum[...] += dot(packed_grad[...], normed, 1, 0)
    grad_normed = dot(packed_grad[...], turned[...], 0, 0)
    grad_rows, gain_grad, shift_grad = normalize_back(grad_normed, gain_ref[...], hat, inverse)
    from_groups(grad_after + grad_rows, grad_box.at[slot], spare)
    begin(grad_moves(step, slot))
    vector_grad[0:1, :] += gain_grad
    vector_grad[1:2, :] += shift_grad
    vector_grad[2:3, :] += jnp.sum(low_grad.astype(F32), axis=0, keepdims=True)
    vector_grad[3:4, :] += dense_gain_grad
    vector_grad[4:5, :] += dense_shift_grad
    vector_grad[5:6, :] += jnp.sum(stream, axis=0, keepdims=True)

    @pl.when(step == pl.num_programs(0) - 1)
    def _():
        vectors_ref[...] = jnp.concatenate(
            [vector_grad[...]]
            + [hidden_grad[index].reshape(chunk // width, width) for index in range(chunks)]
            + [jnp.zeros((8 - hidden_grad.size // width, width), F32)], axis=0,
        )
        sums = [up_sum.at[index] for index in range(chunks)]
        sums += [down_sum.at[index] for index in range(chunks)]
        sums += [project_sum.at[part * width:(part + 1) * width] for part in range(3)]
        rows_per_job = stacked_ref.shape[2]
        for piece, total in enumerate(sums + [output_sum]):
            job, first = divmod(piece * width, rows_per_job)
            for column in range(width // LANES):
                stacked_ref[job, column, first:first + width, :] = total[
                    :, column * LANES:(column + 1) * LANES
                ].astype(BF)
        for send in cotangent_moves(step):
            send.wait_send()
        drain(result_moves(step, slot))
        drain(grad_moves(step, slot))
        if steps > 1:
            for send in cotangent_moves(step - 1):
                send.wait_send()
            drain(result_moves(step - 1, 1 - slot))
            drain(grad_moves(step - 1, 1 - slot))
        for hop in range(1, peers):
            source = (me + peers - hop) % peers
            arrived(results_ref.at[source], result_recvs.at[hop])
            arrived(grads_ref.at[source], grad_recvs.at[hop])


def whole(shape):
    return pl.BlockSpec(shape, lambda step: (0,) * len(shape), pipeline_mode=pl.Buffered(1))


def whole_out(shape):
    return pl.BlockSpec(shape, lambda step: (0,) * len(shape))


def call(kernel, grid, in_specs, out_specs, out_shape, scratch, name, flops, nbytes, remote=None):
    return pl.pallas_call(
        kernel,
        grid=(grid,),
        in_specs=in_specs,
        out_specs=out_specs,
        out_shape=[jax.ShapeDtypeStruct(*one) for one in out_shape],
        scratch_shapes=scratch,
        compiler_params=pltpu.CompilerParams(
            dimension_semantics=("arbitrary",), vmem_limit_bytes=LIMIT,
            collective_id=remote, has_side_effects=remote is not None,
        ),
        cost_estimate=pl.CostEstimate(flops=flops, bytes_accessed=nbytes, transcendentals=0),
        name=name,
    )


def body(
    peers, tasks,
    inputs, context, sample_mask,
    sample_gain, sample_shift, sample_project, sample_output, sample_bias,
    feature_gain, feature_shift, feature_project, feature_output, feature_bias,
    dense_gain, dense_shift, up_weight, up_bias, down_weight, down_bias,
    cotangent,
):
    _, local, samples, width = inputs.shape
    hidden = up_weight.shape[1]
    features = local * peers
    share = samples // peers
    group = 8
    chunk = 512
    chunks = hidden // chunk
    row = lambda vector: vector.reshape(1, -1)
    columns = width // LANES
    pieces_in = (2 * chunks + 4, 4)
    size = max(LANES, peers * tasks)
    job_rows = 2 * size * TILE // columns
    feature_jobs, sample_jobs = (count * width // job_rows for count in pieces_in)
    jobs = feature_jobs + sample_jobs
    bits = (peers * tasks).bit_length() - 1

    position = lax.iota(jnp.int32, samples)
    visible = (position < context[0]) & (sample_mask[0] == 1)
    mask = jnp.where(visible, 0.0, MASKED).astype(F32).reshape(samples, 1)
    tokens = inputs[0]

    square = whole((width, width))
    line = whole((1, width))
    token_spec = pl.BlockSpec((1, samples, width), lambda step: (step, 0, 0))
    peer_spec = pl.BlockSpec((peers, 1, share, width), lambda step: (0, step, 0, 0))
    saved_spec = pl.BlockSpec((1, 3, samples, width), lambda step: (step, 0, 0, 0))
    log_spec = pl.BlockSpec((1, HEADS, samples), lambda step: (step, 0, 0))
    anywhere = pl.BlockSpec(memory_space=pl.ANY)
    peer_shape = (peers, local, share, width)
    sems = pltpu.SemaphoreType.DMA
    seen, saved, mixed, logs = call(
        functools.partial(sample_forward_kernel, peers), local,
        [token_spec, whole((samples, 1)), line, line, whole((width, 3 * width)), square, line],
        [anywhere, saved_spec, token_spec, log_spec],
        [
            (peer_shape, BF), ((local, 3, samples, width), BF),
            ((local, width, samples), BF), ((local, HEADS, samples), F32),
        ],
        [
            pltpu.VMEM((3 * width, width), BF), pltpu.VMEM((2, peers, share, width), BF),
            sems((2, peers)), sems((peers,)), sems((2,)),
        ],
        "sample_forward", 60_000_000_000, 30_000_000, 0,
    )(
        tokens, mask, row(sample_gain), row(sample_shift), sample_project, sample_output, row(sample_bias),
    )

    block_tokens = features * group
    block_spec = pl.BlockSpec((features, group, width), lambda step: (0, step, 0))
    down_chunks = down_weight.reshape(chunks, chunk, width)
    result_returned, grad_returned, feature_stacked, feature_vectors = call(
        functools.partial(feature_kernel, peers), share // group,
        [
            block_spec, anywhere, line, line, whole((width, 3 * width)),
            square, line, line, line, whole((width, hidden)), whole((chunks, 1, chunk)),
            whole((chunks, chunk, width)), line,
        ],
        [
            anywhere, anywhere, whole_out((feature_jobs, columns, job_rows, LANES)),
            whole_out((16, width)),
        ],
        [
            (peer_shape, BF), (peer_shape, BF),
            ((feature_jobs, columns, job_rows, LANES), BF), ((16, width), F32),
        ],
        [
            pltpu.VMEM((8, width), F32), pltpu.VMEM((chunks, 1, chunk), F32),
            pltpu.VMEM((3 * width, width), F32), pltpu.VMEM((width, width), F32),
            pltpu.VMEM((chunks, width, chunk), F32), pltpu.VMEM((chunks, chunk, width), F32),
            pltpu.VMEM((3 * width, width), BF), pltpu.VMEM((width // 128, block_tokens, 128), F32),
            pltpu.VMEM((width, block_tokens), BF),
            pltpu.VMEM((block_tokens, width), BF), pltpu.VMEM((width, block_tokens), BF),
            pltpu.VMEM((width, block_tokens), BF), pltpu.VMEM((HEADS, block_tokens), F32),
            pltpu.VMEM((3 * width, block_tokens), BF),
            pltpu.VMEM((share // group, features, group, width), BF),
            pltpu.VMEM((2, features, group, width), BF), pltpu.VMEM((2, features, group, width), BF),
            sems((2, peers)), sems((share // group,)), sems((2, peers)), sems((2, peers)),
            sems((peers,)), sems((peers,)), sems((2, 2)),
        ],
        "feature_block", 130_000_000_000, 40_000_000, 1,
    )(
        seen.reshape(features, share, width), cotangent[0],
        row(feature_gain), row(feature_shift), feature_project,
        feature_output, row(feature_bias), row(dense_gain), row(dense_shift),
        up_weight, up_bias.reshape(chunks, 1, chunk), down_chunks, row(down_bias),
    )
    stack_shape = (jobs, 2, size, TILE, LANES)
    input_grad, summed, vectors = call(
        functools.partial(sample_backward_kernel, peers, tasks, feature_jobs, sample_jobs), local,
        [
            token_spec, whole((samples, 1)), line, line, whole((width, 3 * width)), square,
            saved_spec, token_spec, log_spec, peer_spec, whole((16, width)), anywhere,
        ],
        [token_spec, anywhere, whole_out((24, width))],
        [((local, samples, width), BF), (stack_shape, BF), ((24, width), F32)],
        [
            pltpu.VMEM((3 * width, width), F32), pltpu.VMEM((width, width), F32),
            pltpu.VMEM((8, width), F32),
            pltpu.VMEM((3 * width, width), BF), pltpu.VMEM((3 * width, samples), BF),
            pltpu.VMEM(stack_shape, BF), pltpu.VMEM(stack_shape, BF), pltpu.VMEM(stack_shape, BF),
            pltpu.VMEM((bits + 1, 24, width), F32), pltpu.VMEM((bits, 24, width), F32),
            sems((feature_jobs,)), sems((jobs,)), sems((2, 2, 2 * bits)), sems((2, 2, 2 * bits)),
            sems((bits,)), sems((bits,)),
        ],
        "sample_backward", 110_000_000_000, 50_000_000, 2,
    )(
        tokens, mask, row(sample_gain), row(sample_shift), sample_project, sample_output,
        saved, mixed, logs, grad_returned, feature_vectors,
        feature_stacked.reshape((feature_jobs,) + stack_shape[1:]),
    )
    blocks = sum(pieces_in)
    per_job = job_rows // width
    per_feature = blocks // local
    rows = samples // per_feature
    token_rows = pl.BlockSpec(
        (1, rows, width), lambda step: (step // per_feature, step % per_feature, 0)
    )

    def piece_out(shape, start, count, across):
        def place(step):
            at = jnp.clip(step - start, 0, count - 1)
            return (0, at) if across else (at, 0)

        return pl.BlockSpec(shape, place)

    (
        up_grad, down_grad, feature_project_grad, feature_output_grad,
        sample_project_grad, sample_output_grad, input_grad, output,
    ) = call(
        functools.partial(finish_kernel, chunks), blocks,
        [
            pl.BlockSpec(
                (1, columns, width, LANES), lambda step: (step // per_job, 0, step % per_job, 0)
            ),
            token_rows,
            pl.BlockSpec(
                (peers // per_feature, 1, share, width),
                lambda step: (step % per_feature, step // per_feature, 0, 0),
            ),
        ],
        [
            piece_out((width, chunk), 0, chunks, True),
            piece_out((chunk, width), chunks, chunks, False),
            piece_out((width, width), 2 * chunks, 3, True),
            piece_out((width, width), 2 * chunks + 3, 1, True),
            piece_out((width, width), 2 * chunks + 4, 3, True),
            piece_out((width, width), 2 * chunks + 7, 1, True),
            token_rows, token_rows,
        ],
        [
            ((width, hidden), F32), ((hidden, width), F32), ((width, 3 * width), F32),
            ((width, width), F32), ((width, 3 * width), F32), ((width, width), F32),
            ((local, samples, width), F32), ((local, samples, width), BF),
        ],
        [], "finish", 0, 46_000_000,
    )(summed.reshape(jobs, columns, job_rows, LANES), input_grad, result_returned)
    return (
        output[None], input_grad[None],
        vectors[16], vectors[17], sample_project_grad, sample_output_grad,
        vectors[18], vectors[0], vectors[1], feature_project_grad,
        feature_output_grad, vectors[2], vectors[3], vectors[4],
        up_grad, vectors[8:8 + hidden // width].reshape(hidden), down_grad, vectors[5],
    )


def solution(mesh):
    split = P("task", "feat", None, None)
    return jax.shard_map(
        functools.partial(body, mesh.shape["feat"], mesh.shape["task"]),
        mesh=mesh,
        in_specs=(split, P("task"), P("task", None)) + (P(),) * 16 + (split,),
        out_specs=(split, split) + (P(),) * 16,
        check_vma=False,
    )
```

```python
import functools
import math

import jax
import jax.numpy as jnp
from jax import lax
from jax.experimental import pallas as pl
from jax.experimental.pallas import tpu as pltpu
from jax.sharding import PartitionSpec as P

HEADS = 8
HEAD = 64
PAIR = 2 * HEAD
EPSILON = 1e-05
SCALE = HEAD ** (-0.5)
POWER = SCALE * math.log2(math.e)
MASKED = -1e30
GELU_A = math.sqrt(2.0 / math.pi)
GELU_B = 0.044715
BF = jnp.bfloat16
F32 = jnp.float32
LIMIT = 60 * 1024 * 1024
MESH = pl.DeviceIdType.MESH
TILE = 16
LANES = 128
TICKS = 2


def dot(left, right, left_dim, right_dim):
    return lax.dot_general(
        left, right, (((left_dim,), (right_dim,)), ((), ())), preferred_element_type=F32
    )


def normalize(rows):
    center = rows - jnp.mean(rows, axis=-1, keepdims=True)
    spread = jnp.mean(center * center, axis=-1, keepdims=True)
    inverse = lax.rsqrt(spread + EPSILON)
    return center * inverse, inverse


def normalize_back(grad_normed, gain, hat, inverse):
    scaled = grad_normed * gain
    middle = jnp.mean(scaled, axis=-1, keepdims=True)
    along = jnp.mean(scaled * hat, axis=-1, keepdims=True)
    grad_rows = inverse * (scaled - middle - hat * along)
    grad_gain = jnp.sum(grad_normed * hat, axis=0, keepdims=True)
    grad_shift = jnp.sum(grad_normed, axis=0, keepdims=True)
    return grad_rows, grad_gain, grad_shift


def pieces(row):
    high = row.astype(BF).astype(F32)
    rest = row - high
    middle = rest.astype(BF).astype(F32)
    return high, middle, rest - middle


def extra_rows(count, width, rows):
    place = lax.broadcasted_iota(jnp.int32, (16, width), 0)
    block = jnp.zeros((16, width), F32)
    for index, row in enumerate(rows):
        block = jnp.where(place == index, row, block)
    return jnp.concatenate([block.astype(BF), jnp.zeros((HEAD - 16, width), BF)], axis=0)


def half_ones(odd, depth):
    lane = lax.broadcasted_iota(jnp.int32, (depth, PAIR), 1)
    own = (lane >= HEAD) if odd else (lane < HEAD)
    return own.astype(F32).astype(BF)


def stack_half(odd, own, extra):
    return jnp.concatenate([extra, own] if odd else [own, extra], axis=0)


def extra_columns(odd, depth, columns):
    lane = lax.broadcasted_iota(jnp.int32, (depth, PAIR), 1)
    first = 0 if odd else HEAD
    block = jnp.zeros((depth, PAIR), F32)
    for index, column in enumerate(columns):
        block = jnp.where(lane == first + index, column, block)
    return block.astype(BF)


def attend_head(keys, left_extra, own, query_rows, extra, odd, value_rows):
    left = keys * own + left_extra
    scores = dot(left, stack_half(odd, query_rows, extra), 1, 0)
    highest = jnp.max(scores, axis=0, keepdims=True)
    weights = jnp.exp2((scores - highest) * POWER)
    totals = jnp.sum(weights, axis=0, keepdims=True)
    mixed = dot(value_rows, weights.astype(BF), 1, 0) / totals
    log_total = highest + jnp.log2(totals) * (1.0 / POWER)
    return mixed, log_total


def attend_head_back(left, right, value_left, value_right, query_rows, key_rows, grad_rows):
    shares = jnp.exp2(dot(left, right, 1, 0) * POWER)
    grad_shares = dot(value_left, value_right, 1, 0)
    low_scores = (shares * grad_shares).astype(BF)
    grad_values = dot(grad_rows, shares.astype(BF), 1, 1)
    grad_keys = dot(query_rows, low_scores, 1, 1) * SCALE
    grad_queries = dot(key_rows, low_scores, 1, 0) * SCALE
    return grad_queries, grad_keys, grad_values


def push(source, target, send_sem, recv_sem, peer):
    return pltpu.make_async_remote_copy(
        src_ref=source, dst_ref=target, send_sem=send_sem, recv_sem=recv_sem,
        device_id={"feat": peer}, device_id_type=MESH,
    )


def greet(peers, me):
    barrier = pltpu.get_barrier_semaphore()
    for hop in range(1, peers):
        pl.semaphore_signal(
            barrier, inc=1, device_id={"feat": (me + hop) % peers}, device_id_type=MESH
        )
    pl.semaphore_wait(barrier, peers - 1)


def arrived(buffer, sem):
    pltpu.make_async_copy(buffer, buffer, sem).wait()


def sample_forward_kernel(
    peers,
    inputs_ref, mask_ref, gain_ref, shift_ref, project, output_w, bias_ref,
    seen_ref, saved_ref, mixed_ref, log_ref,
    turned, outbox, send_sems, recv_sems, own_sems,
):
    step = pl.program_id(0)
    steps = pl.num_programs(0)
    slot = step % 2
    me = lax.axis_index("feat")

    @pl.when(step == 0)
    def _():
        greet(peers, me)
        turned[...] = project[...].T

    def moves(at, slot):
        sends = []
        for hop in range(1, peers):
            peer = (me + hop) % peers
            sends.append(
                push(
                    outbox.at[slot, peer], seen_ref.at[me, at],
                    send_sems.at[slot, hop], recv_sems.at[hop], peer,
                )
            )
        own = pltpu.make_async_copy(outbox.at[slot, me], seen_ref.at[me, at], own_sems.at[slot])
        return sends, own

    def drain(at, slot):
        sends, own = moves(at, slot)
        for send in sends:
            send.wait_send()
        own.wait()

    rows = inputs_ref[0].astype(F32)
    samples, width = rows.shape
    hat, _ = normalize(rows)
    normed = (hat * gain_ref[...] + shift_ref[...]).astype(BF)
    saved_ref[0, 0] = dot(turned[:width], normed, 1, 1).astype(BF)
    saved_ref[0, 1] = dot(normed, project[:, width:2 * width], 1, 0).astype(BF)
    saved_ref[0, 2] = dot(turned[2 * width:], normed, 1, 1).astype(BF)
    mask = mask_ref[...]
    extra = extra_rows(1, samples, [jnp.ones((1, samples), F32)])
    for odd in (False, True):
        own = half_ones(odd, samples)
        left_extra = extra_columns(odd, samples, [mask])
        for pair in range(width // PAIR):
            head = 2 * pair + odd
            first = head * HEAD
            mixed, log_total = attend_head(
                saved_ref[0, 1, :, pair * PAIR:(pair + 1) * PAIR], left_extra, own,
                saved_ref[0, 0, first:first + HEAD, :], extra, odd,
                saved_ref[0, 2, first:first + HEAD, :],
            )
            mixed_ref[0, first:first + HEAD, :] = mixed.astype(BF)
            log_ref[0, head:head + 1, :] = log_total
    branch = dot(mixed_ref[0], output_w[...], 0, 0) + bias_ref[...]
    after = (inputs_ref[0].astype(F32) + branch).astype(BF)

    @pl.when(step >= 2)
    def _():
        drain(step - 2, slot)

    outbox[slot] = after.reshape(outbox.shape[1:])
    sends, own = moves(step, slot)
    for send in sends:
        send.start()
    own.start()

    @pl.when(step == steps - 1)
    def _():
        drain(step, slot)
        if seen_ref.shape[1] > 1:
            drain(step - 1, 1 - slot)
        for hop in range(1, peers):
            arrived(seen_ref.at[(me + peers - hop) % peers], recv_sems.at[hop])


def axis_orders(peers, tasks):
    feat_bits = peers.bit_length() - 1
    task_bits = tasks.bit_length() - 1
    half = (feat_bits - 1) // 2
    core = ("feat", 0, 1)
    across = ("feat", 1, half)
    along = ("feat", 1 + half, feat_bits - 1 - half)
    task = ("task", 0, task_bits)
    kept = lambda order: [where for where in order if where[2] > 0]
    return (
        kept([core, across, along, task]), kept([core, along, across, task]),
        kept([("feat", 0, feat_bits), task]),
    )


def hop_offsets(order):
    offsets = [0]
    for _, _, bits in order:
        offsets.append(offsets[-1] + 2 ** bits - 1)
    return offsets


def sample_backward_kernel(
    peers, tasks, feature_jobs, sample_jobs,
    inputs_ref, mask_ref, gain_ref, shift_ref, project, output_w,
    saved_ref, mixed_ref, log_ref, grad_ref, feature_vectors, feature_stacked,
    input_grad_ref, summed_ref, vectors_ref,
    project_sum, output_sum, vector_grad, turned, packed_all,
    parts, inbox, full, feature_parts, feature_inbox, sample_parts, sample_inbox,
    load_sems, store_sems, sends, recvs, vector_sends, vector_recvs,
):
    step = pl.program_id(0)
    steps = pl.num_programs(0)
    local = packed_all.shape[0]
    *orders, vector_order = axis_orders(peers, tasks)
    stages = len(orders[0])
    last = 2 * stages
    size = parts.shape[2]
    place = {"feat": lax.axis_index("feat"), "task": lax.axis_index("task")}

    def digit(where):
        axis, bit, bits = where
        return (place[axis] // 2 ** bit) % 2 ** bits

    def partner(where, hop):
        axis, bit, bits = where
        own = digit(where)
        return {axis: place[axis] + ((own + hop) % 2 ** bits - own) * 2 ** bit}

    hops, bases, sizes = [], [], []
    for order in orders:
        hops.append(hop_offsets(order + order[::-1]))
        base, left = [0], [size]
        for where in order:
            left.append(left[-1] >> where[2])
            base.append(base[-1] + digit(where) * left[-1])
        bases.append(base)
        sizes.append(left)

    def exchanges(job, lane, stage):
        index = stage if stage < stages else last - 1 - stage
        where = orders[lane][index]
        part = sizes[lane][index + 1]
        copies = []
        for hop in range(1, 2 ** where[2]):
            if stage < stages:
                gone = bases[lane][index] + ((digit(where) + hop) % 2 ** where[2]) * part
                source = parts.at[job, lane, pl.ds(gone, part)]
                begin = size - sizes[lane][index] + (hop - 1) * part
                target = inbox.at[job, lane, pl.ds(begin, part)]
            else:
                source = target = full.at[job, lane, pl.ds(bases[lane][index + 1], part)]
            at = hops[lane][stage] + hop - 1
            copies.append(
                pltpu.make_async_remote_copy(
                    src_ref=source, dst_ref=target, send_sem=sends.at[job, lane, at],
                    recv_sem=recvs.at[job, lane, at], device_id=partner(where, hop),
                    device_id_type=MESH,
                )
            )
        return copies

    def load(job):
        return pltpu.make_async_copy(feature_stacked.at[job], parts.at[job], load_sems.at[job])

    def store(job):
        return pltpu.make_async_copy(full.at[job], summed_ref.at[job], store_sems.at[job])

    def advance(action, job, loaded):
        if action == 0 and loaded:
            load(job).wait()
        for lane in range(2):
            if action > 0:
                for copy in exchanges(job, lane, action - 1):
                    copy.wait()
            if 0 < action <= stages:
                part = sizes[lane][action]
                kept = pl.ds(bases[lane][action], part)
                total = parts[job, lane, kept].astype(F32)
                for hop in range(1, 2 ** orders[lane][action - 1][2]):
                    begin = size - sizes[lane][action - 1] + (hop - 1) * part
                    total = total + inbox[job, lane, pl.ds(begin, part)].astype(F32)
                if action < stages:
                    parts[job, lane, kept] = total.astype(BF)
                else:
                    full[job, lane, kept] = total.astype(BF)
            if action < last:
                for copy in exchanges(job, lane, action):
                    copy.start()
        if action == last:
            store(job).start()

    offsets = [0, 1] + [2 * action - 1 for action in range(2, last)] + [2 * last - 2]

    def feature_tick(point):
        for action in reversed(range(last + 1)):
            job = TICKS * step + point - offsets[action]

            @pl.when((job >= 0) & (job < feature_jobs))
            def _():
                advance(action, job, True)

    def sample_tick():
        for action in reversed(range(last + 1)):
            job = step - local - action

            @pl.when((job >= 0) & (job < sample_jobs))
            def _():
                advance(action, feature_jobs + job, False)

    vector_hops = hop_offsets(vector_order)

    def vector_exchanges(kind, stage):
        source, target = [(feature_parts, feature_inbox), (sample_parts, sample_inbox)][kind]
        where = vector_order[stage]
        slot = vector_hops[stage] + stage + digit(where)
        copies = []
        for hop in range(1, 2 ** where[2]):
            at = vector_hops[stage] + hop - 1
            copies.append(
                pltpu.make_async_remote_copy(
                    src_ref=source.at[stage], dst_ref=target.at[slot],
                    send_sem=vector_sends.at[kind, at], recv_sem=vector_recvs.at[kind, at],
                    device_id=partner(where, hop), device_id_type=MESH,
                )
            )
        return copies

    def vector_advance(kind, action):
        source, target = [(feature_parts, feature_inbox), (sample_parts, sample_inbox)][kind]
        if action > 0:
            for copy in vector_exchanges(kind, action - 1):
                copy.wait()
            where = vector_order[action - 1]
            first = vector_hops[action - 1] + action - 1
            target[first + digit(where)] = source[action - 1]
            total = target[first]
            for other in range(1, 2 ** where[2]):
                total = total + target[first + other]
            source[action] = total
        if action < len(vector_order):
            for copy in vector_exchanges(kind, action):
                copy.start()
        else:
            rows = source.shape[1]
            first = kind * feature_parts.shape[1]
            vectors_ref[first:first + rows] = source[action]

    @pl.when(step == 0)
    def _():
        barrier = pltpu.get_barrier_semaphore()
        for where in vector_order:
            for hop in range(1, 2 ** where[2]):
                pl.semaphore_signal(
                    barrier, inc=1, device_id=partner(where, hop), device_id_type=MESH
                )
        for job in range(feature_jobs):
            load(job).start()
        turned[...] = project[...].T
        project_sum[...] = jnp.zeros_like(project_sum)
        output_sum[...] = jnp.zeros_like(output_sum)
        vector_grad[...] = jnp.zeros_like(vector_grad)
        feature_parts[0] = feature_vectors[...]
        pl.semaphore_wait(barrier, vector_hops[-1])
        vector_advance(0, 0)

    for action in range(1, len(vector_order) + 1):
        @pl.when(step == action)
        def _():
            vector_advance(0, action)

    pl.when(step < local)(
        lambda: sample_backward_attention(
            step, feature_tick, inputs_ref, mask_ref, gain_ref, shift_ref, output_w, saved_ref,
            mixed_ref, log_ref, grad_ref, project_sum, output_sum, vector_grad, packed_all,
        )
    )

    @pl.when(step == local - 1)
    def _():
        width = project_sum.shape[1]
        sums = [project_sum.at[part * width:(part + 1) * width] for part in range(3)]
        per_column = size // 2
        for piece, total in enumerate(sums + [output_sum]):
            job, first = divmod(piece * width // TILE, per_column)
            for column in range(width // LANES):
                lane, inner = divmod(column, width // LANES // 2)
                begin = inner * per_column + first
                parts[feature_jobs + job, lane, begin:begin + width // TILE] = total[
                    :, column * LANES:(column + 1) * LANES
                ].astype(BF).reshape(width // TILE, TILE, LANES)

    @pl.when(step >= local)
    def _():
        feature_tick(0)
        sample_tick()
        samples, width = inputs_ref.shape[1:]
        hat, inverse = normalize(inputs_ref[0].astype(F32))
        grad_normed = dot(packed_all[step - local], turned[...], 0, 0)
        grad_rows, grad_gain, grad_shift = normalize_back(grad_normed, gain_ref[...], hat, inverse)
        stream = grad_ref[...].reshape(samples, width).astype(F32)
        input_grad_ref[0] = (stream + grad_rows).astype(BF)
        vector_grad[0:1, :] += grad_gain
        vector_grad[1:2, :] += grad_shift
        feature_tick(1)

    @pl.when(step == steps - 1)
    def _():
        sample_parts[0] = vector_grad[...]
        vector_advance(1, 0)
        for at in range(2 * local, 2 * local + feature_jobs + sample_jobs + last + 1):
            for tick in range(TICKS * at, TICKS * (at + 1)):
                for action in reversed(range(last + 1)):
                    job = tick - offsets[action]
                    if 0 <= job < feature_jobs:
                        advance(action, job, True)
            for action in reversed(range(last + 1)):
                job = at - local - action
                if 0 <= job < sample_jobs:
                    advance(action, feature_jobs + job, False)
            if 0 < at - 2 * local < len(vector_order) + 1:
                vector_advance(1, at - 2 * local)
        for job in range(feature_jobs + sample_jobs):
            store(job).wait()


def sample_backward_attention(
    step, feature_tick, inputs_ref, mask_ref, gain_ref, shift_ref, output_w, saved_ref,
    mixed_ref, log_ref, grad_ref, project_sum, output_sum, vector_grad, packed_all,
):
    packed_grad = packed_all.at[step]
    samples, width = inputs_ref.shape[1:]
    low_grad = grad_ref[...].reshape(samples, width)
    output_sum[...] += dot(mixed_ref[0], low_grad, 1, 0)
    grad_mixed = dot(output_w[...], low_grad, 1, 1)
    low_mixed = grad_mixed.astype(BF)
    delta = (low_mixed.astype(F32) * mixed_ref[0].astype(F32))
    delta = jnp.sum(delta.reshape(width // HEAD, HEAD, samples), axis=1)
    mask = mask_ref[...]
    ones = jnp.ones((samples, 1), F32)
    one_row = jnp.ones((1, samples), F32)
    for odd in (False, True):
        own = half_ones(odd, samples)
        key_extra = extra_columns(odd, samples, [mask, ones, ones, ones])
        value_extra = extra_columns(odd, samples, [ones, ones, ones])
        for pair in range(width // PAIR):
            head = 2 * pair + odd
            first = head * HEAD
            done = odd * (width // PAIR) + pair
            if done % (HEADS // TICKS) == 0:
                feature_tick(done // (HEADS // TICKS))
            lanes = slice(pair * PAIR, (pair + 1) * PAIR)
            query_rows = saved_ref[0, 0, first:first + HEAD, :]
            value_rows = saved_ref[0, 2, first:first + HEAD, :]
            grad_rows = low_mixed[first:first + HEAD, :]
            keys = saved_ref[0, 1, :, lanes]
            key_rows = keys.T[HEAD:] if odd else keys.T[:HEAD]
            high, middle, low = pieces(-log_ref[0, head:head + 1, :])
            right = stack_half(odd, query_rows, extra_rows(4, samples, [one_row, high, middle, low]))
            high, middle, low = pieces(-delta[head:head + 1, :])
            value_right = jnp.concatenate(
                [grad_rows, extra_rows(3, samples, [high, middle, low])], axis=0
            )
            value_left = jnp.concatenate(
                [value_rows, extra_rows(3, samples, [one_row] * 3)], axis=0
            )
            shares = jnp.exp2(dot(keys * own + key_extra, right, 1, 0) * POWER)
            grad_shares = dot(value_left, value_right, 0, 0)
            low_scores = (shares * grad_shares).astype(BF)
            packed_grad[2 * width + first:2 * width + first + HEAD, :] = dot(
                grad_rows, shares.astype(BF), 1, 1
            ).astype(BF)
            packed_grad[width + first:width + first + HEAD, :] = (
                dot(query_rows, low_scores, 1, 1) * SCALE
            ).astype(BF)
            packed_grad[first:first + HEAD, :] = (
                dot(key_rows, low_scores, 1, 0) * SCALE
            ).astype(BF)
    hat, _ = normalize(inputs_ref[0].astype(F32))
    normed = (hat * gain_ref[...] + shift_ref[...]).astype(BF)
    project_sum[...] += dot(packed_grad[...], normed, 1, 0)
    vector_grad[2:3, :] += jnp.sum(low_grad.astype(F32), axis=0, keepdims=True)


def finish_kernel(
    chunks, summed_ref, input_ref, result_ref,
    up_grad, down_grad, feature_project, feature_output, sample_project, sample_output,
    input_grad_ref, output_ref,
):
    step = pl.program_id(0)
    _, rows, width = output_ref.shape
    input_grad_ref[...] = input_ref[...].astype(F32)
    output_ref[...] = result_ref[...].reshape(1, rows, width)
    bounds = [
        (up_grad, chunks, False), (down_grad, chunks, False), (feature_project, 3, True),
        (feature_output, 1, False), (sample_project, 3, True), (sample_output, 1, False),
    ]
    start = 0
    for target, count, turn in bounds:
        @pl.when((step >= start) & (step < start + count))
        def _():
            for column in range(width // LANES):
                piece = summed_ref[0, column].astype(F32)
                span = slice(column * LANES, (column + 1) * LANES)
                if turn:
                    target[span, :] = piece.T
                else:
                    target[:, span] = piece

        start += count


def to_groups(block_ref, spare):
    features, group, width = block_ref.shape
    rows = block_ref[...].astype(F32).reshape(features * group, width)
    columns = []
    for lanes in range(width // 128):
        spare[lanes] = rows[:, lanes * 128:(lanes + 1) * 128]
        columns.append(
            jnp.concatenate(
                [spare[lanes, pl.ds(one, features, stride=group), :] for one in range(group)],
                axis=0,
            )
        )
    return jnp.concatenate(columns, axis=1)


def from_groups(rows, block_ref, spare):
    features, group, width = block_ref.shape
    for lanes in range(width // 128):
        span = slice(lanes * 128, (lanes + 1) * 128)
        for one in range(group):
            spare[lanes, pl.ds(one, features, stride=group), :] = rows[
                one * features:(one + 1) * features, span
            ]
        block_ref[:, :, span] = spare[lanes].reshape(features, group, 128).astype(BF)


def feature_kernel(
    peers,
    stream_ref, cotangent_hbm, gain_ref, shift_ref, project, output_w,
    bias_ref, dense_gain_ref, dense_shift_ref, up_ref, up_bias_ref, down_ref, down_bias_ref,
    results_ref, grads_ref, stacked_ref, vectors_ref,
    vector_grad, hidden_grad, project_sum, output_sum, up_sum, down_sum, turned, spare, query_t, keys_s, value_t, mixed_t, logs,
    packed_grad, cotangents, result_box, grad_box,
    cotangent_sends, cotangent_recvs, result_sends, grad_sends, result_recvs, grad_recvs, own_sems,
):
    step = pl.program_id(0)
    steps, features, group, _ = cotangents.shape
    slot = step % 2
    me = lax.axis_index("feat")
    local = features // peers
    share = steps * group
    chunks, chunk, width = down_ref.shape
    tokens = features * group
    joined = 2 * features

    def cotangent_moves(at, own=False):
        def part(peer):
            return cotangent_hbm.at[:, pl.ds(pl.multiple_of(peer * share + at * group, group), group), :]

        inbox = cotangents.at[at, pl.ds(me * local, local)]
        if own:
            return pltpu.make_async_copy(part(me), inbox, cotangent_recvs.at[at])
        sends = []
        for hop in range(1, peers):
            peer = (me + hop) % peers
            sends.append(
                push(part(peer), inbox, cotangent_sends.at[at % 2, hop], cotangent_recvs.at[at], peer)
            )
        return sends

    def start_cotangent(at):
        for send in cotangent_moves(at):
            send.start()
        cotangent_moves(at, own=True).start()

    def back_moves(at, slot, box, target, send_sems, recv_sems, own_sem):
        place = target.at[me, :, pl.ds(pl.multiple_of(at * group, group), group), :]
        sends = []
        for hop in range(1, peers):
            peer = (me + hop) % peers
            sends.append(
                push(
                    box.at[slot, pl.ds(peer * local, local)], place,
                    send_sems.at[slot, hop], recv_sems.at[hop], peer,
                )
            )
        own = pltpu.make_async_copy(box.at[slot, pl.ds(me * local, local)], place, own_sem)
        return sends, own

    def result_moves(at, slot):
        return back_moves(
            at, slot, result_box, results_ref, result_sends, result_recvs, own_sems.at[0, slot]
        )

    def grad_moves(at, slot):
        return back_moves(
            at, slot, grad_box, grads_ref, grad_sends, grad_recvs, own_sems.at[1, slot]
        )

    def begin(moves):
        sends, own = moves
        for send in sends:
            send.start()
        own.start()

    def drain(moves):
        sends, own = moves
        for send in sends:
            send.wait_send()
        own.wait()

    @pl.when(step == 0)
    def _():
        greet(peers, me)
        start_cotangent(0)
        turned[...] = project[...].T

    @pl.when(step + 1 < steps)
    def _():
        @pl.when(step >= 1)
        def _():
            for send in cotangent_moves(step - 1):
                send.wait_send()

        start_cotangent(step + 1)

    @pl.when(step == 0)
    def _():
        project_sum[...] = jnp.zeros_like(project_sum)
        output_sum[...] = jnp.zeros_like(output_sum)
        up_sum[...] = jnp.zeros_like(up_sum)
        down_sum[...] = jnp.zeros_like(down_sum)
        vector_grad[...] = jnp.zeros_like(vector_grad)
        hidden_grad[...] = jnp.zeros_like(hidden_grad)

    rows = to_groups(stream_ref, spare)
    hat, inverse = normalize(rows)
    normed = (hat * gain_ref[...] + shift_ref[...]).astype(BF)
    query_t[...] = dot(turned[:width], normed, 1, 1).astype(BF)
    keys_s[...] = dot(normed, project[:, width:2 * width], 1, 0).astype(BF)
    value_t[...] = dot(turned[2 * width:], normed, 1, 1).astype(BF)
    place = lax.broadcasted_iota(jnp.int32, (joined, 1), 0)
    place_row = lax.broadcasted_iota(jnp.int32, (1, joined), 1)
    key_first = (place < features).astype(F32)
    key_second = (place >= features).astype(F32)
    hide_first = jnp.where(place_row >= features, MASKED, 0.0)
    hide_second = jnp.where(place_row < features, MASKED, 0.0)
    ones = jnp.ones((joined, 1), F32)
    one_row = jnp.ones((1, joined), F32)
    extra = extra_rows(2, joined, [hide_first, hide_second])
    for odd in (False, True):
        own = half_ones(odd, joined)
        left_extra = extra_columns(odd, joined, [key_first, key_second])
        for pair in range(width // PAIR):
            head = 2 * pair + odd
            first = head * HEAD
            for part in range(tokens // joined):
                span = slice(part * joined, (part + 1) * joined)
                mixed, log_total = attend_head(
                    keys_s[span, pair * PAIR:(pair + 1) * PAIR], left_extra, own,
                    query_t[first:first + HEAD, span], extra, odd,
                    value_t[first:first + HEAD, span],
                )
                mixed_t[first:first + HEAD, span] = mixed.astype(BF)
                logs[head:head + 1, span] = log_total
    after = rows + dot(mixed_t[...], output_w[...], 0, 0) + bias_ref[...]

    dense_hat, dense_inverse = normalize(after)
    dense_in = (dense_hat * dense_gain_ref[...] + dense_shift_ref[...]).astype(BF)
    arrived(cotangents.at[step], cotangent_recvs.at[step])
    stream = to_groups(cotangents.at[step], spare)
    low_stream = stream.astype(BF)
    result = after + down_bias_ref[...]
    grad_dense = jnp.zeros((tokens, width), F32)
    for index in range(chunks):
        up = up_ref[:, index * chunk:(index + 1) * chunk]
        pre = dot(dense_in, up, 1, 0) + up_bias_ref[index]
        square = pre * pre
        bend = jnp.tanh(pre * (GELU_A + (GELU_A * GELU_B) * square))
        half = 0.5 + 0.5 * bend
        activated = (pre * half).astype(BF)
        slope = half + (pre * half) * (1.0 - bend) * (GELU_A + (3.0 * GELU_A * GELU_B) * square)
        result = result + dot(activated, down_ref[index], 1, 0)
        grad_pre = (slope * dot(low_stream, down_ref[index], 1, 1)).astype(BF)
        grad_dense = grad_dense + dot(grad_pre, up, 1, 1)
        down_sum[index] += dot(activated, low_stream, 0, 0)
        up_sum[index] += dot(dense_in, grad_pre, 0, 0)
        hidden_grad[index] += jnp.sum(grad_pre.astype(F32), axis=0, keepdims=True)

    @pl.when(step >= 2)
    def _():
        drain(result_moves(step - 2, slot))
        drain(grad_moves(step - 2, slot))

    from_groups(result, result_box.at[slot], spare)
    begin(result_moves(step, slot))
    dense_rows, dense_gain_grad, dense_shift_grad = normalize_back(
        grad_dense, dense_gain_ref[...], dense_hat, dense_inverse
    )
    grad_after = stream + dense_rows

    low_grad = grad_after.astype(BF)
    output_sum[...] += dot(mixed_t[...], low_grad, 1, 0)
    low_mixed = dot(output_w[...], low_grad, 1, 1).astype(BF)
    delta = low_mixed.astype(F32) * mixed_t[...].astype(F32)
    delta = jnp.sum(delta.reshape(width // HEAD, HEAD, tokens), axis=1)
    for odd in (False, True):
        own = half_ones(odd, joined)
        key_extra = extra_columns(odd, joined, [key_first, key_second, ones, ones, ones])
        for pair in range(width // PAIR):
            head = 2 * pair + odd
            first = head * HEAD
            for part in range(tokens // joined):
                span = slice(part * joined, (part + 1) * joined)
                query_rows = query_t[first:first + HEAD, span]
                value_rows = value_t[first:first + HEAD, span]
                grad_rows = low_mixed[first:first + HEAD, span]
                keys = keys_s[span, pair * PAIR:(pair + 1) * PAIR]
                key_rows = keys.T[HEAD:] if odd else keys.T[:HEAD]
                high, middle, low = pieces(-logs[head:head + 1, span])
                right = stack_half(
                    odd, query_rows,
                    extra_rows(5, joined, [hide_first, hide_second, high, middle, low]),
                )
                high, middle, low = pieces(-delta[head:head + 1, span])
                value_right = jnp.concatenate(
                    [grad_rows, extra_rows(3, joined, [high, middle, low])], axis=0
                )
                value_left = jnp.concatenate(
                    [value_rows, extra_rows(3, joined, [one_row] * 3)], axis=0
                )
                shares = jnp.exp2(dot(keys * own + key_extra, right, 1, 0) * POWER)
                grad_shares = dot(value_left, value_right, 0, 0)
                low_scores = (shares * grad_shares).astype(BF)
                packed_grad[2 * width + first:2 * width + first + HEAD, span] = dot(
                    grad_rows, shares.astype(BF), 1, 1
                ).astype(BF)
                packed_grad[width + first:width + first + HEAD, span] = (
                    dot(query_rows, low_scores, 1, 1) * SCALE
                ).astype(BF)
                packed_grad[first:first + HEAD, span] = (
                    dot(key_rows, low_scores, 1, 0) * SCALE
                ).astype(BF)
    project_sum[...] += dot(packed_grad[...], normed, 1, 0)
    grad_normed = dot(packed_grad[...], turned[...], 0, 0)
    grad_rows, gain_grad, shift_grad = normalize_back(grad_normed, gain_ref[...], hat, inverse)
    from_groups(grad_after + grad_rows, grad_box.at[slot], spare)
    begin(grad_moves(step, slot))
    vector_grad[0:1, :] += gain_grad
    vector_grad[1:2, :] += shift_grad
    vector_grad[2:3, :] += jnp.sum(low_grad.astype(F32), axis=0, keepdims=True)
    vector_grad[3:4, :] += dense_gain_grad
    vector_grad[4:5, :] += dense_shift_grad
    vector_grad[5:6, :] += jnp.sum(stream, axis=0, keepdims=True)

    @pl.when(step == pl.num_programs(0) - 1)
    def _():
        vectors_ref[...] = jnp.concatenate(
            [vector_grad[...]]
            + [hidden_grad[index].reshape(chunk // width, width) for index in range(chunks)]
            + [jnp.zeros((8 - hidden_grad.size // width, width), F32)], axis=0,
        )
        sums = [up_sum.at[index] for index in range(chunks)]
        sums += [down_sum.at[index] for index in range(chunks)]
        sums += [project_sum.at[part * width:(part + 1) * width] for part in range(3)]
        rows_per_job = stacked_ref.shape[2]
        for piece, total in enumerate(sums + [output_sum]):
            job, first = divmod(piece * width, rows_per_job)
            for column in range(width // LANES):
                stacked_ref[job, column, first:first + width, :] = total[
                    :, column * LANES:(column + 1) * LANES
                ].astype(BF)
        for send in cotangent_moves(step):
            send.wait_send()
        drain(result_moves(step, slot))
        drain(grad_moves(step, slot))
        if steps > 1:
            for send in cotangent_moves(step - 1):
                send.wait_send()
            drain(result_moves(step - 1, 1 - slot))
            drain(grad_moves(step - 1, 1 - slot))
        for hop in range(1, peers):
            source = (me + peers - hop) % peers
            arrived(results_ref.at[source], result_recvs.at[hop])
            arrived(grads_ref.at[source], grad_recvs.at[hop])


def whole(shape):
    return pl.BlockSpec(shape, lambda step: (0,) * len(shape), pipeline_mode=pl.Buffered(1))


def whole_out(shape):
    return pl.BlockSpec(shape, lambda step: (0,) * len(shape))


def call(kernel, grid, in_specs, out_specs, out_shape, scratch, name, flops, nbytes, remote=None):
    return pl.pallas_call(
        kernel,
        grid=(grid,),
        in_specs=in_specs,
        out_specs=out_specs,
        out_shape=[jax.ShapeDtypeStruct(*one) for one in out_shape],
        scratch_shapes=scratch,
        compiler_params=pltpu.CompilerParams(
            dimension_semantics=("arbitrary",), vmem_limit_bytes=LIMIT,
            collective_id=remote, has_side_effects=remote is not None,
        ),
        cost_estimate=pl.CostEstimate(flops=flops, bytes_accessed=nbytes, transcendentals=0),
        name=name,
    )


def body(
    peers, tasks,
    inputs, context, sample_mask,
    sample_gain, sample_shift, sample_project, sample_output, sample_bias,
    feature_gain, feature_shift, feature_project, feature_output, feature_bias,
    dense_gain, dense_shift, up_weight, up_bias, down_weight, down_bias,
    cotangent,
):
    _, local, samples, width = inputs.shape
    hidden = up_weight.shape[1]
    features = local * peers
    share = samples // peers
    group = 8
    chunk = 512
    chunks = hidden // chunk
    row = lambda vector: vector.reshape(1, -1)
    columns = width // LANES
    pieces_in = (2 * chunks + 4, 4)
    size = max(LANES, peers * tasks)
    job_rows = 2 * size * TILE // columns
    feature_jobs, sample_jobs = (count * width // job_rows for count in pieces_in)
    jobs = feature_jobs + sample_jobs
    *orders, vector_order = axis_orders(peers, tasks)
    lane_hops = hop_offsets(orders[0] + orders[0][::-1])[-1]
    vector_hops = hop_offsets(vector_order)[-1]
    vector_stages = len(vector_order)

    position = lax.iota(jnp.int32, samples)
    visible = (position < context[0]) & (sample_mask[0] == 1)
    mask = jnp.where(visible, 0.0, MASKED).astype(F32).reshape(samples, 1)
    tokens = inputs[0]

    square = whole((width, width))
    line = whole((1, width))
    token_spec = pl.BlockSpec((1, samples, width), lambda step: (step, 0, 0))
    peer_spec = pl.BlockSpec((peers, 1, share, width), lambda step: (0, step, 0, 0))
    saved_spec = pl.BlockSpec((1, 3, samples, width), lambda step: (step, 0, 0, 0))
    log_spec = pl.BlockSpec((1, HEADS, samples), lambda step: (step, 0, 0))
    anywhere = pl.BlockSpec(memory_space=pl.ANY)
    peer_shape = (peers, local, share, width)
    sems = pltpu.SemaphoreType.DMA
    seen, saved, mixed, logs = call(
        functools.partial(sample_forward_kernel, peers), local,
        [token_spec, whole((samples, 1)), line, line, whole((width, 3 * width)), square, line],
        [anywhere, saved_spec, token_spec, log_spec],
        [
            (peer_shape, BF), ((local, 3, samples, width), BF),
            ((local, width, samples), BF), ((local, HEADS, samples), F32),
        ],
        [
            pltpu.VMEM((3 * width, width), BF), pltpu.VMEM((2, peers, share, width), BF),
            sems((2, peers)), sems((peers,)), sems((2,)),
        ],
        "sample_forward", 60_000_000_000, 30_000_000, 0,
    )(
        tokens, mask, row(sample_gain), row(sample_shift), sample_project, sample_output, row(sample_bias),
    )

    block_tokens = features * group
    block_spec = pl.BlockSpec((features, group, width), lambda step: (0, step, 0))
    down_chunks = down_weight.reshape(chunks, chunk, width)
    result_returned, grad_returned, feature_stacked, feature_vectors = call(
        functools.partial(feature_kernel, peers), share // group,
        [
            block_spec, anywhere, line, line, whole((width, 3 * width)),
            square, line, line, line, whole((width, hidden)), whole((chunks, 1, chunk)),
            whole((chunks, chunk, width)), line,
        ],
        [
            anywhere, anywhere, whole_out((feature_jobs, columns, job_rows, LANES)),
            whole_out((16, width)),
        ],
        [
            (peer_shape, BF), (peer_shape, BF),
            ((feature_jobs, columns, job_rows, LANES), BF), ((16, width), F32),
        ],
        [
            pltpu.VMEM((8, width), F32), pltpu.VMEM((chunks, 1, chunk), F32),
            pltpu.VMEM((3 * width, width), F32), pltpu.VMEM((width, width), F32),
            pltpu.VMEM((chunks, width, chunk), F32), pltpu.VMEM((chunks, chunk, width), F32),
            pltpu.VMEM((3 * width, width), BF), pltpu.VMEM((width // 128, block_tokens, 128), F32),
            pltpu.VMEM((width, block_tokens), BF),
            pltpu.VMEM((block_tokens, width), BF), pltpu.VMEM((width, block_tokens), BF),
            pltpu.VMEM((width, block_tokens), BF), pltpu.VMEM((HEADS, block_tokens), F32),
            pltpu.VMEM((3 * width, block_tokens), BF),
            pltpu.VMEM((share // group, features, group, width), BF),
            pltpu.VMEM((2, features, group, width), BF), pltpu.VMEM((2, features, group, width), BF),
            sems((2, peers)), sems((share // group,)), sems((2, peers)), sems((2, peers)),
            sems((peers,)), sems((peers,)), sems((2, 2)),
        ],
        "feature_block", 130_000_000_000, 40_000_000, 1,
    )(
        seen.reshape(features, share, width), cotangent[0],
        row(feature_gain), row(feature_shift), feature_project,
        feature_output, row(feature_bias), row(dense_gain), row(dense_shift),
        up_weight, up_bias.reshape(chunks, 1, chunk), down_chunks, row(down_bias),
    )
    stack_shape = (jobs, 2, size, TILE, LANES)
    again = lambda *tail: lambda step: (step % local,) + tail
    early = lambda *tail: lambda step: (jnp.minimum(step, local - 1),) + tail
    input_grad, summed, vectors = call(
        functools.partial(sample_backward_kernel, peers, tasks, feature_jobs, sample_jobs),
        2 * local,
        [
            pl.BlockSpec((1, samples, width), again(0, 0)), whole((samples, 1)), line, line,
            whole((width, 3 * width)), square,
            pl.BlockSpec((1, 3, samples, width), early(0, 0, 0)),
            pl.BlockSpec((1, samples, width), early(0, 0)),
            pl.BlockSpec((1, HEADS, samples), early(0, 0)),
            pl.BlockSpec((peers, 1, share, width), lambda step: (0, step % local, 0, 0)),
            whole((16, width)), anywhere,
        ],
        [
            pl.BlockSpec((1, samples, width), lambda step: (jnp.maximum(step - local, 0), 0, 0)),
            anywhere, whole_out((24, width)),
        ],
        [((local, samples, width), BF), (stack_shape, BF), ((24, width), F32)],
        [
            pltpu.VMEM((3 * width, width), F32), pltpu.VMEM((width, width), F32),
            pltpu.VMEM((8, width), F32), pltpu.VMEM((3 * width, width), BF),
            pltpu.VMEM((local, 3 * width, samples), BF),
            pltpu.VMEM(stack_shape, BF), pltpu.VMEM(stack_shape, BF), pltpu.VMEM(stack_shape, BF),
            pltpu.VMEM((vector_stages + 1, 16, width), F32),
            pltpu.VMEM((vector_hops + vector_stages, 16, width), F32),
            pltpu.VMEM((vector_stages + 1, 8, width), F32),
            pltpu.VMEM((vector_hops + vector_stages, 8, width), F32),
            sems((feature_jobs,)), sems((jobs,)), sems((jobs, 2, lane_hops)), sems((jobs, 2, lane_hops)),
            sems((2, vector_hops)), sems((2, vector_hops)),
        ],
        "sample_backward", 110_000_000_000, 50_000_000, 2,
    )(
        tokens, mask, row(sample_gain), row(sample_shift), sample_project, sample_output,
        saved, mixed, logs, grad_returned, feature_vectors,
        feature_stacked.reshape((feature_jobs,) + stack_shape[1:]),
    )
    blocks = sum(pieces_in)
    per_job = job_rows // width
    per_feature = blocks // local
    rows = samples // per_feature
    token_rows = pl.BlockSpec(
        (1, rows, width), lambda step: (step // per_feature, step % per_feature, 0)
    )

    def piece_out(shape, start, count, across):
        def place(step):
            at = jnp.clip(step - start, 0, count - 1)
            return (0, at) if across else (at, 0)

        return pl.BlockSpec(shape, place)

    (
        up_grad, down_grad, feature_project_grad, feature_output_grad,
        sample_project_grad, sample_output_grad, input_grad, output,
    ) = call(
        functools.partial(finish_kernel, chunks), blocks,
        [
            pl.BlockSpec(
                (1, columns, width, LANES), lambda step: (step // per_job, 0, step % per_job, 0)
            ),
            token_rows,
            pl.BlockSpec(
                (peers // per_feature, 1, share, width),
                lambda step: (step % per_feature, step // per_feature, 0, 0),
            ),
        ],
        [
            piece_out((width, chunk), 0, chunks, True),
            piece_out((chunk, width), chunks, chunks, False),
            piece_out((width, width), 2 * chunks, 3, True),
            piece_out((width, width), 2 * chunks + 3, 1, True),
            piece_out((width, width), 2 * chunks + 4, 3, True),
            piece_out((width, width), 2 * chunks + 7, 1, True),
            token_rows, token_rows,
        ],
        [
            ((width, hidden), F32), ((hidden, width), F32), ((width, 3 * width), F32),
            ((width, width), F32), ((width, 3 * width), F32), ((width, width), F32),
            ((local, samples, width), F32), ((local, samples, width), BF),
        ],
        [], "finish", 0, 46_000_000,
    )(summed.reshape(jobs, columns, job_rows, LANES), input_grad, result_returned)
    return (
        output[None], input_grad[None],
        vectors[16], vectors[17], sample_project_grad, sample_output_grad,
        vectors[18], vectors[0], vectors[1], feature_project_grad,
        feature_output_grad, vectors[2], vectors[3], vectors[4],
        up_grad, vectors[8:8 + hidden // width].reshape(hidden), down_grad, vectors[5],
    )


def solution(mesh):
    split = P("task", "feat", None, None)
    return jax.shard_map(
        functools.partial(body, mesh.shape["feat"], mesh.shape["task"]),
        mesh=mesh,
        in_specs=(split, P("task"), P("task", None)) + (P(),) * 16 + (split,),
        out_specs=(split, split) + (P(),) * 16,
        check_vma=False,
    )
```

```python
import functools
import math

import jax
import jax.numpy as jnp
from jax import lax
from jax.experimental import pallas as pl
from jax.experimental.pallas import tpu as pltpu
from jax.sharding import PartitionSpec as P

HEADS = 8
HEAD = 64
PAIR = 2 * HEAD
EPSILON = 1e-05
SCALE = HEAD ** (-0.5)
POWER = SCALE * math.log2(math.e)
MASKED = -1e30
GELU_A = math.sqrt(2.0 / math.pi)
GELU_B = 0.044715
BF = jnp.bfloat16
F32 = jnp.float32
LIMIT = 60 * 1024 * 1024
MESH = pl.DeviceIdType.MESH
TILE = 16
LANES = 128
TICKS = 2


def dot(left, right, left_dim, right_dim):
    return lax.dot_general(
        left, right, (((left_dim,), (right_dim,)), ((), ())), preferred_element_type=F32
    )


def normalize(rows):
    center = rows - jnp.mean(rows, axis=-1, keepdims=True)
    spread = jnp.mean(center * center, axis=-1, keepdims=True)
    inverse = lax.rsqrt(spread + EPSILON)
    return center * inverse, inverse


def normalize_back(grad_normed, gain, hat, inverse):
    scaled = grad_normed * gain
    middle = jnp.mean(scaled, axis=-1, keepdims=True)
    along = jnp.mean(scaled * hat, axis=-1, keepdims=True)
    grad_rows = inverse * (scaled - middle - hat * along)
    grad_gain = jnp.sum(grad_normed * hat, axis=0, keepdims=True)
    grad_shift = jnp.sum(grad_normed, axis=0, keepdims=True)
    return grad_rows, grad_gain, grad_shift


def pieces(row):
    high = row.astype(BF).astype(F32)
    rest = row - high
    middle = rest.astype(BF).astype(F32)
    return high, middle, rest - middle


def extra_rows(count, width, rows):
    place = lax.broadcasted_iota(jnp.int32, (16, width), 0)
    block = jnp.zeros((16, width), F32)
    for index, row in enumerate(rows):
        block = jnp.where(place == index, row, block)
    return jnp.concatenate([block.astype(BF), jnp.zeros((HEAD - 16, width), BF)], axis=0)


def half_ones(odd, depth):
    lane = lax.broadcasted_iota(jnp.int32, (depth, PAIR), 1)
    own = (lane >= HEAD) if odd else (lane < HEAD)
    return own.astype(F32).astype(BF)


def stack_half(odd, own, extra):
    return jnp.concatenate([extra, own] if odd else [own, extra], axis=0)


def extra_columns(odd, depth, columns):
    lane = lax.broadcasted_iota(jnp.int32, (depth, PAIR), 1)
    first = 0 if odd else HEAD
    block = jnp.zeros((depth, PAIR), F32)
    for index, column in enumerate(columns):
        block = jnp.where(lane == first + index, column, block)
    return block.astype(BF)


def attend_head(keys, left_extra, own, query_rows, extra, odd, value_rows):
    left = keys * own + left_extra
    scores = dot(left, stack_half(odd, query_rows, extra), 1, 0)
    highest = jnp.max(scores, axis=0, keepdims=True)
    weights = jnp.exp2((scores - highest) * POWER)
    totals = jnp.sum(weights, axis=0, keepdims=True)
    mixed = dot(value_rows, weights.astype(BF), 1, 0) / totals
    log_total = highest + jnp.log2(totals) * (1.0 / POWER)
    return mixed, log_total


def attend_head_back(left, right, value_left, value_right, query_rows, key_rows, grad_rows):
    shares = jnp.exp2(dot(left, right, 1, 0) * POWER)
    grad_shares = dot(value_left, value_right, 1, 0)
    low_scores = (shares * grad_shares).astype(BF)
    grad_values = dot(grad_rows, shares.astype(BF), 1, 1)
    grad_keys = dot(query_rows, low_scores, 1, 1) * SCALE
    grad_queries = dot(key_rows, low_scores, 1, 0) * SCALE
    return grad_queries, grad_keys, grad_values


def push(source, target, send_sem, recv_sem, peer):
    return pltpu.make_async_remote_copy(
        src_ref=source, dst_ref=target, send_sem=send_sem, recv_sem=recv_sem,
        device_id={"feat": peer}, device_id_type=MESH,
    )


def greet(peers, me):
    barrier = pltpu.get_barrier_semaphore()
    for hop in range(1, peers):
        pl.semaphore_signal(
            barrier, inc=1, device_id={"feat": (me + hop) % peers}, device_id_type=MESH
        )
    pl.semaphore_wait(barrier, peers - 1)


def arrived(buffer, sem):
    pltpu.make_async_copy(buffer, buffer, sem).wait()


def sample_forward_kernel(
    peers,
    inputs_ref, mask_ref, gain_ref, shift_ref, project, output_w, bias_ref,
    seen_ref, saved_ref, mixed_ref, log_ref,
    turned, outbox, send_sems, recv_sems, own_sems,
):
    step = pl.program_id(0)
    steps = pl.num_programs(0)
    slot = step % 2
    me = lax.axis_index("feat")

    @pl.when(step == 0)
    def _():
        greet(peers, me)
        turned[...] = project[...].T

    def moves(at, slot):
        sends = []
        for hop in range(1, peers):
            peer = (me + hop) % peers
            sends.append(
                push(
                    outbox.at[slot, peer], seen_ref.at[me, at],
                    send_sems.at[slot, hop], recv_sems.at[hop], peer,
                )
            )
        own = pltpu.make_async_copy(outbox.at[slot, me], seen_ref.at[me, at], own_sems.at[slot])
        return sends, own

    def drain(at, slot):
        sends, own = moves(at, slot)
        for send in sends:
            send.wait_send()
        own.wait()

    rows = inputs_ref[0].astype(F32)
    samples, width = rows.shape
    hat, _ = normalize(rows)
    normed = (hat * gain_ref[...] + shift_ref[...]).astype(BF)
    saved_ref[0, 0] = dot(turned[:width], normed, 1, 1).astype(BF)
    saved_ref[0, 1] = dot(normed, project[:, width:2 * width], 1, 0).astype(BF)
    saved_ref[0, 2] = dot(turned[2 * width:], normed, 1, 1).astype(BF)
    mask = mask_ref[...]
    extra = extra_rows(1, samples, [jnp.ones((1, samples), F32)])
    for odd in (False, True):
        own = half_ones(odd, samples)
        left_extra = extra_columns(odd, samples, [mask])
        for pair in range(width // PAIR):
            head = 2 * pair + odd
            first = head * HEAD
            mixed, log_total = attend_head(
                saved_ref[0, 1, :, pair * PAIR:(pair + 1) * PAIR], left_extra, own,
                saved_ref[0, 0, first:first + HEAD, :], extra, odd,
                saved_ref[0, 2, first:first + HEAD, :],
            )
            mixed_ref[0, first:first + HEAD, :] = mixed.astype(BF)
            log_ref[0, head:head + 1, :] = log_total
    branch = dot(mixed_ref[0], output_w[...], 0, 0) + bias_ref[...]
    after = (inputs_ref[0].astype(F32) + branch).astype(BF)

    @pl.when(step >= 2)
    def _():
        drain(step - 2, slot)

    outbox[slot] = after.reshape(outbox.shape[1:])
    sends, own = moves(step, slot)
    for send in sends:
        send.start()
    own.start()

    @pl.when(step == steps - 1)
    def _():
        drain(step, slot)
        if seen_ref.shape[1] > 1:
            drain(step - 1, 1 - slot)
        for hop in range(1, peers):
            arrived(seen_ref.at[(me + peers - hop) % peers], recv_sems.at[hop])


def axis_orders(peers, tasks):
    feat_bits = peers.bit_length() - 1
    task_bits = tasks.bit_length() - 1
    half = (feat_bits - 1) // 2
    core = ("feat", 0, 1)
    across = ("feat", 1, half)
    along = ("feat", 1 + half, feat_bits - 1 - half)
    task = ("task", 0, task_bits)
    kept = lambda order: [where for where in order if where[2] > 0]
    return (
        kept([core, across, along, task]), kept([core, along, across, task]),
        kept([("feat", 0, feat_bits), task]),
    )


def hop_offsets(order):
    offsets = [0]
    for _, _, bits in order:
        offsets.append(offsets[-1] + 2 ** bits - 1)
    return offsets


def sample_backward_kernel(
    peers, tasks, feature_jobs, sample_jobs,
    inputs_ref, mask_ref, gain_ref, shift_ref, project, output_w,
    saved_ref, mixed_ref, log_ref, grad_ref, feature_vectors, feature_stacked,
    input_grad_ref, summed_ref, vectors_ref,
    project_sum, output_sum, vector_grad, turned, packed_all,
    parts, inbox, full, feature_parts, feature_inbox, sample_parts, sample_inbox,
    load_sems, store_sems, sends, recvs, vector_sends, vector_recvs,
):
    step = pl.program_id(0)
    steps = pl.num_programs(0)
    local = packed_all.shape[0]
    *orders, vector_order = axis_orders(peers, tasks)
    stages = len(orders[0])
    last = 2 * stages
    size = parts.shape[2]
    place = {"feat": lax.axis_index("feat"), "task": lax.axis_index("task")}

    def digit(where):
        axis, bit, bits = where
        return (place[axis] // 2 ** bit) % 2 ** bits

    def partner(where, hop):
        axis, bit, bits = where
        own = digit(where)
        return {axis: place[axis] + ((own + hop) % 2 ** bits - own) * 2 ** bit}

    hops, bases, sizes = [], [], []
    for order in orders:
        hops.append(hop_offsets(order + order[::-1]))
        base, left = [0], [size]
        for where in order:
            left.append(left[-1] >> where[2])
            base.append(base[-1] + digit(where) * left[-1])
        bases.append(base)
        sizes.append(left)

    def exchanges(job, lane, stage):
        index = stage if stage < stages else last - 1 - stage
        where = orders[lane][index]
        part = sizes[lane][index + 1]
        copies = []
        for hop in range(1, 2 ** where[2]):
            if stage < stages:
                gone = bases[lane][index] + ((digit(where) + hop) % 2 ** where[2]) * part
                source = parts.at[job, lane, pl.ds(gone, part)]
                begin = size - sizes[lane][index] + (hop - 1) * part
                target = inbox.at[job, lane, pl.ds(begin, part)]
            else:
                source = target = full.at[job, lane, pl.ds(bases[lane][index + 1], part)]
            at = hops[lane][stage] + hop - 1
            copies.append(
                pltpu.make_async_remote_copy(
                    src_ref=source, dst_ref=target, send_sem=sends.at[job, lane, at],
                    recv_sem=recvs.at[job, lane, at], device_id=partner(where, hop),
                    device_id_type=MESH,
                )
            )
        return copies

    def load(job):
        return pltpu.make_async_copy(feature_stacked.at[job], parts.at[job], load_sems.at[job])

    def store(job):
        return pltpu.make_async_copy(full.at[job], summed_ref.at[job], store_sems.at[job])

    def advance(action, job, loaded):
        if action == 0 and loaded:
            load(job).wait()
        for lane in range(2):
            if action > 0:
                for copy in exchanges(job, lane, action - 1):
                    copy.wait()
            if 0 < action <= stages:
                part = sizes[lane][action]
                kept = pl.ds(bases[lane][action], part)
                total = parts[job, lane, kept].astype(F32)
                for hop in range(1, 2 ** orders[lane][action - 1][2]):
                    begin = size - sizes[lane][action - 1] + (hop - 1) * part
                    total = total + inbox[job, lane, pl.ds(begin, part)].astype(F32)
                if action < stages:
                    parts[job, lane, kept] = total.astype(BF)
                else:
                    full[job, lane, kept] = total.astype(BF)
            if action < last:
                for copy in exchanges(job, lane, action):
                    copy.start()
        if action == last:
            store(job).start()

    offsets = [0, 1] + [2 * action - 1 for action in range(2, last)] + [2 * last - 2]

    def feature_tick(point):
        for action in reversed(range(last + 1)):
            job = TICKS * step + point - offsets[action]

            @pl.when((job >= 0) & (job < feature_jobs))
            def _():
                advance(action, job, True)

    def sample_tick():
        for action in reversed(range(last + 1)):
            job = step - local - action

            @pl.when((job >= 0) & (job < sample_jobs))
            def _():
                advance(action, feature_jobs + job, False)

    vector_hops = hop_offsets(vector_order)

    def vector_exchanges(kind, stage):
        source, target = [(feature_parts, feature_inbox), (sample_parts, sample_inbox)][kind]
        where = vector_order[stage]
        slot = vector_hops[stage] + stage + digit(where)
        copies = []
        for hop in range(1, 2 ** where[2]):
            at = vector_hops[stage] + hop - 1
            copies.append(
                pltpu.make_async_remote_copy(
                    src_ref=source.at[stage], dst_ref=target.at[slot],
                    send_sem=vector_sends.at[kind, at], recv_sem=vector_recvs.at[kind, at],
                    device_id=partner(where, hop), device_id_type=MESH,
                )
            )
        return copies

    def vector_advance(kind, action):
        source, target = [(feature_parts, feature_inbox), (sample_parts, sample_inbox)][kind]
        if action > 0:
            for copy in vector_exchanges(kind, action - 1):
                copy.wait()
            where = vector_order[action - 1]
            first = vector_hops[action - 1] + action - 1
            target[first + digit(where)] = source[action - 1]
            total = target[first]
            for other in range(1, 2 ** where[2]):
                total = total + target[first + other]
            source[action] = total
        if action < len(vector_order):
            for copy in vector_exchanges(kind, action):
                copy.start()
        else:
            rows = source.shape[1]
            first = kind * feature_parts.shape[1]
            vectors_ref[first:first + rows] = source[action]

    @pl.when(step == 0)
    def _():
        barrier = pltpu.get_barrier_semaphore()
        for where in vector_order:
            for hop in range(1, 2 ** where[2]):
                pl.semaphore_signal(
                    barrier, inc=1, device_id=partner(where, hop), device_id_type=MESH
                )
        for job in range(feature_jobs):
            load(job).start()
        turned[...] = project[...].T
        project_sum[...] = jnp.zeros_like(project_sum)
        output_sum[...] = jnp.zeros_like(output_sum)
        vector_grad[...] = jnp.zeros_like(vector_grad)
        feature_parts[0] = feature_vectors[...]
        pl.semaphore_wait(barrier, vector_hops[-1])
        vector_advance(0, 0)

    for action in range(1, len(vector_order) + 1):
        @pl.when(step == action)
        def _():
            vector_advance(0, action)

    pl.when(step < local)(
        lambda: sample_backward_attention(
            step, feature_tick, inputs_ref, mask_ref, gain_ref, shift_ref, output_w, saved_ref,
            mixed_ref, log_ref, grad_ref, project_sum, output_sum, vector_grad, packed_all,
        )
    )

    @pl.when(step == local - 1)
    def _():
        width = project_sum.shape[1]
        sums = [project_sum.at[part * width:(part + 1) * width] for part in range(3)]
        per_column = size // 2
        for piece, total in enumerate(sums + [output_sum]):
            job, first = divmod(piece * width // TILE, per_column)
            for column in range(width // LANES):
                lane, inner = divmod(column, width // LANES // 2)
                begin = inner * per_column + first
                parts[feature_jobs + job, lane, begin:begin + width // TILE] = total[
                    :, column * LANES:(column + 1) * LANES
                ].astype(BF).reshape(width // TILE, TILE, LANES)

    @pl.when(step >= local)
    def _():
        feature_tick(0)
        sample_tick()
        samples, width = inputs_ref.shape[1:]
        hat, inverse = normalize(inputs_ref[0].astype(F32))
        grad_normed = dot(packed_all[step - local], turned[...], 0, 0)
        grad_rows, grad_gain, grad_shift = normalize_back(grad_normed, gain_ref[...], hat, inverse)
        stream = grad_ref[...].reshape(samples, width).astype(F32)
        input_grad_ref[0] = (stream + grad_rows).astype(BF)
        vector_grad[0:1, :] += grad_gain
        vector_grad[1:2, :] += grad_shift
        feature_tick(1)

    @pl.when(step == steps - 1)
    def _():
        sample_parts[0] = vector_grad[...]
        vector_advance(1, 0)
        for at in range(2 * local, 2 * local + feature_jobs + sample_jobs + last + 1):
            for tick in range(TICKS * at, TICKS * (at + 1)):
                for action in reversed(range(last + 1)):
                    job = tick - offsets[action]
                    if 0 <= job < feature_jobs:
                        advance(action, job, True)
            for action in reversed(range(last + 1)):
                job = at - local - action
                if 0 <= job < sample_jobs:
                    advance(action, feature_jobs + job, False)
            if 0 < at - 2 * local < len(vector_order) + 1:
                vector_advance(1, at - 2 * local)
        for job in range(feature_jobs + sample_jobs):
            store(job).wait()


def sample_backward_attention(
    step, feature_tick, inputs_ref, mask_ref, gain_ref, shift_ref, output_w, saved_ref,
    mixed_ref, log_ref, grad_ref, project_sum, output_sum, vector_grad, packed_all,
):
    packed_grad = packed_all.at[step]
    samples, width = inputs_ref.shape[1:]
    low_grad = grad_ref[...].reshape(samples, width)
    output_sum[...] += dot(mixed_ref[0], low_grad, 1, 0)
    grad_mixed = dot(output_w[...], low_grad, 1, 1)
    low_mixed = grad_mixed.astype(BF)
    delta = (low_mixed.astype(F32) * mixed_ref[0].astype(F32))
    delta = jnp.sum(delta.reshape(width // HEAD, HEAD, samples), axis=1)
    mask = mask_ref[...]
    ones = jnp.ones((samples, 1), F32)
    one_row = jnp.ones((1, samples), F32)
    for odd in (False, True):
        own = half_ones(odd, samples)
        key_extra = extra_columns(odd, samples, [mask, ones, ones, ones])
        value_extra = extra_columns(odd, samples, [ones, ones, ones])
        for pair in range(width // PAIR):
            head = 2 * pair + odd
            first = head * HEAD
            done = odd * (width // PAIR) + pair
            if done % (HEADS // TICKS) == 0:
                feature_tick(done // (HEADS // TICKS))
            lanes = slice(pair * PAIR, (pair + 1) * PAIR)
            query_rows = saved_ref[0, 0, first:first + HEAD, :]
            value_rows = saved_ref[0, 2, first:first + HEAD, :]
            grad_rows = low_mixed[first:first + HEAD, :]
            keys = saved_ref[0, 1, :, lanes]
            key_rows = keys.T[HEAD:] if odd else keys.T[:HEAD]
            high, middle, low = pieces(-log_ref[0, head:head + 1, :])
            right = stack_half(odd, query_rows, extra_rows(4, samples, [one_row, high, middle, low]))
            high, middle, low = pieces(-delta[head:head + 1, :])
            value_right = jnp.concatenate(
                [grad_rows, extra_rows(3, samples, [high, middle, low])], axis=0
            )
            value_left = jnp.concatenate(
                [value_rows, extra_rows(3, samples, [one_row] * 3)], axis=0
            )
            shares = jnp.exp2(dot(keys * own + key_extra, right, 1, 0) * POWER)
            grad_shares = dot(value_left, value_right, 0, 0)
            low_scores = (shares * grad_shares).astype(BF)
            packed_grad[2 * width + first:2 * width + first + HEAD, :] = dot(
                grad_rows, shares.astype(BF), 1, 1
            ).astype(BF)
            packed_grad[width + first:width + first + HEAD, :] = (
                dot(query_rows, low_scores, 1, 1) * SCALE
            ).astype(BF)
            packed_grad[first:first + HEAD, :] = (
                dot(key_rows, low_scores, 1, 0) * SCALE
            ).astype(BF)
    hat, _ = normalize(inputs_ref[0].astype(F32))
    normed = (hat * gain_ref[...] + shift_ref[...]).astype(BF)
    project_sum[...] += dot(packed_grad[...], normed, 1, 0)
    vector_grad[2:3, :] += jnp.sum(low_grad.astype(F32), axis=0, keepdims=True)


def finish_kernel(
    chunks, summed, inputs, results, vectors_ref,
    up_grad, down_grad, feature_project, feature_output, sample_project, sample_output,
    input_grad, output, hidden_ref, *refs,
):
    *vector_refs, piece_in, piece_out, token_in, token_out, result_box, loads, stores = refs
    pieces, columns, width, _ = piece_in.shape
    local = token_in.shape[0]
    per_job = summed.shape[2] // width

    def load_piece(index):
        part = pl.ds(index % per_job * width, width)
        return pltpu.make_async_copy(
            summed.at[index // per_job, :, part], piece_in.at[index], loads.at[0, index]
        )

    def load_token(index):
        return pltpu.make_async_copy(inputs.at[index], token_in.at[index], loads.at[1, index])

    def load_result(index):
        return pltpu.make_async_copy(results.at[:, index], result_box.at[index], loads.at[2, index])

    across = lambda target, count: [
        (target.at[:, pl.ds(at * width, width)], count == 3) for at in range(count)
    ]
    down = lambda target, count: [
        (target.at[pl.ds(at * width, width)], False) for at in range(count)
    ]
    places = (
        across(up_grad, chunks) + down(down_grad, chunks) + across(feature_project, 3)
        + down(feature_output, 1) + across(sample_project, 3) + down(sample_output, 1)
    )
    copies = []
    for index in range(pieces):
        load_piece(index).start()
        if index < local:
            load_token(index).start()
            load_result(index).start()
    for index, target in enumerate(vector_refs):
        first = index if index < 6 else index + 10
        target[...] = vectors_ref[first:first + 1, :]
    for index in range(hidden_ref.shape[1] // width):
        hidden_ref[:, index * width:(index + 1) * width] = vectors_ref[8 + index:9 + index, :]
    for index, (target, turn) in enumerate(places):
        load_piece(index).wait()
        for column in range(columns):
            piece = piece_in[index, column].astype(F32)
            span = slice(column * LANES, (column + 1) * LANES)
            if turn:
                piece_out[index, span, :] = piece.T
            else:
                piece_out[index, :, span] = piece
        copies.append(pltpu.make_async_copy(piece_out.at[index], target, stores.at[0, index]))
        copies[-1].start()
        if index < local:
            load_token(index).wait()
            token_out[index] = token_in[index].astype(F32)
            copies.append(
                pltpu.make_async_copy(token_out.at[index], input_grad.at[index], stores.at[1, index])
            )
            copies[-1].start()
            load_result(index).wait()
            copies.append(
                pltpu.make_async_copy(result_box.at[index], output.at[index], stores.at[2, index])
            )
            copies[-1].start()
    for copy in copies:
        copy.wait()


def to_groups(block_ref, spare):
    features, group, width = block_ref.shape
    rows = block_ref[...].astype(F32).reshape(features * group, width)
    columns = []
    for lanes in range(width // 128):
        spare[lanes] = rows[:, lanes * 128:(lanes + 1) * 128]
        columns.append(
            jnp.concatenate(
                [spare[lanes, pl.ds(one, features, stride=group), :] for one in range(group)],
                axis=0,
            )
        )
    return jnp.concatenate(columns, axis=1)


def from_groups(rows, block_ref, spare):
    features, group, width = block_ref.shape
    for lanes in range(width // 128):
        span = slice(lanes * 128, (lanes + 1) * 128)
        for one in range(group):
            spare[lanes, pl.ds(one, features, stride=group), :] = rows[
                one * features:(one + 1) * features, span
            ]
        block_ref[:, :, span] = spare[lanes].reshape(features, group, 128).astype(BF)


def feature_kernel(
    peers,
    stream_ref, cotangent_hbm, gain_ref, shift_ref, project, output_w,
    bias_ref, dense_gain_ref, dense_shift_ref, up_ref, up_bias_ref, down_ref, down_bias_ref,
    results_ref, grads_ref, stacked_ref, vectors_ref,
    vector_grad, hidden_grad, project_sum, output_sum, up_sum, down_sum, turned, spare, query_t, keys_s, value_t, mixed_t, logs,
    packed_grad, cotangents, result_box, grad_box,
    cotangent_sends, cotangent_recvs, result_sends, grad_sends, result_recvs, grad_recvs, own_sems,
):
    step = pl.program_id(0)
    steps, features, group, _ = cotangents.shape
    slot = step % 2
    me = lax.axis_index("feat")
    local = features // peers
    share = steps * group
    chunks, chunk, width = down_ref.shape
    tokens = features * group
    joined = 2 * features

    def cotangent_moves(at, own=False):
        def part(peer):
            return cotangent_hbm.at[:, pl.ds(pl.multiple_of(peer * share + at * group, group), group), :]

        inbox = cotangents.at[at, pl.ds(me * local, local)]
        if own:
            return pltpu.make_async_copy(part(me), inbox, cotangent_recvs.at[at])
        sends = []
        for hop in range(1, peers):
            peer = (me + hop) % peers
            sends.append(
                push(part(peer), inbox, cotangent_sends.at[at % 2, hop], cotangent_recvs.at[at], peer)
            )
        return sends

    def start_cotangent(at):
        for send in cotangent_moves(at):
            send.start()
        cotangent_moves(at, own=True).start()

    def back_moves(at, slot, box, target, send_sems, recv_sems, own_sem):
        place = target.at[me, :, pl.ds(pl.multiple_of(at * group, group), group), :]
        sends = []
        for hop in range(1, peers):
            peer = (me + hop) % peers
            sends.append(
                push(
                    box.at[slot, pl.ds(peer * local, local)], place,
                    send_sems.at[slot, hop], recv_sems.at[hop], peer,
                )
            )
        own = pltpu.make_async_copy(box.at[slot, pl.ds(me * local, local)], place, own_sem)
        return sends, own

    def result_moves(at, slot):
        return back_moves(
            at, slot, result_box, results_ref, result_sends, result_recvs, own_sems.at[0, slot]
        )

    def grad_moves(at, slot):
        return back_moves(
            at, slot, grad_box, grads_ref, grad_sends, grad_recvs, own_sems.at[1, slot]
        )

    def begin(moves):
        sends, own = moves
        for send in sends:
            send.start()
        own.start()

    def drain(moves):
        sends, own = moves
        for send in sends:
            send.wait_send()
        own.wait()

    @pl.when(step == 0)
    def _():
        greet(peers, me)
        start_cotangent(0)
        turned[...] = project[...].T

    @pl.when(step + 1 < steps)
    def _():
        @pl.when(step >= 1)
        def _():
            for send in cotangent_moves(step - 1):
                send.wait_send()

        start_cotangent(step + 1)

    @pl.when(step == 0)
    def _():
        project_sum[...] = jnp.zeros_like(project_sum)
        output_sum[...] = jnp.zeros_like(output_sum)
        up_sum[...] = jnp.zeros_like(up_sum)
        down_sum[...] = jnp.zeros_like(down_sum)
        vector_grad[...] = jnp.zeros_like(vector_grad)
        hidden_grad[...] = jnp.zeros_like(hidden_grad)

    rows = to_groups(stream_ref, spare)
    hat, inverse = normalize(rows)
    normed = (hat * gain_ref[...] + shift_ref[...]).astype(BF)
    query_t[...] = dot(turned[:width], normed, 1, 1).astype(BF)
    keys_s[...] = dot(normed, project[:, width:2 * width], 1, 0).astype(BF)
    value_t[...] = dot(turned[2 * width:], normed, 1, 1).astype(BF)
    place = lax.broadcasted_iota(jnp.int32, (joined, 1), 0)
    place_row = lax.broadcasted_iota(jnp.int32, (1, joined), 1)
    key_first = (place < features).astype(F32)
    key_second = (place >= features).astype(F32)
    hide_first = jnp.where(place_row >= features, MASKED, 0.0)
    hide_second = jnp.where(place_row < features, MASKED, 0.0)
    ones = jnp.ones((joined, 1), F32)
    one_row = jnp.ones((1, joined), F32)
    extra = extra_rows(2, joined, [hide_first, hide_second])
    for odd in (False, True):
        own = half_ones(odd, joined)
        left_extra = extra_columns(odd, joined, [key_first, key_second])
        for pair in range(width // PAIR):
            head = 2 * pair + odd
            first = head * HEAD
            for part in range(tokens // joined):
                span = slice(part * joined, (part + 1) * joined)
                mixed, log_total = attend_head(
                    keys_s[span, pair * PAIR:(pair + 1) * PAIR], left_extra, own,
                    query_t[first:first + HEAD, span], extra, odd,
                    value_t[first:first + HEAD, span],
                )
                mixed_t[first:first + HEAD, span] = mixed.astype(BF)
                logs[head:head + 1, span] = log_total
    after = rows + dot(mixed_t[...], output_w[...], 0, 0) + bias_ref[...]

    dense_hat, dense_inverse = normalize(after)
    dense_in = (dense_hat * dense_gain_ref[...] + dense_shift_ref[...]).astype(BF)
    arrived(cotangents.at[step], cotangent_recvs.at[step])
    stream = to_groups(cotangents.at[step], spare)
    low_stream = stream.astype(BF)
    result = after + down_bias_ref[...]
    grad_dense = jnp.zeros((tokens, width), F32)
    for index in range(chunks):
        up = up_ref[:, index * chunk:(index + 1) * chunk]
        pre = dot(dense_in, up, 1, 0) + up_bias_ref[index]
        square = pre * pre
        bend = jnp.tanh(pre * (GELU_A + (GELU_A * GELU_B) * square))
        half = 0.5 + 0.5 * bend
        activated = (pre * half).astype(BF)
        slope = half + (pre * half) * (1.0 - bend) * (GELU_A + (3.0 * GELU_A * GELU_B) * square)
        result = result + dot(activated, down_ref[index], 1, 0)
        grad_pre = (slope * dot(low_stream, down_ref[index], 1, 1)).astype(BF)
        grad_dense = grad_dense + dot(grad_pre, up, 1, 1)
        down_sum[index] += dot(activated, low_stream, 0, 0)
        up_sum[index] += dot(dense_in, grad_pre, 0, 0)
        hidden_grad[index] += jnp.sum(grad_pre.astype(F32), axis=0, keepdims=True)

    @pl.when(step >= 2)
    def _():
        drain(result_moves(step - 2, slot))
        drain(grad_moves(step - 2, slot))

    from_groups(result, result_box.at[slot], spare)
    begin(result_moves(step, slot))
    dense_rows, dense_gain_grad, dense_shift_grad = normalize_back(
        grad_dense, dense_gain_ref[...], dense_hat, dense_inverse
    )
    grad_after = stream + dense_rows

    low_grad = grad_after.astype(BF)
    output_sum[...] += dot(mixed_t[...], low_grad, 1, 0)
    low_mixed = dot(output_w[...], low_grad, 1, 1).astype(BF)
    delta = low_mixed.astype(F32) * mixed_t[...].astype(F32)
    delta = jnp.sum(delta.reshape(width // HEAD, HEAD, tokens), axis=1)
    for odd in (False, True):
        own = half_ones(odd, joined)
        key_extra = extra_columns(odd, joined, [key_first, key_second, ones, ones, ones])
        for pair in range(width // PAIR):
            head = 2 * pair + odd
            first = head * HEAD
            for part in range(tokens // joined):
                span = slice(part * joined, (part + 1) * joined)
                query_rows = query_t[first:first + HEAD, span]
                value_rows = value_t[first:first + HEAD, span]
                grad_rows = low_mixed[first:first + HEAD, span]
                keys = keys_s[span, pair * PAIR:(pair + 1) * PAIR]
                key_rows = keys.T[HEAD:] if odd else keys.T[:HEAD]
                high, middle, low = pieces(-logs[head:head + 1, span])
                right = stack_half(
                    odd, query_rows,
                    extra_rows(5, joined, [hide_first, hide_second, high, middle, low]),
                )
                high, middle, low = pieces(-delta[head:head + 1, span])
                value_right = jnp.concatenate(
                    [grad_rows, extra_rows(3, joined, [high, middle, low])], axis=0
                )
                value_left = jnp.concatenate(
                    [value_rows, extra_rows(3, joined, [one_row] * 3)], axis=0
                )
                shares = jnp.exp2(dot(keys * own + key_extra, right, 1, 0) * POWER)
                grad_shares = dot(value_left, value_right, 0, 0)
                low_scores = (shares * grad_shares).astype(BF)
                packed_grad[2 * width + first:2 * width + first + HEAD, span] = dot(
                    grad_rows, shares.astype(BF), 1, 1
                ).astype(BF)
                packed_grad[width + first:width + first + HEAD, span] = (
                    dot(query_rows, low_scores, 1, 1) * SCALE
                ).astype(BF)
                packed_grad[first:first + HEAD, span] = (
                    dot(key_rows, low_scores, 1, 0) * SCALE
                ).astype(BF)
    project_sum[...] += dot(packed_grad[...], normed, 1, 0)
    grad_normed = dot(packed_grad[...], turned[...], 0, 0)
    grad_rows, gain_grad, shift_grad = normalize_back(grad_normed, gain_ref[...], hat, inverse)
    from_groups(grad_after + grad_rows, grad_box.at[slot], spare)
    begin(grad_moves(step, slot))
    vector_grad[0:1, :] += gain_grad
    vector_grad[1:2, :] += shift_grad
    vector_grad[2:3, :] += jnp.sum(low_grad.astype(F32), axis=0, keepdims=True)
    vector_grad[3:4, :] += dense_gain_grad
    vector_grad[4:5, :] += dense_shift_grad
    vector_grad[5:6, :] += jnp.sum(stream, axis=0, keepdims=True)

    @pl.when(step == pl.num_programs(0) - 1)
    def _():
        vectors_ref[...] = jnp.concatenate(
            [vector_grad[...]]
            + [hidden_grad[index].reshape(chunk // width, width) for index in range(chunks)]
            + [jnp.zeros((8 - hidden_grad.size // width, width), F32)], axis=0,
        )
        sums = [up_sum.at[index] for index in range(chunks)]
        sums += [down_sum.at[index] for index in range(chunks)]
        sums += [project_sum.at[part * width:(part + 1) * width] for part in range(3)]
        rows_per_job = stacked_ref.shape[2]
        for piece, total in enumerate(sums + [output_sum]):
            job, first = divmod(piece * width, rows_per_job)
            for column in range(width // LANES):
                stacked_ref[job, column, first:first + width, :] = total[
                    :, column * LANES:(column + 1) * LANES
                ].astype(BF)
        for send in cotangent_moves(step):
            send.wait_send()
        drain(result_moves(step, slot))
        drain(grad_moves(step, slot))
        if steps > 1:
            for send in cotangent_moves(step - 1):
                send.wait_send()
            drain(result_moves(step - 1, 1 - slot))
            drain(grad_moves(step - 1, 1 - slot))
        for hop in range(1, peers):
            source = (me + peers - hop) % peers
            arrived(results_ref.at[source], result_recvs.at[hop])
            arrived(grads_ref.at[source], grad_recvs.at[hop])


def whole(shape):
    return pl.BlockSpec(shape, lambda step: (0,) * len(shape), pipeline_mode=pl.Buffered(1))


def whole_out(shape):
    return pl.BlockSpec(shape, lambda step: (0,) * len(shape))


def call(kernel, grid, in_specs, out_specs, out_shape, scratch, name, flops, nbytes, remote=None):
    return pl.pallas_call(
        kernel,
        grid=(grid,),
        in_specs=in_specs,
        out_specs=out_specs,
        out_shape=[jax.ShapeDtypeStruct(*one) for one in out_shape],
        scratch_shapes=scratch,
        compiler_params=pltpu.CompilerParams(
            dimension_semantics=("arbitrary",), vmem_limit_bytes=LIMIT,
            collective_id=remote, has_side_effects=remote is not None,
        ),
        cost_estimate=pl.CostEstimate(flops=flops, bytes_accessed=nbytes, transcendentals=0),
        name=name,
    )


def body(
    peers, tasks,
    inputs, context, sample_mask,
    sample_gain, sample_shift, sample_project, sample_output, sample_bias,
    feature_gain, feature_shift, feature_project, feature_output, feature_bias,
    dense_gain, dense_shift, up_weight, up_bias, down_weight, down_bias,
    cotangent,
):
    _, local, samples, width = inputs.shape
    hidden = up_weight.shape[1]
    features = local * peers
    share = samples // peers
    group = 8
    chunk = 512
    chunks = hidden // chunk
    row = lambda vector: vector.reshape(1, -1)
    columns = width // LANES
    pieces_in = (2 * chunks + 4, 4)
    size = max(LANES, peers * tasks)
    job_rows = 2 * size * TILE // columns
    feature_jobs, sample_jobs = (count * width // job_rows for count in pieces_in)
    jobs = feature_jobs + sample_jobs
    *orders, vector_order = axis_orders(peers, tasks)
    lane_hops = hop_offsets(orders[0] + orders[0][::-1])[-1]
    vector_hops = hop_offsets(vector_order)[-1]
    vector_stages = len(vector_order)

    position = lax.iota(jnp.int32, samples)
    visible = (position < context[0]) & (sample_mask[0] == 1)
    mask = jnp.where(visible, 0.0, MASKED).astype(F32).reshape(samples, 1)
    tokens = inputs[0]

    square = whole((width, width))
    line = whole((1, width))
    token_spec = pl.BlockSpec((1, samples, width), lambda step: (step, 0, 0))
    peer_spec = pl.BlockSpec((peers, 1, share, width), lambda step: (0, step, 0, 0))
    saved_spec = pl.BlockSpec((1, 3, samples, width), lambda step: (step, 0, 0, 0))
    log_spec = pl.BlockSpec((1, HEADS, samples), lambda step: (step, 0, 0))
    anywhere = pl.BlockSpec(memory_space=pl.ANY)
    peer_shape = (peers, local, share, width)
    sems = pltpu.SemaphoreType.DMA
    seen, saved, mixed, logs = call(
        functools.partial(sample_forward_kernel, peers), local,
        [token_spec, whole((samples, 1)), line, line, whole((width, 3 * width)), square, line],
        [anywhere, saved_spec, token_spec, log_spec],
        [
            (peer_shape, BF), ((local, 3, samples, width), BF),
            ((local, width, samples), BF), ((local, HEADS, samples), F32),
        ],
        [
            pltpu.VMEM((3 * width, width), BF), pltpu.VMEM((2, peers, share, width), BF),
            sems((2, peers)), sems((peers,)), sems((2,)),
        ],
        "sample_forward", 60_000_000_000, 30_000_000, 0,
    )(
        tokens, mask, row(sample_gain), row(sample_shift), sample_project, sample_output, row(sample_bias),
    )

    block_tokens = features * group
    block_spec = pl.BlockSpec((features, group, width), lambda step: (0, step, 0))
    down_chunks = down_weight.reshape(chunks, chunk, width)
    result_returned, grad_returned, feature_stacked, feature_vectors = call(
        functools.partial(feature_kernel, peers), share // group,
        [
            block_spec, anywhere, line, line, whole((width, 3 * width)),
            square, line, line, line, whole((width, hidden)), whole((chunks, 1, chunk)),
            whole((chunks, chunk, width)), line,
        ],
        [
            anywhere, anywhere, whole_out((feature_jobs, columns, job_rows, LANES)),
            whole_out((16, width)),
        ],
        [
            (peer_shape, BF), (peer_shape, BF),
            ((feature_jobs, columns, job_rows, LANES), BF), ((16, width), F32),
        ],
        [
            pltpu.VMEM((8, width), F32), pltpu.VMEM((chunks, 1, chunk), F32),
            pltpu.VMEM((3 * width, width), F32), pltpu.VMEM((width, width), F32),
            pltpu.VMEM((chunks, width, chunk), F32), pltpu.VMEM((chunks, chunk, width), F32),
            pltpu.VMEM((3 * width, width), BF), pltpu.VMEM((width // 128, block_tokens, 128), F32),
            pltpu.VMEM((width, block_tokens), BF),
            pltpu.VMEM((block_tokens, width), BF), pltpu.VMEM((width, block_tokens), BF),
            pltpu.VMEM((width, block_tokens), BF), pltpu.VMEM((HEADS, block_tokens), F32),
            pltpu.VMEM((3 * width, block_tokens), BF),
            pltpu.VMEM((share // group, features, group, width), BF),
            pltpu.VMEM((2, features, group, width), BF), pltpu.VMEM((2, features, group, width), BF),
            sems((2, peers)), sems((share // group,)), sems((2, peers)), sems((2, peers)),
            sems((peers,)), sems((peers,)), sems((2, 2)),
        ],
        "feature_block", 130_000_000_000, 40_000_000, 1,
    )(
        seen.reshape(features, share, width), cotangent[0],
        row(feature_gain), row(feature_shift), feature_project,
        feature_output, row(feature_bias), row(dense_gain), row(dense_shift),
        up_weight, up_bias.reshape(chunks, 1, chunk), down_chunks, row(down_bias),
    )
    stack_shape = (jobs, 2, size, TILE, LANES)
    again = lambda *tail: lambda step: (step % local,) + tail
    early = lambda *tail: lambda step: (jnp.minimum(step, local - 1),) + tail
    input_grad, summed, vectors = call(
        functools.partial(sample_backward_kernel, peers, tasks, feature_jobs, sample_jobs),
        2 * local,
        [
            pl.BlockSpec((1, samples, width), again(0, 0)), whole((samples, 1)), line, line,
            whole((width, 3 * width)), square,
            pl.BlockSpec((1, 3, samples, width), early(0, 0, 0)),
            pl.BlockSpec((1, samples, width), early(0, 0)),
            pl.BlockSpec((1, HEADS, samples), early(0, 0)),
            pl.BlockSpec((peers, 1, share, width), lambda step: (0, step % local, 0, 0)),
            whole((16, width)), anywhere,
        ],
        [
            pl.BlockSpec((1, samples, width), lambda step: (jnp.maximum(step - local, 0), 0, 0)),
            anywhere, whole_out((24, width)),
        ],
        [((local, samples, width), BF), (stack_shape, BF), ((24, width), F32)],
        [
            pltpu.VMEM((3 * width, width), F32), pltpu.VMEM((width, width), F32),
            pltpu.VMEM((8, width), F32), pltpu.VMEM((3 * width, width), BF),
            pltpu.VMEM((local, 3 * width, samples), BF),
            pltpu.VMEM(stack_shape, BF), pltpu.VMEM(stack_shape, BF), pltpu.VMEM(stack_shape, BF),
            pltpu.VMEM((vector_stages + 1, 16, width), F32),
            pltpu.VMEM((vector_hops + vector_stages, 16, width), F32),
            pltpu.VMEM((vector_stages + 1, 8, width), F32),
            pltpu.VMEM((vector_hops + vector_stages, 8, width), F32),
            sems((feature_jobs,)), sems((jobs,)), sems((jobs, 2, lane_hops)), sems((jobs, 2, lane_hops)),
            sems((2, vector_hops)), sems((2, vector_hops)),
        ],
        "sample_backward", 110_000_000_000, 50_000_000, 2,
    )(
        tokens, mask, row(sample_gain), row(sample_shift), sample_project, sample_output,
        saved, mixed, logs, grad_returned, feature_vectors,
        feature_stacked.reshape((feature_jobs,) + stack_shape[1:]),
    )
    blocks = sum(pieces_in)
    once = lambda shape: pl.BlockSpec(shape, lambda step: (0,) * len(shape))
    (
        up_grad, down_grad, feature_project_grad, feature_output_grad,
        sample_project_grad, sample_output_grad, input_grad, output, hidden_grad, *vectors,
    ) = call(
        functools.partial(finish_kernel, chunks), 1,
        [anywhere, anywhere, anywhere, whole((24, width))],
        [anywhere] * 8 + [once((1, hidden))] + [once((1, width))] * 9,
        [
            ((width, hidden), F32), ((hidden, width), F32), ((width, 3 * width), F32),
            ((width, width), F32), ((width, 3 * width), F32), ((width, width), F32),
            ((local, samples, width), F32), ((local, peers, share, width), BF), ((1, hidden), F32),
        ] + [((1, width), F32)] * 9,
        [
            pltpu.VMEM((blocks, columns, width, LANES), BF), pltpu.VMEM((blocks, width, width), F32),
            pltpu.VMEM((local, samples, width), BF), pltpu.VMEM((local, samples, width), F32),
            pltpu.VMEM((local, peers, share, width), BF), sems((3, blocks)), sems((3, blocks)),
        ],
        "finish", 0, 46_000_000,
    )(summed.reshape(jobs, columns, job_rows, LANES), input_grad, result_returned, vectors)
    output = output.reshape(local, samples, width)
    vectors = [vector.reshape(width) for vector in vectors]
    return (
        output[None], input_grad[None],
        vectors[6], vectors[7], sample_project_grad, sample_output_grad,
        vectors[8], vectors[0], vectors[1], feature_project_grad,
        feature_output_grad, vectors[2], vectors[3], vectors[4],
        up_grad, hidden_grad.reshape(hidden), down_grad, vectors[5],
    )


def solution(mesh):
    split = P("task", "feat", None, None)
    return jax.shard_map(
        functools.partial(body, mesh.shape["feat"], mesh.shape["task"]),
        mesh=mesh,
        in_specs=(split, P("task"), P("task", None)) + (P(),) * 16 + (split,),
        out_specs=(split, split) + (P(),) * 16,
        check_vma=False,
    )
```

```python
import functools
import math

import jax
import jax.numpy as jnp
from jax import lax
from jax.experimental import pallas as pl
from jax.experimental.pallas import tpu as pltpu
from jax.sharding import PartitionSpec as P

HEADS = 8
HEAD = 64
PAIR = 2 * HEAD
EPSILON = 1e-05
SCALE = HEAD ** (-0.5)
POWER = SCALE * math.log2(math.e)
MASKED = -1e30
GELU_A = math.sqrt(2.0 / math.pi)
GELU_B = 0.044715
BF = jnp.bfloat16
F32 = jnp.float32
LIMIT = 60 * 1024 * 1024
MESH = pl.DeviceIdType.MESH
TILE = 16
LANES = 128
TICKS = 2


def dot(left, right, left_dim, right_dim):
    return lax.dot_general(
        left, right, (((left_dim,), (right_dim,)), ((), ())), preferred_element_type=F32
    )


def normalize(rows):
    center = rows - jnp.mean(rows, axis=-1, keepdims=True)
    spread = jnp.mean(center * center, axis=-1, keepdims=True)
    inverse = lax.rsqrt(spread + EPSILON)
    return center * inverse, inverse


def normalize_back(grad_normed, gain, hat, inverse):
    scaled = grad_normed * gain
    middle = jnp.mean(scaled, axis=-1, keepdims=True)
    along = jnp.mean(scaled * hat, axis=-1, keepdims=True)
    grad_rows = inverse * (scaled - middle - hat * along)
    grad_gain = jnp.sum(grad_normed * hat, axis=0, keepdims=True)
    grad_shift = jnp.sum(grad_normed, axis=0, keepdims=True)
    return grad_rows, grad_gain, grad_shift


def pieces(row):
    high = row.astype(BF).astype(F32)
    rest = row - high
    middle = rest.astype(BF).astype(F32)
    return high, middle, rest - middle


def extra_rows(count, width, rows):
    place = lax.broadcasted_iota(jnp.int32, (16, width), 0)
    block = jnp.zeros((16, width), F32)
    for index, row in enumerate(rows):
        block = jnp.where(place == index, row, block)
    return jnp.concatenate([block.astype(BF), jnp.zeros((HEAD - 16, width), BF)], axis=0)


def half_ones(odd, depth):
    lane = lax.broadcasted_iota(jnp.int32, (depth, PAIR), 1)
    own = (lane >= HEAD) if odd else (lane < HEAD)
    return own.astype(F32).astype(BF)


def stack_half(odd, own, extra):
    return jnp.concatenate([extra, own] if odd else [own, extra], axis=0)


def extra_columns(odd, depth, columns):
    lane = lax.broadcasted_iota(jnp.int32, (depth, PAIR), 1)
    first = 0 if odd else HEAD
    block = jnp.zeros((depth, PAIR), F32)
    for index, column in enumerate(columns):
        block = jnp.where(lane == first + index, column, block)
    return block.astype(BF)


def attend_head(keys, left_extra, own, query_rows, extra, odd, value_rows):
    left = keys * own + left_extra
    scores = dot(left, stack_half(odd, query_rows, extra), 1, 0)
    highest = jnp.max(scores, axis=0, keepdims=True)
    weights = jnp.exp2((scores - highest) * POWER)
    totals = jnp.sum(weights, axis=0, keepdims=True)
    mixed = dot(value_rows, weights.astype(BF), 1, 0) / totals
    log_total = highest + jnp.log2(totals) * (1.0 / POWER)
    return mixed, log_total


def attend_head_back(left, right, value_left, value_right, query_rows, key_rows, grad_rows):
    shares = jnp.exp2(dot(left, right, 1, 0) * POWER)
    grad_shares = dot(value_left, value_right, 1, 0)
    low_scores = (shares * grad_shares).astype(BF)
    grad_values = dot(grad_rows, shares.astype(BF), 1, 1)
    grad_keys = dot(query_rows, low_scores, 1, 1) * SCALE
    grad_queries = dot(key_rows, low_scores, 1, 0) * SCALE
    return grad_queries, grad_keys, grad_values


def push(source, target, send_sem, recv_sem, peer):
    return pltpu.make_async_remote_copy(
        src_ref=source, dst_ref=target, send_sem=send_sem, recv_sem=recv_sem,
        device_id={"feat": peer}, device_id_type=MESH,
    )


def greet(peers, me):
    barrier = pltpu.get_barrier_semaphore()
    for hop in range(1, peers):
        pl.semaphore_signal(
            barrier, inc=1, device_id={"feat": (me + hop) % peers}, device_id_type=MESH
        )
    pl.semaphore_wait(barrier, peers - 1)


def arrived(buffer, sem):
    pltpu.make_async_copy(buffer, buffer, sem).wait()


def sample_forward_kernel(
    peers,
    inputs_ref, mask_ref, gain_ref, shift_ref, project, output_w, bias_ref,
    seen_ref, saved_ref, mixed_ref, log_ref,
    turned, outbox, send_sems, recv_sems, own_sems,
):
    step = pl.program_id(0)
    steps = pl.num_programs(0)
    slot = step % 2
    me = lax.axis_index("feat")

    @pl.when(step == 0)
    def _():
        greet(peers, me)
        turned[...] = project[...].T

    def moves(at, slot):
        sends = []
        for hop in range(1, peers):
            peer = (me + hop) % peers
            sends.append(
                push(
                    outbox.at[slot, peer], seen_ref.at[me, at],
                    send_sems.at[slot, hop], recv_sems.at[hop], peer,
                )
            )
        own = pltpu.make_async_copy(outbox.at[slot, me], seen_ref.at[me, at], own_sems.at[slot])
        return sends, own

    def drain(at, slot):
        sends, own = moves(at, slot)
        for send in sends:
            send.wait_send()
        own.wait()

    rows = inputs_ref[0].astype(F32)
    samples, width = rows.shape
    hat, _ = normalize(rows)
    normed = (hat * gain_ref[...] + shift_ref[...]).astype(BF)
    saved_ref[0, 0] = dot(turned[:width], normed, 1, 1).astype(BF)
    saved_ref[0, 1] = dot(normed, project[:, width:2 * width], 1, 0).astype(BF)
    saved_ref[0, 2] = dot(turned[2 * width:], normed, 1, 1).astype(BF)
    mask = mask_ref[...]
    extra = extra_rows(1, samples, [jnp.ones((1, samples), F32)])
    for odd in (False, True):
        own = half_ones(odd, samples)
        left_extra = extra_columns(odd, samples, [mask])
        for pair in range(width // PAIR):
            head = 2 * pair + odd
            first = head * HEAD
            mixed, log_total = attend_head(
                saved_ref[0, 1, :, pair * PAIR:(pair + 1) * PAIR], left_extra, own,
                saved_ref[0, 0, first:first + HEAD, :], extra, odd,
                saved_ref[0, 2, first:first + HEAD, :],
            )
            mixed_ref[0, first:first + HEAD, :] = mixed.astype(BF)
            log_ref[0, head:head + 1, :] = log_total
    branch = dot(mixed_ref[0], output_w[...], 0, 0) + bias_ref[...]
    after = (inputs_ref[0].astype(F32) + branch).astype(BF)

    @pl.when(step >= 2)
    def _():
        drain(step - 2, slot)

    outbox[slot] = after.reshape(outbox.shape[1:])
    sends, own = moves(step, slot)
    for send in sends:
        send.start()
    own.start()

    @pl.when(step == steps - 1)
    def _():
        drain(step, slot)
        if seen_ref.shape[1] > 1:
            drain(step - 1, 1 - slot)
        for hop in range(1, peers):
            arrived(seen_ref.at[(me + peers - hop) % peers], recv_sems.at[hop])


def axis_orders(peers, tasks):
    feat_bits = peers.bit_length() - 1
    task_bits = tasks.bit_length() - 1
    half = (feat_bits - 1) // 2
    core = ("feat", 0, 1)
    across = ("feat", 1, half)
    along = ("feat", 1 + half, feat_bits - 1 - half)
    task = ("task", 0, task_bits)
    kept = lambda order: [where for where in order if where[2] > 0]
    return (
        kept([core, across, along, task]), kept([core, along, across, task]),
        kept([("feat", 0, feat_bits), task]),
    )


def hop_offsets(order):
    offsets = [0]
    for _, _, bits in order:
        offsets.append(offsets[-1] + 2 ** bits - 1)
    return offsets


def sample_backward_kernel(
    peers, tasks, feature_jobs, sample_jobs,
    inputs_ref, mask_ref, gain_ref, shift_ref, project, output_w,
    saved_ref, mixed_ref, log_ref, grad_ref, feature_vectors, feature_stacked,
    input_grad_ref, summed_ref, vectors_ref,
    project_sum, output_sum, vector_grad, turned, packed_all,
    parts, inbox, full, feature_parts, feature_inbox, sample_parts, sample_inbox,
    load_sems, store_sems, sends, recvs, vector_sends, vector_recvs,
):
    step = pl.program_id(0)
    steps = pl.num_programs(0)
    local = packed_all.shape[0]
    *orders, vector_order = axis_orders(peers, tasks)
    stages = len(orders[0])
    last = 2 * stages
    size = parts.shape[2]
    place = {"feat": lax.axis_index("feat"), "task": lax.axis_index("task")}

    def digit(where):
        axis, bit, bits = where
        return (place[axis] // 2 ** bit) % 2 ** bits

    def partner(where, hop):
        axis, bit, bits = where
        own = digit(where)
        return {axis: place[axis] + ((own + hop) % 2 ** bits - own) * 2 ** bit}

    hops, bases, sizes = [], [], []
    for order in orders:
        hops.append(hop_offsets(order + order[::-1]))
        base, left = [0], [size]
        for where in order:
            left.append(left[-1] >> where[2])
            base.append(base[-1] + digit(where) * left[-1])
        bases.append(base)
        sizes.append(left)

    def exchanges(job, lane, stage):
        index = stage if stage < stages else last - 1 - stage
        where = orders[lane][index]
        part = sizes[lane][index + 1]
        copies = []
        for hop in range(1, 2 ** where[2]):
            if stage < stages:
                gone = bases[lane][index] + ((digit(where) + hop) % 2 ** where[2]) * part
                source = parts.at[job, lane, pl.ds(gone, part)]
                begin = size - sizes[lane][index] + (hop - 1) * part
                target = inbox.at[job, lane, pl.ds(begin, part)]
            else:
                source = target = full.at[job, lane, pl.ds(bases[lane][index + 1], part)]
            at = hops[lane][stage] + hop - 1
            copies.append(
                pltpu.make_async_remote_copy(
                    src_ref=source, dst_ref=target, send_sem=sends.at[job, lane, at],
                    recv_sem=recvs.at[job, lane, at], device_id=partner(where, hop),
                    device_id_type=MESH,
                )
            )
        return copies

    def load(job):
        return pltpu.make_async_copy(feature_stacked.at[job], parts.at[job], load_sems.at[job])

    def store(job):
        return pltpu.make_async_copy(full.at[job], summed_ref.at[job], store_sems.at[job])

    def advance(action, job, loaded):
        if action == 0 and loaded:
            load(job).wait()
        for lane in range(2):
            if action > 0:
                for copy in exchanges(job, lane, action - 1):
                    copy.wait()
            if 0 < action <= stages:
                part = sizes[lane][action]
                kept = pl.ds(bases[lane][action], part)
                total = parts[job, lane, kept].astype(F32)
                for hop in range(1, 2 ** orders[lane][action - 1][2]):
                    begin = size - sizes[lane][action - 1] + (hop - 1) * part
                    total = total + inbox[job, lane, pl.ds(begin, part)].astype(F32)
                if action < stages:
                    parts[job, lane, kept] = total.astype(BF)
                else:
                    full[job, lane, kept] = total.astype(BF)
            if action < last:
                for copy in exchanges(job, lane, action):
                    copy.start()
        if action == last:
            store(job).start()

    offsets = [0, 1] + [2 * action - 1 for action in range(2, last)] + [2 * last - 2]

    def feature_tick(point):
        for action in reversed(range(last + 1)):
            job = TICKS * step + point - offsets[action]

            @pl.when((job >= 0) & (job < feature_jobs))
            def _():
                advance(action, job, True)

    def sample_tick():
        for action in reversed(range(last + 1)):
            job = step - local - action

            @pl.when((job >= 0) & (job < sample_jobs))
            def _():
                advance(action, feature_jobs + job, False)

    vector_hops = hop_offsets(vector_order)

    def vector_exchanges(kind, stage):
        source, target = [(feature_parts, feature_inbox), (sample_parts, sample_inbox)][kind]
        where = vector_order[stage]
        slot = vector_hops[stage] + stage + digit(where)
        copies = []
        for hop in range(1, 2 ** where[2]):
            at = vector_hops[stage] + hop - 1
            copies.append(
                pltpu.make_async_remote_copy(
                    src_ref=source.at[stage], dst_ref=target.at[slot],
                    send_sem=vector_sends.at[kind, at], recv_sem=vector_recvs.at[kind, at],
                    device_id=partner(where, hop), device_id_type=MESH,
                )
            )
        return copies

    def vector_advance(kind, action):
        source, target = [(feature_parts, feature_inbox), (sample_parts, sample_inbox)][kind]
        if action > 0:
            for copy in vector_exchanges(kind, action - 1):
                copy.wait()
            where = vector_order[action - 1]
            first = vector_hops[action - 1] + action - 1
            target[first + digit(where)] = source[action - 1]
            total = target[first]
            for other in range(1, 2 ** where[2]):
                total = total + target[first + other]
            source[action] = total
        if action < len(vector_order):
            for copy in vector_exchanges(kind, action):
                copy.start()
        else:
            rows = source.shape[1]
            first = kind * feature_parts.shape[1]
            vectors_ref[first:first + rows] = source[action]

    @pl.when(step == 0)
    def _():
        barrier = pltpu.get_barrier_semaphore()
        for where in vector_order:
            for hop in range(1, 2 ** where[2]):
                pl.semaphore_signal(
                    barrier, inc=1, device_id=partner(where, hop), device_id_type=MESH
                )
        for job in range(feature_jobs):
            load(job).start()
        turned[...] = project[...].T
        project_sum[...] = jnp.zeros_like(project_sum)
        output_sum[...] = jnp.zeros_like(output_sum)
        vector_grad[...] = jnp.zeros_like(vector_grad)
        feature_parts[0] = feature_vectors[...]
        pl.semaphore_wait(barrier, vector_hops[-1])
        vector_advance(0, 0)

    for action in range(1, len(vector_order) + 1):
        @pl.when(step == action)
        def _():
            vector_advance(0, action)

    pl.when(step < local)(
        lambda: sample_backward_attention(
            step, feature_tick, inputs_ref, mask_ref, gain_ref, shift_ref, output_w, saved_ref,
            mixed_ref, log_ref, grad_ref, project_sum, output_sum, vector_grad, packed_all,
        )
    )

    @pl.when(step == local - 1)
    def _():
        width = project_sum.shape[1]
        sums = [project_sum.at[part * width:(part + 1) * width] for part in range(3)]
        per_column = size // 2
        for piece, total in enumerate(sums + [output_sum]):
            job, first = divmod(piece * width // TILE, per_column)
            for column in range(width // LANES):
                lane, inner = divmod(column, width // LANES // 2)
                begin = inner * per_column + first
                parts[feature_jobs + job, lane, begin:begin + width // TILE] = total[
                    :, column * LANES:(column + 1) * LANES
                ].astype(BF).reshape(width // TILE, TILE, LANES)

    @pl.when(step >= local)
    def _():
        feature_tick(0)
        sample_tick()
        samples, width = inputs_ref.shape[1:]
        hat, inverse = normalize(inputs_ref[0].astype(F32))
        grad_normed = dot(packed_all[step - local], turned[...], 0, 0)
        grad_rows, grad_gain, grad_shift = normalize_back(grad_normed, gain_ref[...], hat, inverse)
        stream = grad_ref[...].reshape(samples, width).astype(F32)
        input_grad_ref[0] = (stream + grad_rows).astype(BF)
        vector_grad[0:1, :] += grad_gain
        vector_grad[1:2, :] += grad_shift
        feature_tick(1)

    @pl.when(step == steps - 1)
    def _():
        sample_parts[0] = vector_grad[...]
        vector_advance(1, 0)
        for at in range(2 * local, 2 * local + feature_jobs + sample_jobs + last + 1):
            for tick in range(TICKS * at, TICKS * (at + 1)):
                for action in reversed(range(last + 1)):
                    job = tick - offsets[action]
                    if 0 <= job < feature_jobs:
                        advance(action, job, True)
            for action in reversed(range(last + 1)):
                job = at - local - action
                if 0 <= job < sample_jobs:
                    advance(action, feature_jobs + job, False)
            if 0 < at - 2 * local < len(vector_order) + 1:
                vector_advance(1, at - 2 * local)
        for job in range(feature_jobs + sample_jobs):
            store(job).wait()


def sample_backward_attention(
    step, feature_tick, inputs_ref, mask_ref, gain_ref, shift_ref, output_w, saved_ref,
    mixed_ref, log_ref, grad_ref, project_sum, output_sum, vector_grad, packed_all,
):
    packed_grad = packed_all.at[step]
    samples, width = inputs_ref.shape[1:]
    low_grad = grad_ref[...].reshape(samples, width)
    output_sum[...] += dot(mixed_ref[0], low_grad, 1, 0)
    grad_mixed = dot(output_w[...], low_grad, 1, 1)
    low_mixed = grad_mixed.astype(BF)
    delta = (low_mixed.astype(F32) * mixed_ref[0].astype(F32))
    delta = jnp.sum(delta.reshape(width // HEAD, HEAD, samples), axis=1)
    mask = mask_ref[...]
    ones = jnp.ones((samples, 1), F32)
    one_row = jnp.ones((1, samples), F32)
    for odd in (False, True):
        own = half_ones(odd, samples)
        key_extra = extra_columns(odd, samples, [mask, ones, ones, ones])
        value_extra = extra_columns(odd, samples, [ones, ones, ones])
        for pair in range(width // PAIR):
            head = 2 * pair + odd
            first = head * HEAD
            done = odd * (width // PAIR) + pair
            if done % (HEADS // TICKS) == 0:
                feature_tick(done // (HEADS // TICKS))
            lanes = slice(pair * PAIR, (pair + 1) * PAIR)
            query_rows = saved_ref[0, 0, first:first + HEAD, :]
            value_rows = saved_ref[0, 2, first:first + HEAD, :]
            grad_rows = low_mixed[first:first + HEAD, :]
            keys = saved_ref[0, 1, :, lanes]
            key_rows = keys.T[HEAD:] if odd else keys.T[:HEAD]
            high, middle, low = pieces(-log_ref[0, head:head + 1, :])
            right = stack_half(odd, query_rows, extra_rows(4, samples, [one_row, high, middle, low]))
            high, middle, low = pieces(-delta[head:head + 1, :])
            value_right = jnp.concatenate(
                [grad_rows, extra_rows(3, samples, [high, middle, low])], axis=0
            )
            value_left = jnp.concatenate(
                [value_rows, extra_rows(3, samples, [one_row] * 3)], axis=0
            )
            shares = jnp.exp2(dot(keys * own + key_extra, right, 1, 0) * POWER)
            grad_shares = dot(value_left, value_right, 0, 0)
            low_scores = (shares * grad_shares).astype(BF)
            packed_grad[2 * width + first:2 * width + first + HEAD, :] = dot(
                grad_rows, shares.astype(BF), 1, 1
            ).astype(BF)
            packed_grad[width + first:width + first + HEAD, :] = (
                dot(query_rows, low_scores, 1, 1) * SCALE
            ).astype(BF)
            packed_grad[first:first + HEAD, :] = (
                dot(key_rows, low_scores, 1, 0) * SCALE
            ).astype(BF)
    hat, _ = normalize(inputs_ref[0].astype(F32))
    normed = (hat * gain_ref[...] + shift_ref[...]).astype(BF)
    project_sum[...] += dot(packed_grad[...], normed, 1, 0)
    vector_grad[2:3, :] += jnp.sum(low_grad.astype(F32), axis=0, keepdims=True)


def finish_kernel(
    chunks, summed, inputs, results, vectors_ref,
    up_grad, down_grad, feature_project, feature_output, sample_project, sample_output,
    input_grad, output, hidden_ref, *refs,
):
    *vector_refs, piece_in, piece_out, token_in, token_out, result_box, loads, stores = refs
    pieces, columns, width, _ = piece_in.shape
    local = token_in.shape[0]
    per_job = summed.shape[2] // width

    def load_piece(index):
        part = pl.ds(index % per_job * width, width)
        return pltpu.make_async_copy(
            summed.at[index // per_job, :, part], piece_in.at[index], loads.at[0, index]
        )

    def load_token(index):
        return pltpu.make_async_copy(inputs.at[index], token_in.at[index], loads.at[1, index])

    def load_result(index):
        return pltpu.make_async_copy(results.at[:, index], result_box.at[index], loads.at[2, index])

    across = lambda target, count: [
        (target.at[:, pl.ds(at * width, width)], count == 3) for at in range(count)
    ]
    down = lambda target, count: [
        (target.at[pl.ds(at * width, width)], False) for at in range(count)
    ]
    places = (
        across(up_grad, chunks) + down(down_grad, chunks) + across(feature_project, 3)
        + down(feature_output, 1) + across(sample_project, 3) + down(sample_output, 1)
    )
    copies = []
    for index in range(pieces):
        load_piece(index).start()
        if index < local:
            load_token(index).start()
            load_result(index).start()
    for index, target in enumerate(vector_refs):
        first = index if index < 6 else index + 10
        target[...] = vectors_ref[first:first + 1, :]
    for index in range(hidden_ref.shape[1] // width):
        hidden_ref[:, index * width:(index + 1) * width] = vectors_ref[8 + index:9 + index, :]
    for index, (target, turn) in enumerate(places):
        load_piece(index).wait()
        for column in range(columns):
            piece = piece_in[index, column].astype(F32)
            span = slice(column * LANES, (column + 1) * LANES)
            if turn:
                piece_out[index, span, :] = piece.T
            else:
                piece_out[index, :, span] = piece
        copies.append(pltpu.make_async_copy(piece_out.at[index], target, stores.at[0, index]))
        copies[-1].start()
        if index < local:
            load_token(index).wait()
            token_out[index] = token_in[index].astype(F32)
            copies.append(
                pltpu.make_async_copy(token_out.at[index], input_grad.at[index], stores.at[1, index])
            )
            copies[-1].start()
            load_result(index).wait()
            copies.append(
                pltpu.make_async_copy(result_box.at[index], output.at[index], stores.at[2, index])
            )
            copies[-1].start()
    for copy in copies:
        copy.wait()


def to_groups(block_ref, spare):
    features, group, width = block_ref.shape
    rows = block_ref[...].astype(F32).reshape(features * group, width)
    columns = []
    for lanes in range(width // 128):
        spare[lanes] = rows[:, lanes * 128:(lanes + 1) * 128]
        columns.append(
            jnp.concatenate(
                [spare[lanes, pl.ds(one, features, stride=group), :] for one in range(group)],
                axis=0,
            )
        )
    return jnp.concatenate(columns, axis=1)


def from_groups(rows, block_ref, spare):
    features, group, width = block_ref.shape
    for lanes in range(width // 128):
        span = slice(lanes * 128, (lanes + 1) * 128)
        for one in range(group):
            spare[lanes, pl.ds(one, features, stride=group), :] = rows[
                one * features:(one + 1) * features, span
            ]
        block_ref[:, :, span] = spare[lanes].reshape(features, group, 128).astype(BF)


def feature_kernel(
    peers,
    stream_ref, cotangent_hbm, gain_ref, shift_ref, project, output_w,
    bias_ref, dense_gain_ref, dense_shift_ref, up_ref, up_bias_ref, down_ref, down_bias_ref,
    results_ref, grads_ref, stacked_hbm, vectors_ref,
    stacked_ref, stack_sem, vector_grad, hidden_grad, project_sum, output_sum, up_sum, down_sum, turned, spare, query_t, keys_s, value_t, mixed_t, logs,
    packed_grad, cotangents, result_box, grad_box,
    cotangent_sends, cotangent_recvs, result_sends, grad_sends, result_recvs, grad_recvs, own_sems,
):
    step = pl.program_id(0)
    steps, features, group, _ = cotangents.shape
    slot = step % 2
    me = lax.axis_index("feat")
    local = features // peers
    share = steps * group
    chunks, chunk, width = down_ref.shape
    tokens = features * group
    joined = 2 * features

    def cotangent_moves(at, own=False):
        def part(peer):
            return cotangent_hbm.at[:, pl.ds(pl.multiple_of(peer * share + at * group, group), group), :]

        inbox = cotangents.at[at, pl.ds(me * local, local)]
        if own:
            return pltpu.make_async_copy(part(me), inbox, cotangent_recvs.at[at])
        sends = []
        for hop in range(1, peers):
            peer = (me + hop) % peers
            sends.append(
                push(part(peer), inbox, cotangent_sends.at[at % 2, hop], cotangent_recvs.at[at], peer)
            )
        return sends

    def start_cotangent(at):
        for send in cotangent_moves(at):
            send.start()
        cotangent_moves(at, own=True).start()

    def back_moves(at, slot, box, target, send_sems, recv_sems, own_sem):
        place = target.at[me, :, pl.ds(pl.multiple_of(at * group, group), group), :]
        sends = []
        for hop in range(1, peers):
            peer = (me + hop) % peers
            sends.append(
                push(
                    box.at[slot, pl.ds(peer * local, local)], place,
                    send_sems.at[slot, hop], recv_sems.at[hop], peer,
                )
            )
        own = pltpu.make_async_copy(box.at[slot, pl.ds(me * local, local)], place, own_sem)
        return sends, own

    def result_moves(at, slot):
        return back_moves(
            at, slot, result_box, results_ref, result_sends, result_recvs, own_sems.at[0, slot]
        )

    def grad_moves(at, slot):
        return back_moves(
            at, slot, grad_box, grads_ref, grad_sends, grad_recvs, own_sems.at[1, slot]
        )

    def begin(moves):
        sends, own = moves
        for send in sends:
            send.start()
        own.start()

    def drain(moves):
        sends, own = moves
        for send in sends:
            send.wait_send()
        own.wait()

    @pl.when(step == 0)
    def _():
        greet(peers, me)
        start_cotangent(0)
        turned[...] = project[...].T

    @pl.when(step + 1 < steps)
    def _():
        @pl.when(step >= 1)
        def _():
            for send in cotangent_moves(step - 1):
                send.wait_send()

        start_cotangent(step + 1)

    @pl.when(step == 0)
    def _():
        project_sum[...] = jnp.zeros_like(project_sum)
        output_sum[...] = jnp.zeros_like(output_sum)
        up_sum[...] = jnp.zeros_like(up_sum)
        down_sum[...] = jnp.zeros_like(down_sum)
        vector_grad[...] = jnp.zeros_like(vector_grad)
        hidden_grad[...] = jnp.zeros_like(hidden_grad)

    rows = to_groups(stream_ref, spare)
    hat, inverse = normalize(rows)
    normed = (hat * gain_ref[...] + shift_ref[...]).astype(BF)
    query_t[...] = dot(turned[:width], normed, 1, 1).astype(BF)
    keys_s[...] = dot(normed, project[:, width:2 * width], 1, 0).astype(BF)
    value_t[...] = dot(turned[2 * width:], normed, 1, 1).astype(BF)
    place = lax.broadcasted_iota(jnp.int32, (joined, 1), 0)
    place_row = lax.broadcasted_iota(jnp.int32, (1, joined), 1)
    key_first = (place < features).astype(F32)
    key_second = (place >= features).astype(F32)
    hide_first = jnp.where(place_row >= features, MASKED, 0.0)
    hide_second = jnp.where(place_row < features, MASKED, 0.0)
    ones = jnp.ones((joined, 1), F32)
    one_row = jnp.ones((1, joined), F32)
    extra = extra_rows(2, joined, [hide_first, hide_second])
    for odd in (False, True):
        own = half_ones(odd, joined)
        left_extra = extra_columns(odd, joined, [key_first, key_second])
        for pair in range(width // PAIR):
            head = 2 * pair + odd
            first = head * HEAD
            for part in range(tokens // joined):
                span = slice(part * joined, (part + 1) * joined)
                mixed, log_total = attend_head(
                    keys_s[span, pair * PAIR:(pair + 1) * PAIR], left_extra, own,
                    query_t[first:first + HEAD, span], extra, odd,
                    value_t[first:first + HEAD, span],
                )
                mixed_t[first:first + HEAD, span] = mixed.astype(BF)
                logs[head:head + 1, span] = log_total
    after = rows + dot(mixed_t[...], output_w[...], 0, 0) + bias_ref[...]

    dense_hat, dense_inverse = normalize(after)
    dense_in = (dense_hat * dense_gain_ref[...] + dense_shift_ref[...]).astype(BF)
    arrived(cotangents.at[step], cotangent_recvs.at[step])
    stream = to_groups(cotangents.at[step], spare)
    low_stream = stream.astype(BF)
    result = after + down_bias_ref[...]
    grad_dense = jnp.zeros((tokens, width), F32)
    for index in range(chunks):
        up = up_ref[:, index * chunk:(index + 1) * chunk]
        pre = dot(dense_in, up, 1, 0) + up_bias_ref[index]
        square = pre * pre
        bend = jnp.tanh(pre * (GELU_A + (GELU_A * GELU_B) * square))
        half = 0.5 + 0.5 * bend
        activated = (pre * half).astype(BF)
        slope = half + (pre * half) * (1.0 - bend) * (GELU_A + (3.0 * GELU_A * GELU_B) * square)
        result = result + dot(activated, down_ref[index], 1, 0)
        grad_pre = (slope * dot(low_stream, down_ref[index], 1, 1)).astype(BF)
        grad_dense = grad_dense + dot(grad_pre, up, 1, 1)
        down_sum[index] += dot(activated, low_stream, 0, 0)
        up_sum[index] += dot(dense_in, grad_pre, 0, 0)
        hidden_grad[index] += jnp.sum(grad_pre.astype(F32), axis=0, keepdims=True)

    @pl.when(step >= 2)
    def _():
        drain(result_moves(step - 2, slot))
        drain(grad_moves(step - 2, slot))

    from_groups(result, result_box.at[slot], spare)
    begin(result_moves(step, slot))
    dense_rows, dense_gain_grad, dense_shift_grad = normalize_back(
        grad_dense, dense_gain_ref[...], dense_hat, dense_inverse
    )
    grad_after = stream + dense_rows

    low_grad = grad_after.astype(BF)
    output_sum[...] += dot(mixed_t[...], low_grad, 1, 0)
    low_mixed = dot(output_w[...], low_grad, 1, 1).astype(BF)
    delta = low_mixed.astype(F32) * mixed_t[...].astype(F32)
    delta = jnp.sum(delta.reshape(width // HEAD, HEAD, tokens), axis=1)
    for odd in (False, True):
        own = half_ones(odd, joined)
        key_extra = extra_columns(odd, joined, [key_first, key_second, ones, ones, ones])
        for pair in range(width // PAIR):
            head = 2 * pair + odd
            first = head * HEAD
            for part in range(tokens // joined):
                span = slice(part * joined, (part + 1) * joined)
                query_rows = query_t[first:first + HEAD, span]
                value_rows = value_t[first:first + HEAD, span]
                grad_rows = low_mixed[first:first + HEAD, span]
                keys = keys_s[span, pair * PAIR:(pair + 1) * PAIR]
                key_rows = keys.T[HEAD:] if odd else keys.T[:HEAD]
                high, middle, low = pieces(-logs[head:head + 1, span])
                right = stack_half(
                    odd, query_rows,
                    extra_rows(5, joined, [hide_first, hide_second, high, middle, low]),
                )
                high, middle, low = pieces(-delta[head:head + 1, span])
                value_right = jnp.concatenate(
                    [grad_rows, extra_rows(3, joined, [high, middle, low])], axis=0
                )
                value_left = jnp.concatenate(
                    [value_rows, extra_rows(3, joined, [one_row] * 3)], axis=0
                )
                shares = jnp.exp2(dot(keys * own + key_extra, right, 1, 0) * POWER)
                grad_shares = dot(value_left, value_right, 0, 0)
                low_scores = (shares * grad_shares).astype(BF)
                packed_grad[2 * width + first:2 * width + first + HEAD, span] = dot(
                    grad_rows, shares.astype(BF), 1, 1
                ).astype(BF)
                packed_grad[width + first:width + first + HEAD, span] = (
                    dot(query_rows, low_scores, 1, 1) * SCALE
                ).astype(BF)
                packed_grad[first:first + HEAD, span] = (
                    dot(key_rows, low_scores, 1, 0) * SCALE
                ).astype(BF)
    project_sum[...] += dot(packed_grad[...], normed, 1, 0)
    grad_normed = dot(packed_grad[...], turned[...], 0, 0)
    grad_rows, gain_grad, shift_grad = normalize_back(grad_normed, gain_ref[...], hat, inverse)
    from_groups(grad_after + grad_rows, grad_box.at[slot], spare)
    begin(grad_moves(step, slot))
    vector_grad[0:1, :] += gain_grad
    vector_grad[1:2, :] += shift_grad
    vector_grad[2:3, :] += jnp.sum(low_grad.astype(F32), axis=0, keepdims=True)
    vector_grad[3:4, :] += dense_gain_grad
    vector_grad[4:5, :] += dense_shift_grad
    vector_grad[5:6, :] += jnp.sum(stream, axis=0, keepdims=True)

    @pl.when(step == pl.num_programs(0) - 1)
    def _():
        vectors_ref[...] = jnp.concatenate(
            [vector_grad[...]]
            + [hidden_grad[index].reshape(chunk // width, width) for index in range(chunks)]
            + [jnp.zeros((8 - hidden_grad.size // width, width), F32)], axis=0,
        )
        sums = [up_sum.at[index] for index in range(chunks)]
        sums += [down_sum.at[index] for index in range(chunks)]
        sums += [project_sum.at[part * width:(part + 1) * width] for part in range(3)]
        rows_per_job = stacked_ref.shape[2]
        for piece, total in enumerate(sums + [output_sum]):
            job, first = divmod(piece * width, rows_per_job)
            for column in range(width // LANES):
                stacked_ref[job, column, first:first + width, :] = total[
                    :, column * LANES:(column + 1) * LANES
                ].astype(BF)
        stacking = pltpu.make_async_copy(stacked_ref, stacked_hbm, stack_sem)
        stacking.start()
        for send in cotangent_moves(step):
            send.wait_send()
        drain(result_moves(step, slot))
        drain(grad_moves(step, slot))
        if steps > 1:
            for send in cotangent_moves(step - 1):
                send.wait_send()
            drain(result_moves(step - 1, 1 - slot))
            drain(grad_moves(step - 1, 1 - slot))
        for hop in range(1, peers):
            source = (me + peers - hop) % peers
            arrived(results_ref.at[source], result_recvs.at[hop])
            arrived(grads_ref.at[source], grad_recvs.at[hop])
        stacking.wait()


def whole(shape):
    return pl.BlockSpec(shape, lambda step: (0,) * len(shape), pipeline_mode=pl.Buffered(1))


def whole_out(shape):
    return pl.BlockSpec(shape, lambda step: (0,) * len(shape))


def call(kernel, grid, in_specs, out_specs, out_shape, scratch, name, flops, nbytes, remote=None):
    return pl.pallas_call(
        kernel,
        grid=(grid,),
        in_specs=in_specs,
        out_specs=out_specs,
        out_shape=[jax.ShapeDtypeStruct(*one) for one in out_shape],
        scratch_shapes=scratch,
        compiler_params=pltpu.CompilerParams(
            dimension_semantics=("arbitrary",), vmem_limit_bytes=LIMIT,
            collective_id=remote, has_side_effects=remote is not None,
        ),
        cost_estimate=pl.CostEstimate(flops=flops, bytes_accessed=nbytes, transcendentals=0),
        name=name,
    )


def body(
    peers, tasks,
    inputs, context, sample_mask,
    sample_gain, sample_shift, sample_project, sample_output, sample_bias,
    feature_gain, feature_shift, feature_project, feature_output, feature_bias,
    dense_gain, dense_shift, up_weight, up_bias, down_weight, down_bias,
    cotangent,
):
    _, local, samples, width = inputs.shape
    hidden = up_weight.shape[1]
    features = local * peers
    share = samples // peers
    group = 8
    chunk = 512
    chunks = hidden // chunk
    row = lambda vector: vector.reshape(1, -1)
    columns = width // LANES
    pieces_in = (2 * chunks + 4, 4)
    size = max(LANES, peers * tasks)
    job_rows = 2 * size * TILE // columns
    feature_jobs, sample_jobs = (count * width // job_rows for count in pieces_in)
    jobs = feature_jobs + sample_jobs
    *orders, vector_order = axis_orders(peers, tasks)
    lane_hops = hop_offsets(orders[0] + orders[0][::-1])[-1]
    vector_hops = hop_offsets(vector_order)[-1]
    vector_stages = len(vector_order)

    position = lax.iota(jnp.int32, samples)
    visible = (position < context[0]) & (sample_mask[0] == 1)
    mask = jnp.where(visible, 0.0, MASKED).astype(F32).reshape(samples, 1)
    tokens = inputs[0]

    square = whole((width, width))
    line = whole((1, width))
    token_spec = pl.BlockSpec((1, samples, width), lambda step: (step, 0, 0))
    peer_spec = pl.BlockSpec((peers, 1, share, width), lambda step: (0, step, 0, 0))
    saved_spec = pl.BlockSpec((1, 3, samples, width), lambda step: (step, 0, 0, 0))
    log_spec = pl.BlockSpec((1, HEADS, samples), lambda step: (step, 0, 0))
    anywhere = pl.BlockSpec(memory_space=pl.ANY)
    peer_shape = (peers, local, share, width)
    sems = pltpu.SemaphoreType.DMA
    seen, saved, mixed, logs = call(
        functools.partial(sample_forward_kernel, peers), local,
        [token_spec, whole((samples, 1)), line, line, whole((width, 3 * width)), square, line],
        [anywhere, saved_spec, token_spec, log_spec],
        [
            (peer_shape, BF), ((local, 3, samples, width), BF),
            ((local, width, samples), BF), ((local, HEADS, samples), F32),
        ],
        [
            pltpu.VMEM((3 * width, width), BF), pltpu.VMEM((2, peers, share, width), BF),
            sems((2, peers)), sems((peers,)), sems((2,)),
        ],
        "sample_forward", 60_000_000_000, 30_000_000, 0,
    )(
        tokens, mask, row(sample_gain), row(sample_shift), sample_project, sample_output, row(sample_bias),
    )

    block_tokens = features * group
    block_spec = pl.BlockSpec((features, group, width), lambda step: (0, step, 0))
    down_chunks = down_weight.reshape(chunks, chunk, width)
    result_returned, grad_returned, feature_stacked, feature_vectors = call(
        functools.partial(feature_kernel, peers), share // group,
        [
            block_spec, anywhere, line, line, whole((width, 3 * width)),
            square, line, line, line, whole((width, hidden)), whole((chunks, 1, chunk)),
            whole((chunks, chunk, width)), line,
        ],
        [
            anywhere, anywhere, anywhere, whole_out((16, width)),
        ],
        [
            (peer_shape, BF), (peer_shape, BF),
            ((feature_jobs, columns, job_rows, LANES), BF), ((16, width), F32),
        ],
        [
            pltpu.VMEM((feature_jobs, columns, job_rows, LANES), BF), sems,
            pltpu.VMEM((8, width), F32), pltpu.VMEM((chunks, 1, chunk), F32),
            pltpu.VMEM((3 * width, width), F32), pltpu.VMEM((width, width), F32),
            pltpu.VMEM((chunks, width, chunk), F32), pltpu.VMEM((chunks, chunk, width), F32),
            pltpu.VMEM((3 * width, width), BF), pltpu.VMEM((width // 128, block_tokens, 128), F32),
            pltpu.VMEM((width, block_tokens), BF),
            pltpu.VMEM((block_tokens, width), BF), pltpu.VMEM((width, block_tokens), BF),
            pltpu.VMEM((width, block_tokens), BF), pltpu.VMEM((HEADS, block_tokens), F32),
            pltpu.VMEM((3 * width, block_tokens), BF),
            pltpu.VMEM((share // group, features, group, width), BF),
            pltpu.VMEM((2, features, group, width), BF), pltpu.VMEM((2, features, group, width), BF),
            sems((2, peers)), sems((share // group,)), sems((2, peers)), sems((2, peers)),
            sems((peers,)), sems((peers,)), sems((2, 2)),
        ],
        "feature_block", 130_000_000_000, 40_000_000, 1,
    )(
        seen.reshape(features, share, width), cotangent[0],
        row(feature_gain), row(feature_shift), feature_project,
        feature_output, row(feature_bias), row(dense_gain), row(dense_shift),
        up_weight, up_bias.reshape(chunks, 1, chunk), down_chunks, row(down_bias),
    )
    stack_shape = (jobs, 2, size, TILE, LANES)
    again = lambda *tail: lambda step: (step % local,) + tail
    early = lambda *tail: lambda step: (jnp.minimum(step, local - 1),) + tail
    input_grad, summed, vectors = call(
        functools.partial(sample_backward_kernel, peers, tasks, feature_jobs, sample_jobs),
        2 * local,
        [
            pl.BlockSpec((1, samples, width), again(0, 0)), whole((samples, 1)), line, line,
            whole((width, 3 * width)), square,
            pl.BlockSpec((1, 3, samples, width), early(0, 0, 0)),
            pl.BlockSpec((1, samples, width), early(0, 0)),
            pl.BlockSpec((1, HEADS, samples), early(0, 0)),
            pl.BlockSpec((peers, 1, share, width), lambda step: (0, step % local, 0, 0)),
            whole((16, width)), anywhere,
        ],
        [
            pl.BlockSpec((1, samples, width), lambda step: (jnp.maximum(step - local, 0), 0, 0)),
            anywhere, whole_out((24, width)),
        ],
        [((local, samples, width), BF), (stack_shape, BF), ((24, width), F32)],
        [
            pltpu.VMEM((3 * width, width), F32), pltpu.VMEM((width, width), F32),
            pltpu.VMEM((8, width), F32), pltpu.VMEM((3 * width, width), BF),
            pltpu.VMEM((local, 3 * width, samples), BF),
            pltpu.VMEM(stack_shape, BF), pltpu.VMEM(stack_shape, BF), pltpu.VMEM(stack_shape, BF),
            pltpu.VMEM((vector_stages + 1, 16, width), F32),
            pltpu.VMEM((vector_hops + vector_stages, 16, width), F32),
            pltpu.VMEM((vector_stages + 1, 8, width), F32),
            pltpu.VMEM((vector_hops + vector_stages, 8, width), F32),
            sems((feature_jobs,)), sems((jobs,)), sems((jobs, 2, lane_hops)), sems((jobs, 2, lane_hops)),
            sems((2, vector_hops)), sems((2, vector_hops)),
        ],
        "sample_backward", 110_000_000_000, 50_000_000, 2,
    )(
        tokens, mask, row(sample_gain), row(sample_shift), sample_project, sample_output,
        saved, mixed, logs, grad_returned, feature_vectors,
        feature_stacked.reshape((feature_jobs,) + stack_shape[1:]),
    )
    blocks = sum(pieces_in)
    once = lambda shape: pl.BlockSpec(shape, lambda step: (0,) * len(shape))
    (
        up_grad, down_grad, feature_project_grad, feature_output_grad,
        sample_project_grad, sample_output_grad, input_grad, output, hidden_grad, *vectors,
    ) = call(
        functools.partial(finish_kernel, chunks), 1,
        [anywhere, anywhere, anywhere, whole((24, width))],
        [anywhere] * 8 + [once((1, hidden))] + [once((1, width))] * 9,
        [
            ((width, hidden), F32), ((hidden, width), F32), ((width, 3 * width), F32),
            ((width, width), F32), ((width, 3 * width), F32), ((width, width), F32),
            ((local, samples, width), F32), ((local, peers, share, width), BF), ((1, hidden), F32),
        ] + [((1, width), F32)] * 9,
        [
            pltpu.VMEM((blocks, columns, width, LANES), BF), pltpu.VMEM((blocks, width, width), F32),
            pltpu.VMEM((local, samples, width), BF), pltpu.VMEM((local, samples, width), F32),
            pltpu.VMEM((local, peers, share, width), BF), sems((3, blocks)), sems((3, blocks)),
        ],
        "finish", 0, 46_000_000,
    )(summed.reshape(jobs, columns, job_rows, LANES), input_grad, result_returned, vectors)
    output = output.reshape(local, samples, width)
    vectors = [vector.reshape(width) for vector in vectors]
    return (
        output[None], input_grad[None],
        vectors[6], vectors[7], sample_project_grad, sample_output_grad,
        vectors[8], vectors[0], vectors[1], feature_project_grad,
        feature_output_grad, vectors[2], vectors[3], vectors[4],
        up_grad, hidden_grad.reshape(hidden), down_grad, vectors[5],
    )


def solution(mesh):
    split = P("task", "feat", None, None)
    return jax.shard_map(
        functools.partial(body, mesh.shape["feat"], mesh.shape["task"]),
        mesh=mesh,
        in_specs=(split, P("task"), P("task", None)) + (P(),) * 16 + (split,),
        out_specs=(split, split) + (P(),) * 16,
        check_vma=False,
    )
```
